32 devices in a mesh: face: 8 (over z, x), band: 4 (over y, core).
Axes of the slice: x: 2, y: 2, z: 4, core: 2. Of those that a mesh axis runs over, the one named last changes fastest.
Arguments:
- node_latents: bfloat16 [8192, 512], P(('face', 'band')), may hold values from -6 to 6
- coarse_latents: bfloat16 [1024, 512], replicated, may hold values from -6 to 6
- edge_latents: bfloat16 [32768, 512], P(('face', 'band')), may hold values from -6 to 6
- up_latents: bfloat16 [8192, 512], P(('face', 'band')), may hold values from -6 to 6
- edge_weight_in: bfloat16 [1536, 512], replicated, may hold values from -0.15625 to 0.15625
- edge_weight_out: bfloat16 [512, 512], replicated, may hold values from -0.25 to 0.25
- edge_gain: float32 [512], replicated, may hold values from 0.5 to 1.5
- node_weight_in: bfloat16 [1024, 512], replicated, may hold values from -0.1875 to 0.1875
- node_weight_out: bfloat16 [512, 512], replicated, may hold values from -0.25 to 0.25
- node_gain: float32 [512], replicated, may hold values from 0.5 to 1.5
- nodes_cotangent: bfloat16 [8192, 512], P(('face', 'band')), may hold values from -6 to 6
- coarse_cotangent: bfloat16 [1024, 512], replicated, may hold values from -6 to 6
- edges_cotangent: bfloat16 [32768, 512], P(('face', 'band')), may hold values from -6 to 6
- ups_cotangent: bfloat16 [8192, 512], P(('face', 'band')), may hold values from -6 to 6
- send_rows: int32 [32, 32, 4], P(('face', 'band')), may hold values from 0 to 255, as said below
- edge_sender: int32 [32768], P(('face', 'band')), may hold values from 0 to 1407, as said below
- edge_receiver: int32 [32768], P(('face', 'band')), may hold values from 0 to 255
- up_sender: int32 [8192], P(('face', 'band')), may hold values from 0 to 255
- up_receiver: int32 [8192], P(('face', 'band')), may hold values from 0 to 1023
Outputs:
- grad_nodes: float32 [8192, 512], P(('face', 'band'))
- grad_coarse: float32 [1024, 512], replicated
- grad_edges: float32 [32768, 512], P(('face', 'band'))
- grad_ups: float32 [8192, 512], P(('face', 'band'))
- grad_edge_in: float32 [1536, 512], replicated
- grad_edge_out: float32 [512, 512], replicated
- grad_edge_gain: float32 [512], replicated
- grad_node_in: float32 [1024, 512], replicated
- grad_node_out: float32 [512, 512], replicated
- grad_node_gain: float32 [512], replicated
The draws below stay inside these ranges and needn't reach their ends.
Inputs may be any that keep to these rules, and one draw needn't show every extreme that they name: `send_rows`: entry [s, p, k] is a row of device s's nodes sent to device p in slot k. Each pair uses its first few slots, at most 4; every device fills all 4 slots to at least one device, and in every draw some device receives 4 rows from every device. Unused slots hold 0 and no edge reads them. `edge_sender`: an edge of device p reads row t of p's sender table: its own node t below 256; slot k of the rows that device s sends to p for t = 256 + s * 4 + k, always a used slot; coarse node t - 384 from 384 on.
All inputs are finite; a program needn't handle non-finite values.
Results may differ from the reference program's by a relative error of at most 0.0068.
Values may be sent and summed in bfloat16 or wider, within the bound.
No kernel may reach another device: no remote copies, remote signals or barrier semaphores. Data moves between devices by JAX's collectives and lax.ppermute only.
A program may use at most 192 MiB of HBM per device.

```python
import math
import jax
import jax.numpy as jnp
from jax import lax

L = 512
H = 512
NODE_DEV = 256
COARSE = 1024
SLOT = 4
NODES = 8192
EDGES = 32768
UPS = 8192
N_FACE = 8
N_BAND = 4


def pair_counts(key):
    devices = N_FACE * N_BAND
    base_count = jax.random.randint(jax.random.fold_in(key, 11), (devices, devices), 0, SLOT + 1)
    target = jax.random.randint(jax.random.fold_in(key, 12), (), 0, devices)
    row_ids = jnp.arange(devices, dtype=jnp.int32)[:, None]
    col_ids = jnp.arange(devices, dtype=jnp.int32)[None, :]
    forced = (col_ids == (row_ids + 1) % devices) | (col_ids == target)
    return jnp.where(forced, SLOT, base_count).astype(jnp.int32)


def draw_send_rows(key, part):
    devices = N_FACE * N_BAND
    counts = pair_counts(key)
    row_ids = jax.random.randint(jax.random.fold_in(key, 13), (devices, devices, SLOT), 0, NODE_DEV)
    live_slot = jnp.arange(SLOT, dtype=jnp.int32)[None, None, :] < counts[:, :, None]
    return jnp.where(live_slot, row_ids, 0).astype(jnp.int32)


def draw_edge_sender(key, part):
    devices = N_FACE * N_BAND
    counts = pair_counts(key)
    edge_dev = 4 * NODE_DEV
    edge_total = devices * edge_dev
    owner_dev = jnp.arange(edge_total, dtype=jnp.int32) // edge_dev
    category = jax.random.randint(jax.random.fold_in(key, 14), (edge_total,), 0, 20)
    local_row = jax.random.randint(jax.random.fold_in(key, 15), (edge_total,), 0, NODE_DEV)
    source = jax.random.randint(jax.random.fold_in(key, 16), (edge_total,), 0, devices)
    live_count = counts[source, owner_dev]
    fallback = (owner_dev - 1) % devices
    use_source = jnp.where(live_count > 0, source, fallback)
    use_count = jnp.where(live_count > 0, live_count, SLOT)
    pick_slot = jax.random.randint(jax.random.fold_in(key, 17), (edge_total,), 0, 1 << 20) % use_count
    imported = NODE_DEV + use_source * SLOT + pick_slot
    coarse_row = NODE_DEV + devices * SLOT + jax.random.randint(jax.random.fold_in(key, 18), (edge_total,), 0, COARSE)
    return jnp.where(category < 12, local_row, jnp.where(category < 17, imported, coarse_row)).astype(jnp.int32)


def touch_ends(entries, key, smallest, largest):
    spot = [jax.random.randint(jax.random.fold_in(key, axis), (), 0, length) for axis, length in enumerate(entries.shape)]
    longest = entries.shape.index(max(entries.shape))
    next_to = spot[:longest] + [(spot[longest] + 1) % entries.shape[longest]] + spot[longest + 1:]
    return entries.at[tuple(spot)].set(smallest).at[tuple(next_to)].set(largest)


def shard_levels(stream_key, extent, shards, least, top_value):
    level, own = 1.0, jax.random.fold_in(stream_key, 6)
    for position, blocks in shards:
        steps = jnp.exp(jax.random.uniform(jax.random.fold_in(own, position), (blocks,), jnp.float32, least / len(shards), top_value / len(shards)))
        level = level * jnp.repeat(steps, extent[position] // blocks).reshape([-1 if axis == position else 1 for axis in range(len(extent))])
    return level


def scatter_about(rng, dims, scale, bound, split=(), kind=jnp.bfloat16):
    loudness = shard_levels(rng, dims, split, -0.22, 0.18) if split else 1.0
    drawn = jax.random.normal(rng, dims, jnp.float32) * scale * loudness
    return jnp.minimum(jnp.maximum(drawn, -bound), bound).astype(kind)


def setup_inputs(seed: int = 0) -> dict:
    seeds = jax.random.split(jax.random.key(seed), 20)
    node_latents = scatter_about(seeds[0], (NODES, L), 1.0, 6.0, ((0, 32),))
    coarse_latents = scatter_about(seeds[1], (COARSE, L), 1.0, 6.0)
    edge_latents = scatter_about(seeds[2], (EDGES, L), 1.0, 6.0, ((0, 32),))
    up_latents = scatter_about(seeds[3], (UPS, L), 1.0, 6.0, ((0, 32),))
    edge_weight_in = scatter_about(seeds[4], (3 * L, H), (3 * L) ** -0.5, 0.15625)
    edge_weight_out = scatter_about(seeds[5], (H, L), H ** -0.5, 0.25)
    edge_gain = jnp.clip(1.0 + 0.1 * jax.random.normal(seeds[6], (L,), jnp.float32), 0.5, 1.5)
    node_weight_in = scatter_about(seeds[7], (2 * L, H), (2 * L) ** -0.5, 0.1875)
    node_weight_out = scatter_about(seeds[8], (H, L), H ** -0.5, 0.25)
    node_gain = jnp.clip(1.0 + 0.1 * jax.random.normal(seeds[9], (L,), jnp.float32), 0.5, 1.5)
    nodes_cotangent = scatter_about(seeds[10], (NODES, L), 1.0, 6.0, ((0, 32),))
    coarse_cotangent = scatter_about(seeds[11], (COARSE, L), 1.0, 6.0)
    edges_cotangent = scatter_about(seeds[12], (EDGES, L), 1.0, 6.0, ((0, 32),))
    ups_cotangent = scatter_about(seeds[13], (UPS, L), 1.0, 6.0, ((0, 32),))
    send_rows = draw_send_rows(jax.random.fold_in(seeds[19], 71), 0)
    edge_sender = draw_edge_sender(jax.random.fold_in(seeds[19], 71), 0)
    edge_receiver = touch_ends(jax.random.randint(seeds[16], (EDGES,), 0, NODE_DEV), jax.random.fold_in(seeds[16], 1), 0, NODE_DEV - 1).astype(jnp.int32)
    up_sender = touch_ends(jax.random.randint(seeds[17], (UPS,), 0, NODE_DEV), jax.random.fold_in(seeds[17], 1), 0, NODE_DEV - 1).astype(jnp.int32)
    up_receiver = touch_ends(jax.random.randint(seeds[18], (UPS,), 0, COARSE), jax.random.fold_in(seeds[18], 1), 0, COARSE - 1).astype(jnp.int32)
    return {"node_latents": node_latents, "coarse_latents": coarse_latents, "edge_latents": edge_latents, "up_latents": up_latents, "edge_weight_in": edge_weight_in, "edge_weight_out": edge_weight_out, "edge_gain": edge_gain, "node_weight_in": node_weight_in, "node_weight_out": node_weight_out, "node_gain": node_gain, "nodes_cotangent": nodes_cotangent, "coarse_cotangent": coarse_cotangent, "edges_cotangent": edges_cotangent, "ups_cotangent": ups_cotangent, "send_rows": send_rows, "edge_sender": edge_sender, "edge_receiver": edge_receiver, "up_sender": up_sender, "up_receiver": up_receiver}


EPSILON = 1e-05

def mlp_forward(inputs, residual_base, first_weight, second_weight, gain_vec):
    pre_act = jnp.dot(inputs, first_weight, preferred_element_type=jnp.float32)
    hidden_act = jax.nn.silu(pre_act).astype(jnp.bfloat16)
    projected = jnp.dot(hidden_act, second_weight, preferred_element_type=jnp.float32)
    center = projected - lax.optimization_barrier(jnp.mean(projected, axis=1, keepdims=True))
    inv_std = lax.rsqrt(lax.optimization_barrier(jnp.mean(center * center, axis=1, keepdims=True)) + EPSILON)
    normed = center * inv_std
    return (residual_base + normed * gain_vec, (pre_act, hidden_act, normed, inv_std))

def mlp_backward(inputs, first_weight, second_weight, gain_vec, cache_vals, cotangent):
    pre_act, hidden_act, normed, inv_std = cache_vals
    grad_gain = lax.optimization_barrier(jnp.sum(cotangent * normed, axis=0))
    scaled = cotangent * gain_vec
    grad_proj = inv_std * (scaled - lax.optimization_barrier(jnp.mean(scaled, axis=1, keepdims=True)) - normed * lax.optimization_barrier(jnp.mean(scaled * normed, axis=1, keepdims=True)))
    grad_proj = grad_proj.astype(jnp.bfloat16)
    grad_second = jnp.dot(hidden_act.T, grad_proj, preferred_element_type=jnp.float32)
    grad_hidden = jnp.dot(grad_proj, second_weight.T, preferred_element_type=jnp.float32)
    logistic = jax.nn.sigmoid(pre_act)
    grad_pre = (grad_hidden * logistic * (1.0 + pre_act * (1.0 - logistic))).astype(jnp.bfloat16)
    grad_first = jnp.dot(inputs.T, grad_pre, preferred_element_type=jnp.float32)
    grad_inputs = jnp.dot(grad_pre, first_weight.T, preferred_element_type=jnp.float32)
    return (grad_inputs, grad_first, grad_second, grad_gain)

def reference(node_latents, coarse_latents, edge_latents, up_latents, edge_weight_in, edge_weight_out, edge_gain, node_weight_in, node_weight_out, node_gain, nodes_cotangent, coarse_cotangent, edges_cotangent, ups_cotangent, send_rows, edge_sender, edge_receiver, up_sender, up_receiver):
    devices = N_FACE * N_BAND
    latent_width = node_latents.shape[1]
    edge_block = EDGES // devices
    imports = devices * SLOT
    owner_dev = jnp.arange(EDGES, dtype=jnp.int32) // edge_block
    slot_index = jnp.clip(edge_sender - NODE_DEV, 0, imports - 1)
    source_dev = slot_index // SLOT
    slot_pos = slot_index % SLOT
    sent_row = send_rows[source_dev, owner_dev, slot_pos]
    coarse_id = jnp.clip(edge_sender - NODE_DEV - imports, 0, COARSE - 1)
    sender_glob = jnp.where(edge_sender < NODE_DEV, owner_dev * NODE_DEV + edge_sender, jnp.where(edge_sender < NODE_DEV + imports, source_dev * NODE_DEV + sent_row, NODES + coarse_id)).astype(jnp.int32)
    receiver_glob = (owner_dev * NODE_DEV + edge_receiver).astype(jnp.int32)
    up_owner = jnp.arange(UPS, dtype=jnp.int32) // NODE_DEV
    up_sender_glob = (up_owner * NODE_DEV + up_sender).astype(jnp.int32)
    full_table = jnp.concatenate([node_latents, coarse_latents], 0)
    blocks_sender = sender_glob.reshape(devices, edge_block)
    blocks_receiver = receiver_glob.reshape(devices, edge_block)
    blocks_edges = edge_latents.reshape(devices, edge_block, latent_width)
    blocks_cotangent = edges_cotangent.reshape(devices, edge_block, latent_width)

    def edge_inputs(edges_blk, send_blk, recv_blk):
        return jnp.concatenate([edges_blk, full_table[send_blk], node_latents[recv_blk]], 1)

    def forward_block(carry_vals, block_data):
        edges_blk, send_blk, recv_blk = block_data
        output, cache_vals = mlp_forward(edge_inputs(edges_blk, send_blk, recv_blk), edges_blk.astype(jnp.float32), edge_weight_in, edge_weight_out, edge_gain)
        return (carry_vals, output.astype(jnp.bfloat16))
    unused_carry, new_edges = lax.scan(forward_block, jnp.zeros((), jnp.float32), (blocks_edges, blocks_sender, blocks_receiver))
    fine_total = jax.ops.segment_sum(new_edges.reshape(EDGES, latent_width).astype(jnp.float32), receiver_glob, num_segments=NODES)
    up_inputs = jnp.concatenate([up_latents, node_latents[up_sender_glob], coarse_latents[up_receiver]], 1)
    up_output, up_cache = mlp_forward(up_inputs, up_latents.astype(jnp.float32), edge_weight_in, edge_weight_out, edge_gain)
    new_ups = up_output.astype(jnp.bfloat16)
    coarse_total = jax.ops.segment_sum(new_ups.astype(jnp.float32), up_receiver, num_segments=COARSE)
    node_inputs = jnp.concatenate([node_latents, fine_total.astype(jnp.bfloat16)], 1)
    unused_node, node_cache = mlp_forward(node_inputs, node_latents.astype(jnp.float32), node_weight_in, node_weight_out, node_gain)
    node_grad_inputs, node_first, node_second, node_gain_grad = mlp_backward(node_inputs, node_weight_in, node_weight_out, node_gain, node_cache, nodes_cotangent.astype(jnp.float32))
    coarse_inputs = jnp.concatenate([coarse_latents, coarse_total.astype(jnp.bfloat16)], 1)
    unused_coarse, coarse_cache = mlp_forward(coarse_inputs, coarse_latents.astype(jnp.float32), node_weight_in, node_weight_out, node_gain)
    coarse_grad_inputs, coarse_first, coarse_second, coarse_gain_grad = mlp_backward(coarse_inputs, node_weight_in, node_weight_out, node_gain, coarse_cache, coarse_cotangent.astype(jnp.float32))
    fine_grad = node_grad_inputs[:, latent_width:]
    coarse_grad = coarse_grad_inputs[:, latent_width:]
    grad_table = jnp.concatenate([nodes_cotangent.astype(jnp.float32) + node_grad_inputs[:, :latent_width], coarse_cotangent.astype(jnp.float32) + coarse_grad_inputs[:, :latent_width]], 0)
    up_cotangent = ups_cotangent.astype(jnp.float32) + coarse_grad[up_receiver]
    up_grad_inputs, up_first, up_second, up_gain_grad = mlp_backward(up_inputs, edge_weight_in, edge_weight_out, edge_gain, up_cache, up_cotangent)
    grad_ups = up_cotangent + up_grad_inputs[:, :latent_width]
    grad_table = grad_table.at[up_sender_glob].add(up_grad_inputs[:, latent_width:2 * latent_width])
    grad_table = grad_table.at[NODES + up_receiver].add(up_grad_inputs[:, 2 * latent_width:])

    def backward_block(carry_vals, block_data):
        table_acc, first_acc, second_acc, gain_acc = carry_vals
        edges_blk, send_blk, recv_blk, cotangent_blk = block_data
        inputs = edge_inputs(edges_blk, send_blk, recv_blk)
        unused_out, cache_vals = mlp_forward(inputs, edges_blk.astype(jnp.float32), edge_weight_in, edge_weight_out, edge_gain)
        edge_cotangent = cotangent_blk.astype(jnp.float32) + fine_grad[recv_blk]
        grad_inputs, first_part, second_part, gain_part = mlp_backward(inputs, edge_weight_in, edge_weight_out, edge_gain, cache_vals, edge_cotangent)
        table_acc = table_acc.at[send_blk].add(grad_inputs[:, latent_width:2 * latent_width])
        table_acc = table_acc.at[recv_blk].add(grad_inputs[:, 2 * latent_width:])
        return ((table_acc, first_acc + first_part, second_acc + second_part, gain_acc + gain_part), edge_cotangent + grad_inputs[:, :latent_width])
    final_carry, grad_edges = lax.scan(backward_block, (grad_table, up_first, up_second, up_gain_grad), (blocks_edges, blocks_sender, blocks_receiver, blocks_cotangent))
    grad_table, edge_first, edge_second, edge_gain_grad = final_carry
    edge_scale = 1.0 / math.sqrt(EDGES + UPS)
    node_scale = 1.0 / math.sqrt(NODES + COARSE)
    return (grad_table[:NODES], grad_table[NODES:], grad_edges.reshape(EDGES, latent_width), grad_ups, edge_first * edge_scale, edge_second * edge_scale, edge_gain_grad * edge_scale, (node_first + coarse_first) * node_scale, (node_second + coarse_second) * node_scale, (node_gain_grad + coarse_gain_grad) * node_scale)
```

```python
import functools
import math

import jax
import jax.numpy as jnp
from jax import lax
from jax.experimental import pallas as pl
from jax.experimental.pallas import tpu as pltpu
from jax.sharding import Mesh, PartitionSpec as P

EPSILON = 1e-05
BF = jnp.bfloat16
F32 = jnp.float32
VMEM_LIMIT = 56 * 1024 * 1024


def dot(a, b):
    return lax.dot_general(a, b, (((1,), (0,)), ((), ())), preferred_element_type=F32)


def dot_lt(a, b):
    return lax.dot_general(a, b, (((0,), (0,)), ((), ())), preferred_element_type=F32)


def dot_rt(a, b):
    return lax.dot_general(a, b, (((1,), (1,)), ((), ())), preferred_element_type=F32)


def onehot_t(index_row, rows, offset=0):
    ids = lax.broadcasted_iota(jnp.int32, (rows, index_row.shape[1]), 0) + offset
    return jnp.where(ids == index_row, 1.0, 0.0).astype(BF)


def hidden_of(pre):
    return (pre * jax.nn.sigmoid(pre)).astype(BF)


def normalise(projected):
    center = projected - jnp.mean(projected, axis=1, keepdims=True)
    inv_std = lax.rsqrt(jnp.mean(center * center, axis=1, keepdims=True) + EPSILON)
    return center * inv_std, inv_std


def grad_to_pre(pre, hidden, normed, inv_std, cot, gain, w2):
    gain_part = jnp.sum(cot * normed, axis=0, keepdims=True)
    scaled = cot * gain
    d_proj = (
        inv_std
        * (
            scaled
            - jnp.mean(scaled, axis=1, keepdims=True)
            - normed * jnp.mean(scaled * normed, axis=1, keepdims=True)
        )
    ).astype(BF)
    d_hidden = dot_rt(d_proj, w2)
    logistic = jax.nn.sigmoid(pre)
    d_pre = (d_hidden * logistic * (1.0 + pre * (1.0 - logistic))).astype(BF)
    return gain_part, d_proj, d_pre


def gather_f32(onehot, table):
    high = table.astype(BF)
    low = (table - high.astype(F32)).astype(BF)
    return dot_lt(onehot, high) + dot_lt(onehot, low)


def up_forward_kernel(us, ur, up, node, coarse, w1, w2, gain, p_ref, xs_ref, xr_ref, part_ref):
    lat = up.shape[1]
    xs = dot_lt(onehot_t(us[...], node.shape[0]), node[...]).astype(BF)
    hot_r = onehot_t(ur[...], coarse.shape[0])
    xr = dot_lt(hot_r, coarse[...]).astype(BF)
    pre = dot(up[...], w1[0:lat]) + dot(xs, w1[lat : 2 * lat]) + dot(xr, w1[2 * lat :])
    normed, _ = normalise(dot(hidden_of(pre), w2[...]))
    new = (up[...].astype(F32) + normed * gain[...]).astype(BF)
    p_ref[...] = pre
    xs_ref[...] = xs
    xr_ref[...] = xr
    part_ref[...] = dot(hot_r, new).astype(BF)


def edge_forward_kernel(
    es, er, edge, node, halo, coarse, w1, w2, gain, nw1, nw2, ngain, ncot,
    p_ref, xs_ref, fg_ref, gn_ref, ngw1_ref, ngw2_ref, ngg_ref, acc,
):
    step = pl.program_id(0)
    lat = edge.shape[1]
    n = node.shape[0]
    imports = halo.shape[0]

    @pl.when(step == 0)
    def _():
        acc[...] = jnp.zeros_like(acc)

    sender = es[...]
    xs = (
        dot_lt(onehot_t(sender, n), node[...])
        + dot_lt(onehot_t(sender, imports, n), halo[...])
        + dot_lt(onehot_t(sender, coarse.shape[0], n + imports), coarse[...])
    ).astype(BF)
    hot_r = onehot_t(er[...], n)
    xr = dot_lt(hot_r, node[...]).astype(BF)
    pre = dot(edge[...], w1[0:lat]) + dot(xs, w1[lat : 2 * lat]) + dot(xr, w1[2 * lat :])
    normed, _ = normalise(dot(hidden_of(pre), w2[...]))
    new = (edge[...].astype(F32) + normed * gain[...]).astype(BF)
    p_ref[...] = pre
    xs_ref[...] = xs
    acc[...] += dot(hot_r, new)

    @pl.when(step == pl.num_programs(0) - 1)
    def _():
        total = acc[...].astype(BF)
        node_pre = dot(node[...], nw1[0:lat]) + dot(total, nw1[lat:])
        hidden = hidden_of(node_pre)
        node_normed, inv_std = normalise(dot(hidden, nw2[...]))
        cot = ncot[...].astype(F32)
        gain_part, d_proj, d_pre = grad_to_pre(
            node_pre, hidden, node_normed, inv_std, cot, ngain[...], nw2[...]
        )
        ngg_ref[...] = gain_part
        ngw2_ref[...] = dot_lt(hidden, d_proj)
        ngw1_ref[0:lat] = dot_lt(node[...], d_pre)
        ngw1_ref[lat:] = dot_lt(total, d_pre)
        gn_ref[...] = cot + dot_rt(d_pre, nw1[0:lat])
        fg_ref[...] = dot_rt(d_pre, nw1[lat:])


def edge_backward_kernel(
    es, er, edge, xs, pre_ref, ecot, fg, node, w1, w2, gain,
    ge_ref, gw1_ref, gw2_ref, gg_ref, np_ref, ret_ref, cp_ref, sum_s, sum_r,
):
    step = pl.program_id(0)
    lat = edge.shape[1]
    n = node.shape[0]
    imports = ret_ref.shape[0]

    @pl.when(step == 0)
    def _():
        sum_s[...] = jnp.zeros_like(sum_s)
        sum_r[...] = jnp.zeros_like(sum_r)
        gw1_ref[...] = jnp.zeros_like(gw1_ref)
        gw2_ref[...] = jnp.zeros_like(gw2_ref)
        gg_ref[...] = jnp.zeros_like(gg_ref)

    hot_r = onehot_t(er[...], n)
    cot = ecot[...].astype(F32) + gather_f32(hot_r, fg[...])
    pre = pre_ref[...]
    hidden = hidden_of(pre)
    normed, inv_std = normalise(dot(hidden, w2[...]))
    gain_part, d_proj, d_pre = grad_to_pre(pre, hidden, normed, inv_std, cot, gain[...], w2[...])
    gg_ref[...] += gain_part
    gw2_ref[...] += dot_lt(hidden, d_proj)
    gw1_ref[0:lat] += dot_lt(edge[...], d_pre)
    gw1_ref[lat : 2 * lat] += dot_lt(xs[...], d_pre)
    ge_ref[...] = cot + dot_rt(d_pre, w1[0:lat])
    sum_r[...] += dot(hot_r, d_pre)
    sum_s[...] += dot(onehot_t(es[...], sum_s.shape[0]), d_pre)

    @pl.when(step == pl.num_programs(0) - 1)
    def _():
        w_s = w1[lat : 2 * lat]
        recv = sum_r[...].astype(BF)
        gw1_ref[2 * lat :] = dot_lt(node[...], recv)
        np_ref[...] = dot_rt(sum_s[0:n].astype(BF), w_s) + dot_rt(recv, w1[2 * lat :])
        ret_ref[...] = dot_rt(sum_s[n : n + imports].astype(BF), w_s).astype(BF)
        cp_ref[...] = dot_rt(sum_s[n + imports :].astype(BF), w_s)


def coarse_kernel(
    rows, total_in, ccot, nw1, nw2, ngain, ngw1, ngw2, ngg, cg_ref, after_ref, pay_ref, gg_ref
):
    lat = rows.shape[1]
    total = total_in[...].astype(BF)
    pre = dot(rows[...], nw1[0:lat]) + dot(total, nw1[lat:])
    hidden = hidden_of(pre)
    normed, inv_std = normalise(dot(hidden, nw2[...]))
    cot = ccot[...].astype(F32)
    gain_part, d_proj, d_pre = grad_to_pre(pre, hidden, normed, inv_std, cot, ngain[...], nw2[...])
    cg_ref[...] = dot_rt(d_pre, nw1[lat:]).astype(BF)
    after_ref[...] = cot + dot_rt(d_pre, nw1[0:lat])
    pay_ref[0:lat] = (ngw1[0:lat] + dot_lt(rows[...], d_pre)).astype(BF)
    pay_ref[lat : 2 * lat] = (ngw1[lat:] + dot_lt(total, d_pre)).astype(BF)
    pay_ref[2 * lat :] = (ngw2[...] + dot_lt(hidden, d_proj)).astype(BF)
    gg_ref[...] = ngg[...] + gain_part


def up_backward_kernel(
    us, ur, own, up, xs, xr, pre_ref, ucot, cg, w1, w2, gain, gw1, gw2, gg, cp, after,
    gu_ref, np_ref, pay_ref, ggo_ref, csum,
):
    lat = up.shape[1]
    width = gw2.shape[0]
    coarse = cg.shape[0]
    hot_r = onehot_t(ur[...], coarse)
    cot = ucot[...].astype(F32) + dot_lt(hot_r, cg[...])
    pre = pre_ref[...]
    hidden = hidden_of(pre)
    normed, inv_std = normalise(dot(hidden, w2[...]))
    gain_part, d_proj, d_pre = grad_to_pre(pre, hidden, normed, inv_std, cot, gain[...], w2[...])
    ggo_ref[...] = gg[...] + gain_part
    gu_ref[...] = cot + dot_rt(d_pre, w1[0:lat])
    send = dot(onehot_t(us[...], np_ref.shape[0]), d_pre).astype(BF)
    np_ref[...] = dot_rt(send, w1[lat : 2 * lat])
    csum[...] = cp[...] + dot_rt(dot(hot_r, d_pre).astype(BF), w1[2 * lat :])
    count = after.shape[0]
    mine = pl.ds(pl.multiple_of(own[0] * count, 8), count)
    csum[mine, :] = csum[mine, :] + after[...]
    pay_ref[0:coarse] = csum[...].astype(BF)
    pay_ref[coarse : coarse + lat] = (gw1[0:lat] + dot_lt(up[...], d_pre)).astype(BF)
    pay_ref[coarse + lat : coarse + 2 * lat] = (
        gw1[lat : 2 * lat] + dot_lt(xs[...], d_pre)
    ).astype(BF)
    pay_ref[coarse + 2 * lat : coarse + 3 * lat] = (
        gw1[2 * lat :] + dot_lt(xr[...], d_pre)
    ).astype(BF)
    pay_ref[coarse + 3 * lat :] = (gw2[...] + dot_lt(hidden, d_proj)).astype(BF)


def params(*semantics):
    return pltpu.CompilerParams(
        dimension_semantics=semantics or None, vmem_limit_bytes=VMEM_LIMIT
    )


def shape(rows, cols, dtype):
    return jax.ShapeDtypeStruct((rows, cols), dtype)


def whole(arr):
    return pl.BlockSpec(arr.shape, lambda i: (0,) * len(arr.shape))


def swap(x, axes, count):
    if count == 1:
        return x
    return lax.all_to_all(x, axes, 0, 0, tiled=True)


GROUPS = ("core", ("x", "y"), "z")


def group_sizes():
    return tuple(lax.axis_size(axes) for axes in GROUPS)


def owner_index():
    index = jnp.int32(0)
    for axes in GROUPS:
        index = index * lax.axis_size(axes) + lax.axis_index(axes)
    return index


def reduce_scatter(x):
    for axes in GROUPS:
        count = lax.axis_size(axes)
        got = swap(x.astype(BF), axes, count)
        x = jnp.sum(got.reshape(count, -1, x.shape[1]).astype(F32), axis=0)
    return x


def all_gather(x):
    for axes in reversed(GROUPS):
        count = lax.axis_size(axes)
        copies = jnp.broadcast_to(x[None], (count,) + x.shape).reshape(-1, x.shape[1])
        x = swap(copies, axes, count)
    return x


def sum_rows_everywhere(x):
    for axes in GROUPS:
        count = lax.axis_size(axes)
        copies = jnp.broadcast_to(x[None], (count,) + x.shape).reshape(-1, x.shape[1])
        x = jnp.sum(swap(copies, axes, count).reshape(count, -1, x.shape[1]), axis=0)
    return x


def reduce_everywhere(payload):
    devices = math.prod(group_sizes())
    rows = payload.shape[0]
    padded = -(-rows // (16 * devices)) * 16 * devices
    if padded > rows:
        payload = jnp.pad(payload, ((0, padded - rows), (0, 0)))
    return all_gather(reduce_scatter(payload).astype(BF))[:rows]


def per_device(
    node, coarse, edge, up, w1, w2, gain, nw1, nw2, ngain, ncot, ccot, ecot, ucot,
    send_rows, edge_sender, edge_receiver, up_sender, up_receiver,
):
    n, lat = node.shape
    width = w2.shape[0]
    ccount = coarse.shape[0]
    ecount = edge.shape[0]
    ucount = up.shape[0]
    devices, slots = send_rows.shape[1], send_rows.shape[2]
    imports = devices * slots
    everyone = ("z", "x", "y", "core")
    es, er = edge_sender.reshape(1, ecount), edge_receiver.reshape(1, ecount)
    us, ur = up_sender.reshape(1, ucount), up_receiver.reshape(1, ucount)
    gain_row, ngain_row = gain.reshape(1, lat), ngain.reshape(1, lat)
    own = owner_index()

    table = send_rows.reshape(imports)
    hot_send = (table[:, None] == jnp.arange(n, dtype=jnp.int32)[None, :]).astype(BF)
    outgoing = dot(hot_send, node).astype(BF)
    halo = lax.all_to_all(
        outgoing.reshape(devices, slots, lat), everyone, 0, 0, tiled=True
    ).reshape(imports, lat)

    up_pre, up_xs, up_xr, coarse_part = pl.pallas_call(
        up_forward_kernel,
        out_shape=(
            shape(ucount, width, F32), shape(ucount, lat, BF), shape(ucount, lat, BF),
            shape(ccount, lat, BF),
        ),
        compiler_params=params(),
        name="up_forward",
    )(us, ur, up, node, coarse, w1, w2, gain_row)

    coarse_total = reduce_scatter(coarse_part)

    tile = math.gcd(ecount, 256)
    steps = ecount // tile
    rows_spec = pl.BlockSpec((tile, lat), lambda i: (i, 0))
    index_spec = pl.BlockSpec((1, tile), lambda i: (0, i))
    fixed = lambda r, c: pl.BlockSpec((r, c), lambda i: (0, 0))
    pre, xs, fine_grad, grad_n, ngw1, ngw2, ngg = pl.pallas_call(
        edge_forward_kernel,
        grid=(steps,),
        in_specs=[index_spec, index_spec, rows_spec]
        + [whole(a) for a in (node, halo, coarse, w1, w2, gain_row, nw1, nw2, ngain_row, ncot)],
        out_specs=[
            pl.BlockSpec((tile, width), lambda i: (i, 0)), rows_spec, fixed(n, lat), fixed(n, lat),
            fixed(2 * lat, width), fixed(width, lat), fixed(1, lat),
        ],
        out_shape=(
            shape(ecount, width, F32), shape(ecount, lat, BF), shape(n, lat, F32),
            shape(n, lat, F32), shape(2 * lat, width, F32), shape(width, lat, F32),
            shape(1, lat, F32),
        ),
        scratch_shapes=[pltpu.VMEM((n, lat), F32)],
        compiler_params=params("arbitrary"),
        name="edge_forward",
    )(es, er, edge, node, halo, coarse, w1, w2, gain_row, nw1, nw2, ngain_row, ncot)

    grad_e, gw1, gw2, gg, node_part, returning, coarse_local = pl.pallas_call(
        edge_backward_kernel,
        grid=(steps,),
        in_specs=[
            index_spec, index_spec, rows_spec, rows_spec,
            pl.BlockSpec((tile, width), lambda i: (i, 0)), rows_spec,
        ]
        + [whole(a) for a in (fine_grad, node, w1, w2, gain_row)],
        out_specs=[
            rows_spec, fixed(3 * lat, width), fixed(width, lat), fixed(1, lat), fixed(n, lat),
            fixed(imports, lat), fixed(ccount, lat),
        ],
        out_shape=(
            shape(ecount, lat, F32), shape(3 * lat, width, F32), shape(width, lat, F32),
            shape(1, lat, F32), shape(n, lat, F32), shape(imports, lat, BF),
            shape(ccount, lat, F32),
        ),
        scratch_shapes=[
            pltpu.VMEM((n + imports + ccount, width), F32), pltpu.VMEM((n, width), F32),
        ],
        compiler_params=params("arbitrary"),
        name="edge_backward",
    )(es, er, edge, xs, pre, ecot, fine_grad, node, w1, w2, gain_row)

    returned = lax.all_to_all(
        returning.reshape(devices, slots, lat), everyone, 0, 0, tiled=True
    ).reshape(imports, lat)

    mine = ccount // devices
    padded = -(-mine // 16) * 16
    pad = lambda a: jnp.pad(a, ((0, padded - mine), (0, 0))) if padded > mine else a
    own_coarse = pad(lax.dynamic_slice_in_dim(coarse, own * mine, mine, 0))
    own_cot = pad(lax.dynamic_slice_in_dim(ccot, own * mine, mine, 0))
    coarse_grad, coarse_after, node_pay, ngg_sum = pl.pallas_call(
        coarse_kernel,
        out_shape=(
            shape(padded, lat, BF), shape(padded, lat, F32), shape(2 * lat + width, lat, BF),
            shape(1, lat, F32),
        ),
        compiler_params=params(),
        name="coarse_mlp",
    )(own_coarse, pad(coarse_total), own_cot, nw1, nw2, ngain_row, ngw1, ngw2, ngg)
    coarse_grad_all = all_gather(coarse_grad[:mine])

    node_total = reduce_everywhere(node_pay)

    grad_u, up_node_part, edge_pay, gg_sum = pl.pallas_call(
        up_backward_kernel,
        in_specs=[pl.BlockSpec(memory_space=pltpu.VMEM)] * 2
        + [pl.BlockSpec(memory_space=pltpu.SMEM)]
        + [pl.BlockSpec(memory_space=pltpu.VMEM)] * 14,
        out_shape=(
            shape(ucount, lat, F32), shape(n, lat, F32),
            shape(ccount + 3 * lat + width, lat, BF), shape(1, lat, F32),
        ),
        scratch_shapes=[pltpu.VMEM((ccount, lat), F32)],
        compiler_params=params(),
        name="up_backward",
    )(
        us, ur, own.reshape(1), up, up_xs, up_xr, up_pre, ucot, coarse_grad_all, w1, w2, gain_row,
        gw1, gw2, gg, coarse_local, coarse_after[:mine],
    )
    edge_total = reduce_everywhere(edge_pay)
    gains = sum_rows_everywhere(jnp.concatenate([gg_sum, ngg_sum], 0))

    grad_nodes = (
        grad_n
        + node_part
        + up_node_part
        + lax.dot_general(hot_send, returned, (((0,), (0,)), ((), ())), preferred_element_type=F32)
    )
    edge_scale = 1.0 / math.sqrt((ecount + ucount) * devices)
    node_scale = 1.0 / math.sqrt(n * devices + ccount)
    in_end = ccount + 3 * lat
    return (
        grad_nodes,
        edge_total[:ccount].astype(F32),
        grad_e,
        grad_u,
        edge_total[ccount:in_end].astype(F32) * edge_scale,
        edge_total[in_end:].astype(F32) * edge_scale,
        gains[0] * edge_scale,
        node_total[: 2 * lat].astype(F32) * node_scale,
        node_total[2 * lat :].astype(F32) * node_scale,
        gains[1] * node_scale,
    )


def split_mesh(mesh):
    face, band = mesh.shape["face"], mesh.shape["band"]
    z = 1
    while z * z < face or face % z:
        z += 1
    core = 2 if band % 2 == 0 else 1
    return Mesh(
        mesh.devices.reshape(z, face // z, band // core, core), ("z", "x", "y", "core")
    )


def solution(mesh):
    everyone = ("z", "x", "y", "core")
    rows, split = P(everyone, None), P(everyone)
    return jax.shard_map(
        per_device,
        mesh=split_mesh(mesh),
        in_specs=(
            rows, P(), rows, rows, P(), P(), P(), P(), P(), P(), rows, P(), rows, rows,
            P(everyone, None, None), split, split, split, split,
        ),
        out_specs=(rows, P(), rows, rows, P(), P(), P(), P(), P(), P()),
        check_vma=False,
    )
```

```python
import math

import jax
import jax.numpy as jnp
from jax import lax
from jax.experimental import pallas as pl
from jax.experimental.pallas import tpu as pltpu
from jax.sharding import Mesh, PartitionSpec as P

EPSILON = 1e-05
BF = jnp.bfloat16
F32 = jnp.float32
TAIL = 16
EVERYONE = ("z", "x", "y", "core")
VMEM_LIMIT = 56 * 1024 * 1024


def dot(a, b):
    return lax.dot_general(a, b, (((1,), (0,)), ((), ())), preferred_element_type=F32)


def dot_lt(a, b):
    return lax.dot_general(a, b, (((0,), (0,)), ((), ())), preferred_element_type=F32)


def dot_rt(a, b):
    return lax.dot_general(a, b, (((1,), (1,)), ((), ())), preferred_element_type=F32)


def onehot_t(index_row, rows, offset=0):
    ids = lax.broadcasted_iota(jnp.int32, (rows, index_row.shape[1]), 0) + offset
    return jnp.where(ids == index_row, 1.0, 0.0).astype(BF)


def hidden_of(pre):
    return (pre * jax.nn.sigmoid(pre)).astype(BF)


def normalise(projected):
    center = projected - jnp.mean(projected, axis=1, keepdims=True)
    inv_std = lax.rsqrt(jnp.mean(center * center, axis=1, keepdims=True) + EPSILON)
    return center * inv_std, inv_std


def grad_to_pre(pre, hidden, normed, inv_std, cot, gain, w2):
    gain_part = jnp.sum(cot * normed, axis=0, keepdims=True)
    scaled = cot * gain
    d_proj = (
        inv_std
        * (
            scaled
            - jnp.mean(scaled, axis=1, keepdims=True)
            - normed * jnp.mean(scaled * normed, axis=1, keepdims=True)
        )
    ).astype(BF)
    d_hidden = dot_rt(d_proj, w2)
    logistic = jax.nn.sigmoid(pre)
    d_pre = (d_hidden * logistic * (1.0 + pre * (1.0 - logistic))).astype(BF)
    return gain_part, d_proj, d_pre


def gather_f32(onehot, table):
    high = table.astype(BF)
    low = (table - high.astype(F32)).astype(BF)
    return dot_lt(onehot, high) + dot_lt(onehot, low)


def split_rows(ref, bit, keep_ref, send_ref):
    half = keep_ref.shape[0]
    keep_ref[...] = ref[pl.ds(pl.multiple_of(bit * half, 16), half), :].astype(BF)
    send_ref[...] = ref[pl.ds(pl.multiple_of((1 - bit) * half, 16), half), :].astype(BF)


def fold_split_kernel(bit, keep, recv, keep_ref, send_ref, total):
    total[...] = keep[...].astype(F32) + recv[...].astype(F32)
    split_rows(total, bit[0], keep_ref, send_ref)


def fold_pair_kernel(keep, recv, keep_tail, recv_tail, out_ref):
    rows = keep.shape[0]
    out_ref[0, 0:rows] = (keep[...].astype(F32) + recv[...].astype(F32)).astype(BF)
    out_ref[0, rows:] = (keep_tail[...].astype(F32) + recv_tail[...].astype(F32)).astype(BF)


def fold_group_kernel(got, tail, out_ref):
    rows = got.shape[1]
    out_ref[0, 0:rows] = jnp.sum(got[...].astype(F32), axis=0).astype(BF)
    out_ref[0, rows:] = jnp.sum(tail[...].astype(F32), axis=0).astype(BF)


def up_forward_kernel(
    us, ur, core, up, node, coarse, w1, w2, gain, p_ref, xs_ref, xr_ref, keep_ref, send_ref, part
):
    lat = up.shape[1]
    xs = dot_lt(onehot_t(us[...], node.shape[0]), node[...]).astype(BF)
    hot_r = onehot_t(ur[...], coarse.shape[0])
    xr = dot_lt(hot_r, coarse[...]).astype(BF)
    pre = dot(up[...], w1[0:lat]) + dot(xs, w1[lat : 2 * lat]) + dot(xr, w1[2 * lat :])
    normed, _ = normalise(dot(hidden_of(pre), w2[...]))
    new = (up[...].astype(F32) + normed * gain[...]).astype(BF)
    p_ref[...] = pre
    xs_ref[...] = xs
    xr_ref[...] = xr
    part[...] = dot(hot_r, new)
    split_rows(part, core[0], keep_ref, send_ref)


def edge_forward_kernel(
    es, er, edge, node, halo, coarse, w1, w2, gain, nw1, nw2, ngain, ncot,
    p_ref, xs_ref, fg_ref, gn_ref, ngw1_ref, ngw2_ref, ngg_ref, acc,
):
    step = pl.program_id(0)
    lat = edge.shape[1]
    n = node.shape[0]
    imports = halo.shape[0]

    @pl.when(step == 0)
    def _():
        acc[...] = jnp.zeros_like(acc)

    sender = es[...]
    xs = (
        dot_lt(onehot_t(sender, n), node[...])
        + dot_lt(onehot_t(sender, imports, n), halo[...])
        + dot_lt(onehot_t(sender, coarse.shape[0], n + imports), coarse[...])
    ).astype(BF)
    hot_r = onehot_t(er[...], n)
    xr = dot_lt(hot_r, node[...]).astype(BF)
    pre = dot(edge[...], w1[0:lat]) + dot(xs, w1[lat : 2 * lat]) + dot(xr, w1[2 * lat :])
    normed, _ = normalise(dot(hidden_of(pre), w2[...]))
    new = (edge[...].astype(F32) + normed * gain[...]).astype(BF)
    p_ref[...] = pre
    xs_ref[...] = xs
    acc[...] += dot(hot_r, new)

    @pl.when(step == pl.num_programs(0) - 1)
    def _():
        total = acc[...].astype(BF)
        node_pre = dot(node[...], nw1[0:lat]) + dot(total, nw1[lat:])
        hidden = hidden_of(node_pre)
        node_normed, inv_std = normalise(dot(hidden, nw2[...]))
        cot = ncot[...].astype(F32)
        gain_part, d_proj, d_pre = grad_to_pre(
            node_pre, hidden, node_normed, inv_std, cot, ngain[...], nw2[...]
        )
        ngg_ref[...] = gain_part
        ngw2_ref[...] = dot_lt(hidden, d_proj).astype(BF)
        ngw1_ref[0:lat] = dot_lt(node[...], d_pre).astype(BF)
        ngw1_ref[lat:] = dot_lt(total, d_pre).astype(BF)
        gn_ref[...] = cot + dot_rt(d_pre, nw1[0:lat])
        fg_ref[...] = dot_rt(d_pre, nw1[lat:])


def edge_backward_kernel(
    es, er, edge, xs, pre_ref, ecot, fg, node, w1, w2, gain,
    ge_ref, gw1_out, gw2_out, gg_ref, np_ref, ret_ref, cp_ref, sum_s, sum_r, gw1_ref, gw2_ref,
):
    step = pl.program_id(0)
    lat = edge.shape[1]
    n = node.shape[0]
    imports = ret_ref.shape[0]

    @pl.when(step == 0)
    def _():
        sum_s[...] = jnp.zeros_like(sum_s)
        sum_r[...] = jnp.zeros_like(sum_r)
        gw1_ref[...] = jnp.zeros_like(gw1_ref)
        gw2_ref[...] = jnp.zeros_like(gw2_ref)
        gg_ref[...] = jnp.zeros_like(gg_ref)

    hot_r = onehot_t(er[...], n)
    cot = ecot[...].astype(F32) + gather_f32(hot_r, fg[...])
    pre = pre_ref[...]
    hidden = hidden_of(pre)
    normed, inv_std = normalise(dot(hidden, w2[...]))
    gain_part, d_proj, d_pre = grad_to_pre(pre, hidden, normed, inv_std, cot, gain[...], w2[...])
    gg_ref[...] += gain_part
    gw2_ref[...] += dot_lt(hidden, d_proj)
    gw1_ref[0:lat] += dot_lt(edge[...], d_pre)
    gw1_ref[lat : 2 * lat] += dot_lt(xs[...], d_pre)
    ge_ref[...] = cot + dot_rt(d_pre, w1[0:lat])
    sum_r[...] += dot(hot_r, d_pre)
    sum_s[...] += dot(onehot_t(es[...], sum_s.shape[0]), d_pre)

    @pl.when(step == pl.num_programs(0) - 1)
    def _():
        w_s = w1[lat : 2 * lat]
        recv = sum_r[...].astype(BF)
        gw1_out[0 : 2 * lat] = gw1_ref[...].astype(BF)
        gw1_out[2 * lat :] = dot_lt(node[...], recv).astype(BF)
        gw2_out[...] = gw2_ref[...].astype(BF)
        np_ref[...] = dot_rt(sum_s[0:n].astype(BF), w_s) + dot_rt(recv, w1[2 * lat :])
        ret_ref[...] = dot_rt(sum_s[n : n + imports].astype(BF), w_s).astype(BF)
        cp_ref[...] = dot_rt(sum_s[n + imports :].astype(BF), w_s).astype(BF)


def coarse_kernel(
    core, rows, total_in, ccot, nw1, nw2, ngain, ngw1, ngw2, ngg,
    cg_ref, after_ref, keep_ref, send_ref, gg_ref, pay,
):
    lat = rows.shape[1]
    used = ngw1.shape[0] + ngw2.shape[0]
    total = total_in[...].astype(BF)
    pre = dot(rows[...], nw1[0:lat]) + dot(total, nw1[lat:])
    hidden = hidden_of(pre)
    normed, inv_std = normalise(dot(hidden, nw2[...]))
    cot = ccot[...].astype(F32)
    gain_part, d_proj, d_pre = grad_to_pre(pre, hidden, normed, inv_std, cot, ngain[...], nw2[...])
    cg_ref[...] = dot_rt(d_pre, nw1[lat:]).astype(BF)
    after_ref[...] = cot + dot_rt(d_pre, nw1[0:lat])
    pay[0:lat] = ngw1[0:lat].astype(F32) + dot_lt(rows[...], d_pre)
    pay[lat : 2 * lat] = ngw1[lat:].astype(F32) + dot_lt(total, d_pre)
    pay[2 * lat : used] = ngw2[...].astype(F32) + dot_lt(hidden, d_proj)
    if used < pay.shape[0]:
        pay[used:] = jnp.zeros((pay.shape[0] - used, lat), F32)
    split_rows(pay, core[0], keep_ref, send_ref)
    gg_ref[...] = ngg[...] + gain_part


def up_backward_kernel(
    us, ur, place, up, xs, xr, pre_ref, ucot, cg_own, cg_other, w1, w2, gain, gw1, gw2, gg, ngg,
    cp, after, gu_ref, np_ref, keep_ref, send_ref, csum, pay,
):
    lat = up.shape[1]
    half = cg_own.shape[0]
    coarse = csum.shape[0]
    core = place[1]
    hot_r = onehot_t(ur[...], coarse)
    turned = ur[...] - core * half
    turned = jnp.where(turned < 0, turned + coarse, turned)
    cot = (
        ucot[...].astype(F32)
        + dot_lt(onehot_t(turned, half), cg_own[...])
        + dot_lt(onehot_t(turned, half, half), cg_other[...])
    )
    pre = pre_ref[...]
    hidden = hidden_of(pre)
    normed, inv_std = normalise(dot(hidden, w2[...]))
    gain_part, d_proj, d_pre = grad_to_pre(pre, hidden, normed, inv_std, cot, gain[...], w2[...])
    gu_ref[...] = cot + dot_rt(d_pre, w1[0:lat])
    send = dot(onehot_t(us[...], np_ref.shape[0]), d_pre).astype(BF)
    np_ref[...] = dot_rt(send, w1[lat : 2 * lat])
    csum[...] = cp[...].astype(F32) + dot_rt(dot(hot_r, d_pre).astype(BF), w1[2 * lat :])
    count = after.shape[0]
    mine = pl.ds(pl.multiple_of(place[0] * count, 8), count)
    csum[mine, :] = csum[mine, :] + after[...]
    pay[0:coarse] = csum[...].astype(BF)
    start = coarse
    for x in (up, xs, xr):
        piece = slice(start - coarse, start - coarse + lat)
        pay[start : start + lat] = (gw1[piece].astype(F32) + dot_lt(x[...], d_pre)).astype(BF)
        start += lat
    end = start + gw2.shape[0]
    pay[start:end] = (gw2[...].astype(F32) + dot_lt(hidden, d_proj)).astype(BF)
    if end < pay.shape[0]:
        pay[end:] = jnp.zeros((pay.shape[0] - end, lat), BF)
    rows = pay.shape[0] // 2
    split_rows(pay, core, keep_ref.at[0:rows], send_ref.at[0:rows])
    ids = lax.broadcasted_iota(jnp.int32, (TAIL, lat), 0)
    edge_row = jnp.broadcast_to(gg[...] + gain_part, (TAIL, lat))
    node_row = jnp.broadcast_to(ngg[...], (TAIL, lat))
    tail = jnp.where(ids == 0, edge_row, jnp.where(ids == 1, node_row, 0.0)).astype(BF)
    keep_ref[rows:] = tail
    send_ref[rows:] = tail


def params(*semantics):
    return pltpu.CompilerParams(
        dimension_semantics=semantics or None, vmem_limit_bytes=VMEM_LIMIT
    )


def shape(rows, cols, dtype):
    return jax.ShapeDtypeStruct((rows, cols), dtype)


def whole(arr):
    return pl.BlockSpec(arr.shape, lambda i: (0,) * len(arr.shape))


def swap(x, axes, count):
    if count == 1:
        return x
    return lax.all_to_all(x, axes, 0, 0, tiled=True)


GROUPS = ("core", ("x", "y"), "z")


def group_sizes():
    return tuple(lax.axis_size(axes) for axes in GROUPS)


def owner_index():
    index = jnp.int32(0)
    for axes in GROUPS:
        index = index * lax.axis_size(axes) + lax.axis_index(axes)
    return index


def exchange(x, mask):
    devices = lax.axis_size(EVERYONE)
    if devices == 1:
        return x
    return lax.ppermute(x, EVERYONE, [(i, i ^ mask) for i in range(devices)])


def sum_group(got, count):
    return jnp.sum(got.reshape(count, -1, got.shape[1]).astype(F32), axis=0)


def copies(x, count):
    return jnp.broadcast_to(x[None], (count,) + x.shape).reshape(-1, x.shape[1])


def reduce_rows(keep, send):
    x = keep.astype(F32) + exchange(send, 1).astype(F32)
    for axes in GROUPS[1:]:
        count = lax.axis_size(axes)
        x = sum_group(swap(x.astype(BF), axes, count), count)
    return x


def gather_halves(x):
    for axes in reversed(GROUPS[1:]):
        count = lax.axis_size(axes)
        x = swap(copies(x, count), axes, count)
    return x, exchange(x, 1)


def reduce_with_tail(keep, send):
    cols = keep.shape[1]
    rows = keep.shape[0] - TAIL
    got = exchange(send, 1)
    count = lax.axis_size(GROUPS[1])
    part = rows // count
    main = pl.BlockSpec((part, cols), lambda i: (i, 0))
    tail = pl.BlockSpec((TAIL, cols), lambda i: (rows // TAIL, 0))
    x = pl.pallas_call(
        fold_pair_kernel,
        grid=(count,),
        in_specs=[main, main, tail, tail],
        out_specs=pl.BlockSpec((1, part + TAIL, cols), lambda i: (i, 0, 0)),
        out_shape=jax.ShapeDtypeStruct((count, part + TAIL, cols), BF),
        compiler_params=params("arbitrary"),
        name="fold_pair",
    )(keep, got, keep, got)
    got = swap(x.reshape(-1, cols), GROUPS[1], count).reshape(x.shape)
    rows, group = part, count
    count = lax.axis_size(GROUPS[2])
    part = rows // count
    at = rows // TAIL
    x = pl.pallas_call(
        fold_group_kernel,
        grid=(count,),
        in_specs=[
            pl.BlockSpec((group, part, cols), lambda i: (0, i, 0)),
            pl.BlockSpec((group, TAIL, cols), lambda i: (0, at, 0)),
        ],
        out_specs=pl.BlockSpec((1, part + TAIL, cols), lambda i: (i, 0, 0)),
        out_shape=jax.ShapeDtypeStruct((count, part + TAIL, cols), BF),
        compiler_params=params("arbitrary"),
        name="fold_group",
    )(got, got)
    x = sum_group(swap(x.reshape(-1, cols), GROUPS[2], count), count)
    return x[:part].astype(BF), x[part:]


def bit_masks(devices):
    slow = devices // lax.axis_size("z")
    order = [m for m in (1 << b for b in range(1, devices.bit_length())) if m < devices]
    return [m for m in order if m >= slow] + [m for m in order if m < slow]


def halving_sum(keep, send):
    devices = lax.axis_size(EVERYONE)
    masks = [1] + bit_masks(devices)
    place = lax.axis_index(EVERYONE)
    for mask, after in zip(masks, masks[1:]):
        rows, cols = keep.shape
        bit = ((place & after) > 0).astype(jnp.int32).reshape(1)
        keep, send = pl.pallas_call(
            fold_split_kernel,
            in_specs=[pl.BlockSpec(memory_space=pltpu.SMEM)]
            + [pl.BlockSpec(memory_space=pltpu.VMEM)] * 2,
            out_shape=(shape(rows // 2, cols, BF),) * 2,
            scratch_shapes=[pltpu.VMEM((rows, cols), F32)],
            compiler_params=params(),
            name="fold_split",
        )(bit, keep, exchange(send, mask))
    x = (keep.astype(F32) + exchange(send, masks[-1]).astype(F32)).astype(BF)
    for mask in reversed(masks):
        other = exchange(x, mask)
        x = jnp.where(
            (place & mask) > 0, jnp.concatenate([other, x], 0), jnp.concatenate([x, other], 0)
        )
    return x


def padded_rows(rows, devices):
    return -(-rows // (16 * devices)) * 16 * devices


def per_device(
    node, coarse, edge, up, w1, w2, gain, nw1, nw2, ngain, ncot, ccot, ecot, ucot,
    send_rows, edge_sender, edge_receiver, up_sender, up_receiver,
):
    n, lat = node.shape
    width = w2.shape[0]
    ccount = coarse.shape[0]
    ecount = edge.shape[0]
    ucount = up.shape[0]
    devices, slots = send_rows.shape[1], send_rows.shape[2]
    imports = devices * slots
    es, er = edge_sender.reshape(1, ecount), edge_receiver.reshape(1, ecount)
    us, ur = up_sender.reshape(1, ucount), up_receiver.reshape(1, ucount)
    gain_row, ngain_row = gain.reshape(1, lat), ngain.reshape(1, lat)
    own = owner_index()
    core = lax.axis_index("core").reshape(1)
    in_vmem = pl.BlockSpec(memory_space=pltpu.VMEM)
    in_smem = pl.BlockSpec(memory_space=pltpu.SMEM)

    table = send_rows.reshape(imports)
    hot_send = (table[:, None] == jnp.arange(n, dtype=jnp.int32)[None, :]).astype(BF)
    outgoing = dot(hot_send, node).astype(BF)
    halo = lax.all_to_all(
        outgoing.reshape(devices, slots, lat), EVERYONE, 0, 0, tiled=True
    ).reshape(imports, lat)

    up_pre, up_xs, up_xr, keep, send = pl.pallas_call(
        up_forward_kernel,
        in_specs=[in_vmem] * 2 + [in_smem] + [in_vmem] * 6,
        out_shape=(
            shape(ucount, width, F32), shape(ucount, lat, BF), shape(ucount, lat, BF),
            shape(ccount // 2, lat, BF), shape(ccount // 2, lat, BF),
        ),
        scratch_shapes=[pltpu.VMEM((ccount, lat), F32)],
        compiler_params=params(),
        name="up_forward",
    )(us, ur, core, up, node, coarse, w1, w2, gain_row)

    coarse_total = reduce_rows(keep, send)

    tile = math.gcd(ecount, 256)
    steps = ecount // tile
    rows_spec = pl.BlockSpec((tile, lat), lambda i: (i, 0))
    index_spec = pl.BlockSpec((1, tile), lambda i: (0, i))
    fixed = lambda r, c: pl.BlockSpec((r, c), lambda i: (0, 0))
    pre, xs, fine_grad, grad_n, ngw1, ngw2, ngg = pl.pallas_call(
        edge_forward_kernel,
        grid=(steps,),
        in_specs=[index_spec, index_spec, rows_spec]
        + [whole(a) for a in (node, halo, coarse, w1, w2, gain_row, nw1, nw2, ngain_row, ncot)],
        out_specs=[
            pl.BlockSpec((tile, width), lambda i: (i, 0)), rows_spec, fixed(n, lat), fixed(n, lat),
            fixed(2 * lat, width), fixed(width, lat), fixed(1, lat),
        ],
        out_shape=(
            shape(ecount, width, F32), shape(ecount, lat, BF), shape(n, lat, F32),
            shape(n, lat, F32), shape(2 * lat, width, BF), shape(width, lat, BF),
            shape(1, lat, F32),
        ),
        scratch_shapes=[pltpu.VMEM((n, lat), F32)],
        compiler_params=params("arbitrary"),
        name="edge_forward",
    )(es, er, edge, node, halo, coarse, w1, w2, gain_row, nw1, nw2, ngain_row, ncot)

    grad_e, gw1, gw2, gg, node_part, returning, coarse_local = pl.pallas_call(
        edge_backward_kernel,
        grid=(steps,),
        in_specs=[
            index_spec, index_spec, rows_spec, rows_spec,
            pl.BlockSpec((tile, width), lambda i: (i, 0)), rows_spec,
        ]
        + [whole(a) for a in (fine_grad, node, w1, w2, gain_row)],
        out_specs=[
            rows_spec, fixed(3 * lat, width), fixed(width, lat), fixed(1, lat), fixed(n, lat),
            fixed(imports, lat), fixed(ccount, lat),
        ],
        out_shape=(
            shape(ecount, lat, F32), shape(3 * lat, width, BF), shape(width, lat, BF),
            shape(1, lat, F32), shape(n, lat, F32), shape(imports, lat, BF),
            shape(ccount, lat, BF),
        ),
        scratch_shapes=[
            pltpu.VMEM((n + imports + ccount, width), F32), pltpu.VMEM((n, width), F32),
            pltpu.VMEM((2 * lat, width), F32), pltpu.VMEM((width, lat), F32),
        ],
        compiler_params=params("arbitrary"),
        name="edge_backward",
    )(es, er, edge, xs, pre, ecot, fine_grad, node, w1, w2, gain_row)

    returned = lax.all_to_all(
        returning.reshape(devices, slots, lat), EVERYONE, 0, 0, tiled=True
    ).reshape(imports, lat)

    mine = ccount // devices
    padded = -(-mine // 16) * 16
    pad = lambda a: jnp.pad(a, ((0, padded - mine), (0, 0))) if padded > mine else a
    own_coarse = pad(lax.dynamic_slice_in_dim(coarse, own * mine, mine, 0))
    own_cot = pad(lax.dynamic_slice_in_dim(ccot, own * mine, mine, 0))
    node_rows = padded_rows(2 * lat + width, devices)
    coarse_grad, coarse_after, node_keep, node_send, ngg_sum = pl.pallas_call(
        coarse_kernel,
        in_specs=[in_smem] + [in_vmem] * 9,
        out_shape=(
            shape(padded, lat, BF), shape(padded, lat, F32), shape(node_rows // 2, lat, BF),
            shape(node_rows // 2, lat, BF), shape(1, lat, F32),
        ),
        scratch_shapes=[pltpu.VMEM((node_rows, lat), F32)],
        compiler_params=params(),
        name="coarse_mlp",
    )(core, own_coarse, pad(coarse_total), own_cot, nw1, nw2, ngain_row, ngw1, ngw2, ngg)
    cg_own, cg_other = gather_halves(coarse_grad[:mine])

    node_total = halving_sum(node_keep, node_send)

    edge_rows = padded_rows(ccount + 3 * lat + width, devices)
    grad_u, up_node_part, keep, send = pl.pallas_call(
        up_backward_kernel,
        in_specs=[in_vmem] * 2 + [in_smem] + [in_vmem] * 16,
        out_shape=(
            shape(ucount, lat, F32), shape(n, lat, F32), shape(edge_rows // 2 + TAIL, lat, BF),
            shape(edge_rows // 2 + TAIL, lat, BF),
        ),
        scratch_shapes=[pltpu.VMEM((ccount, lat), F32), pltpu.VMEM((edge_rows, lat), BF)],
        compiler_params=params(),
        name="up_backward",
    )(
        us, ur, jnp.stack([own, core[0]]), up, up_xs, up_xr, up_pre, ucot, cg_own, cg_other,
        w1, w2, gain_row, gw1, gw2, gg, ngg_sum, coarse_local, coarse_after[:mine],
    )
    block, gains = reduce_with_tail(keep, send)
    own_half, other_half = gather_halves(block)
    first = core[0] == 0
    edge_total = jnp.concatenate(
        [jnp.where(first, own_half, other_half), jnp.where(first, other_half, own_half)], 0
    )

    grad_nodes = (
        grad_n
        + node_part
        + up_node_part
        + lax.dot_general(hot_send, returned, (((0,), (0,)), ((), ())), preferred_element_type=F32)
    )
    edge_scale = 1.0 / math.sqrt((ecount + ucount) * devices)
    node_scale = 1.0 / math.sqrt(n * devices + ccount)
    in_end = ccount + 3 * lat
    return (
        grad_nodes,
        edge_total[:ccount].astype(F32),
        grad_e,
        grad_u,
        edge_total[ccount:in_end].astype(F32) * edge_scale,
        edge_total[in_end : in_end + width].astype(F32) * edge_scale,
        gains[0] * edge_scale,
        node_total[: 2 * lat].astype(F32) * node_scale,
        node_total[2 * lat : 2 * lat + width].astype(F32) * node_scale,
        gains[1] * node_scale,
    )


def split_mesh(mesh):
    face, band = mesh.shape["face"], mesh.shape["band"]
    z = 1
    while z * z < face or face % z:
        z += 1
    core = 2 if band % 2 == 0 else 1
    return Mesh(
        mesh.devices.reshape(z, face // z, band // core, core), ("z", "x", "y", "core")
    )


def solution(mesh):
    rows, split = P(EVERYONE, None), P(EVERYONE)
    return jax.shard_map(
        per_device,
        mesh=split_mesh(mesh),
        in_specs=(
            rows, P(), rows, rows, P(), P(), P(), P(), P(), P(), rows, P(), rows, rows,
            P(EVERYONE, None, None), split, split, split, split,
        ),
        out_specs=(rows, P(), rows, rows, P(), P(), P(), P(), P(), P()),
        check_vma=False,
    )
```

```python
import math

import jax
import jax.numpy as jnp
from jax import lax
from jax.experimental import pallas as pl
from jax.experimental.pallas import tpu as pltpu
from jax.sharding import Mesh, PartitionSpec as P

EPSILON = 1e-05
BF = jnp.bfloat16
F32 = jnp.float32
TAIL = 16
EVERYONE = ("z", "x", "y", "core")
VMEM_LIMIT = 56 * 1024 * 1024


def dot(a, b):
    return lax.dot_general(a, b, (((1,), (0,)), ((), ())), preferred_element_type=F32)


def dot_lt(a, b):
    return lax.dot_general(a, b, (((0,), (0,)), ((), ())), preferred_element_type=F32)


def dot_rt(a, b):
    return lax.dot_general(a, b, (((1,), (1,)), ((), ())), preferred_element_type=F32)


def onehot_t(index_row, rows, offset=0):
    ids = lax.broadcasted_iota(jnp.int32, (rows, index_row.shape[1]), 0) + offset
    return jnp.where(ids == index_row, 1.0, 0.0).astype(BF)


def hidden_of(pre):
    return (pre * jax.nn.sigmoid(pre)).astype(BF)


def normalise(projected):
    center = projected - jnp.mean(projected, axis=1, keepdims=True)
    inv_std = lax.rsqrt(jnp.mean(center * center, axis=1, keepdims=True) + EPSILON)
    return center * inv_std, inv_std


def grad_to_pre(pre, hidden, normed, inv_std, cot, gain, w2):
    gain_part = jnp.sum(cot * normed, axis=0, keepdims=True)
    scaled = cot * gain
    d_proj = (
        inv_std
        * (
            scaled
            - jnp.mean(scaled, axis=1, keepdims=True)
            - normed * jnp.mean(scaled * normed, axis=1, keepdims=True)
        )
    ).astype(BF)
    d_hidden = dot_rt(d_proj, w2)
    logistic = jax.nn.sigmoid(pre)
    d_pre = (d_hidden * logistic * (1.0 + pre * (1.0 - logistic))).astype(BF)
    return gain_part, d_proj, d_pre


def gather_f32(onehot, table):
    high = table.astype(BF)
    low = (table - high.astype(F32)).astype(BF)
    return dot_lt(onehot, high) + dot_lt(onehot, low)


def split_rows(ref, bit, keep_ref, send_ref):
    half = keep_ref.shape[0]
    keep_ref[...] = ref[pl.ds(pl.multiple_of(bit * half, 16), half), :].astype(BF)
    send_ref[...] = ref[pl.ds(pl.multiple_of((1 - bit) * half, 16), half), :].astype(BF)


def fold_split_kernel(bit, keep, recv, keep_ref, send_ref, total):
    total[...] = keep[...].astype(F32) + recv[...].astype(F32)
    split_rows(total, bit[0], keep_ref, send_ref)


def fold_pair_kernel(keep, recv, keep_tail, recv_tail, out_ref):
    rows = keep.shape[0]
    out_ref[0, 0:rows] = (keep[...].astype(F32) + recv[...].astype(F32)).astype(BF)
    out_ref[0, rows:] = (keep_tail[...].astype(F32) + recv_tail[...].astype(F32)).astype(BF)


def fold_group_kernel(got, tail, out_ref):
    rows = got.shape[1]
    out_ref[0, 0:rows] = jnp.sum(got[...].astype(F32), axis=0).astype(BF)
    out_ref[0, rows:] = jnp.sum(tail[...].astype(F32), axis=0).astype(BF)


def up_forward_kernel(
    us, ur, core, up, node, coarse, w1, w2, gain, p_ref, xs_ref, xr_ref, keep_ref, send_ref, part
):
    lat = up.shape[1]
    xs = dot_lt(onehot_t(us[...], node.shape[0]), node[...]).astype(BF)
    hot_r = onehot_t(ur[...], coarse.shape[0])
    xr = dot_lt(hot_r, coarse[...]).astype(BF)
    pre = dot(up[...], w1[0:lat]) + dot(xs, w1[lat : 2 * lat]) + dot(xr, w1[2 * lat :])
    normed, _ = normalise(dot(hidden_of(pre), w2[...]))
    new = (up[...].astype(F32) + normed * gain[...]).astype(BF)
    p_ref[...] = pre
    xs_ref[...] = xs
    xr_ref[...] = xr
    part[...] = dot(hot_r, new)
    split_rows(part, core[0], keep_ref, send_ref)


def edge_forward_kernel(
    es, er, edge, node, halo, coarse, w1, w2, gain, p_ref, xs_ref, total_ref, acc
):
    step = pl.program_id(0)
    lat = edge.shape[1]
    n = node.shape[0]
    imports = halo.shape[0]

    @pl.when(step == 0)
    def _():
        acc[...] = jnp.zeros_like(acc)

    sender = es[...]
    xs = (
        dot_lt(onehot_t(sender, n), node[...])
        + dot_lt(onehot_t(sender, imports, n), halo[...])
        + dot_lt(onehot_t(sender, coarse.shape[0], n + imports), coarse[...])
    ).astype(BF)
    hot_r = onehot_t(er[...], n)
    xr = dot_lt(hot_r, node[...]).astype(BF)
    pre = dot(edge[...], w1[0:lat]) + dot(xs, w1[lat : 2 * lat]) + dot(xr, w1[2 * lat :])
    normed, _ = normalise(dot(hidden_of(pre), w2[...]))
    new = (edge[...].astype(F32) + normed * gain[...]).astype(BF)
    p_ref[...] = pre
    xs_ref[...] = xs
    acc[...] += dot(hot_r, new)

    @pl.when(step == pl.num_programs(0) - 1)
    def _():
        total_ref[...] = acc[...].astype(BF)


def node_kernel(
    node, total_in, nw1, nw2, ngain, ncot, fg_ref, gn_ref, ngw1_ref, ngw2_ref, ngg_ref
):
    lat = node.shape[1]
    total = total_in[...]
    node_pre = dot(node[...], nw1[0:lat]) + dot(total, nw1[lat:])
    hidden = hidden_of(node_pre)
    node_normed, inv_std = normalise(dot(hidden, nw2[...]))
    cot = ncot[...].astype(F32)
    gain_part, d_proj, d_pre = grad_to_pre(
        node_pre, hidden, node_normed, inv_std, cot, ngain[...], nw2[...]
    )
    ngg_ref[...] = gain_part
    ngw2_ref[...] = dot_lt(hidden, d_proj).astype(BF)
    ngw1_ref[0:lat] = dot_lt(node[...], d_pre).astype(BF)
    ngw1_ref[lat:] = dot_lt(total, d_pre).astype(BF)
    gn_ref[...] = cot + dot_rt(d_pre, nw1[0:lat])
    fg_ref[...] = dot_rt(d_pre, nw1[lat:])


def edge_cotangent_kernel(
    er, edge, pre_ref, ecot, fg, w1, w2, gain, ge_ref, dp_ref, gw2_out, gg_ref, gw2
):
    step = pl.program_id(0)
    lat = edge.shape[1]

    @pl.when(step == 0)
    def _():
        gw2[...] = jnp.zeros_like(gw2)
        gg_ref[...] = jnp.zeros_like(gg_ref)

    cot = ecot[...].astype(F32) + gather_f32(onehot_t(er[...], fg.shape[0]), fg[...])
    pre = pre_ref[...]
    hidden = hidden_of(pre)
    normed, inv_std = normalise(dot(hidden, w2[...]))
    gain_part, d_proj, d_pre = grad_to_pre(pre, hidden, normed, inv_std, cot, gain[...], w2[...])
    gg_ref[...] += gain_part
    gw2[...] += dot_lt(hidden, d_proj)
    ge_ref[...] = cot + dot_rt(d_pre, w1[0:lat])
    dp_ref[...] = d_pre

    @pl.when(step == pl.num_programs(0) - 1)
    def _():
        gw2_out[...] = gw2[...].astype(BF)


def edge_product_kernel(
    es, er, edge, xs, dp, node, w1, gw1_out, np_ref, ret_ref, cp_ref, sum_s, sum_r, gw1
):
    step = pl.program_id(0)
    lat = edge.shape[1]
    n = node.shape[0]
    imports = ret_ref.shape[0]

    @pl.when(step == 0)
    def _():
        sum_s[...] = jnp.zeros_like(sum_s)
        sum_r[...] = jnp.zeros_like(sum_r)
        gw1[...] = jnp.zeros_like(gw1)

    d_pre = dp[...]
    gw1[0:lat] += dot_lt(edge[...], d_pre)
    gw1[lat:] += dot_lt(xs[...], d_pre)
    sum_r[...] += dot(onehot_t(er[...], n), d_pre)
    sum_s[...] += dot(onehot_t(es[...], sum_s.shape[0]), d_pre)

    @pl.when(step == pl.num_programs(0) - 1)
    def _():
        w_s = w1[lat : 2 * lat]
        recv = sum_r[...].astype(BF)
        gw1_out[0 : 2 * lat] = gw1[...].astype(BF)
        gw1_out[2 * lat :] = dot_lt(node[...], recv).astype(BF)
        np_ref[...] = dot_rt(sum_s[0:n].astype(BF), w_s) + dot_rt(recv, w1[2 * lat :])
        ret_ref[...] = dot_rt(sum_s[n : n + imports].astype(BF), w_s).astype(BF)
        cp_ref[...] = dot_rt(sum_s[n + imports :].astype(BF), w_s).astype(BF)


def coarse_kernel(
    core, rows, total_in, ccot, nw1, nw2, ngain, ngw1, ngw2, ngg,
    cg_ref, after_ref, keep_ref, send_ref, gg_ref, pay,
):
    lat = rows.shape[1]
    used = ngw1.shape[0] + ngw2.shape[0]
    total = total_in[...].astype(BF)
    pre = dot(rows[...], nw1[0:lat]) + dot(total, nw1[lat:])
    hidden = hidden_of(pre)
    normed, inv_std = normalise(dot(hidden, nw2[...]))
    cot = ccot[...].astype(F32)
    gain_part, d_proj, d_pre = grad_to_pre(pre, hidden, normed, inv_std, cot, ngain[...], nw2[...])
    cg_ref[...] = dot_rt(d_pre, nw1[lat:]).astype(BF)
    after_ref[...] = cot + dot_rt(d_pre, nw1[0:lat])
    pay[0:lat] = ngw1[0:lat].astype(F32) + dot_lt(rows[...], d_pre)
    pay[lat : 2 * lat] = ngw1[lat:].astype(F32) + dot_lt(total, d_pre)
    pay[2 * lat : used] = ngw2[...].astype(F32) + dot_lt(hidden, d_proj)
    if used < pay.shape[0]:
        pay[used:] = jnp.zeros((pay.shape[0] - used, lat), F32)
    split_rows(pay, core[0], keep_ref, send_ref)
    gg_ref[...] = ngg[...] + gain_part


def up_backward_kernel(
    us, ur, place, up, xs, xr, pre_ref, ucot, cg_own, cg_other, w1, w2, gain, gw1, gw2, gg, ngg,
    cp, after, gu_ref, np_ref, keep_ref, send_ref, csum, pay,
):
    lat = up.shape[1]
    half = cg_own.shape[0]
    coarse = csum.shape[0]
    core = place[1]
    hot_r = onehot_t(ur[...], coarse)
    turned = ur[...] - core * half
    turned = jnp.where(turned < 0, turned + coarse, turned)
    cot = (
        ucot[...].astype(F32)
        + dot_lt(onehot_t(turned, half), cg_own[...])
        + dot_lt(onehot_t(turned, half, half), cg_other[...])
    )
    pre = pre_ref[...]
    hidden = hidden_of(pre)
    normed, inv_std = normalise(dot(hidden, w2[...]))
    gain_part, d_proj, d_pre = grad_to_pre(pre, hidden, normed, inv_std, cot, gain[...], w2[...])
    gu_ref[...] = cot + dot_rt(d_pre, w1[0:lat])
    send = dot(onehot_t(us[...], np_ref.shape[0]), d_pre).astype(BF)
    np_ref[...] = dot_rt(send, w1[lat : 2 * lat])
    csum[...] = cp[...].astype(F32) + dot_rt(dot(hot_r, d_pre).astype(BF), w1[2 * lat :])
    count = after.shape[0]
    mine = pl.ds(pl.multiple_of(place[0] * count, 8), count)
    csum[mine, :] = csum[mine, :] + after[...]
    pay[0:coarse] = csum[...].astype(BF)
    start = coarse
    for x in (up, xs, xr):
        piece = slice(start - coarse, start - coarse + lat)
        pay[start : start + lat] = (gw1[piece].astype(F32) + dot_lt(x[...], d_pre)).astype(BF)
        start += lat
    end = start + gw2.shape[0]
    pay[start:end] = (gw2[...].astype(F32) + dot_lt(hidden, d_proj)).astype(BF)
    if end < pay.shape[0]:
        pay[end:] = jnp.zeros((pay.shape[0] - end, lat), BF)
    rows = pay.shape[0] // 2
    split_rows(pay, core, keep_ref.at[0:rows], send_ref.at[0:rows])
    ids = lax.broadcasted_iota(jnp.int32, (TAIL, lat), 0)
    edge_row = jnp.broadcast_to(gg[...] + gain_part, (TAIL, lat))
    node_row = jnp.broadcast_to(ngg[...], (TAIL, lat))
    tail = jnp.where(ids == 0, edge_row, jnp.where(ids == 1, node_row, 0.0)).astype(BF)
    keep_ref[rows:] = tail
    send_ref[rows:] = tail


def params(*semantics):
    return pltpu.CompilerParams(
        dimension_semantics=semantics or None, vmem_limit_bytes=VMEM_LIMIT
    )


def cost(micros):
    return pl.CostEstimate(
        flops=int(micros * 1.1e9), transcendentals=0, bytes_accessed=int(micros * 3.0e6)
    )


def shape(rows, cols, dtype):
    return jax.ShapeDtypeStruct((rows, cols), dtype)


def whole(arr):
    return pl.BlockSpec(arr.shape, lambda i: (0,) * len(arr.shape))


def swap(x, axes, count):
    if count == 1:
        return x
    return lax.all_to_all(x, axes, 0, 0, tiled=True)


GROUPS = ("core", ("x", "y"), "z")


def group_sizes():
    return tuple(lax.axis_size(axes) for axes in GROUPS)


def owner_index():
    index = jnp.int32(0)
    for axes in GROUPS:
        index = index * lax.axis_size(axes) + lax.axis_index(axes)
    return index


def exchange(x, mask):
    devices = lax.axis_size(EVERYONE)
    if devices == 1:
        return x
    return lax.ppermute(x, EVERYONE, [(i, i ^ mask) for i in range(devices)])


def sum_group(got, count):
    return jnp.sum(got.reshape(count, -1, got.shape[1]).astype(F32), axis=0)


def copies(x, count):
    return jnp.broadcast_to(x[None], (count,) + x.shape).reshape(-1, x.shape[1])


def reduce_rows(keep, send):
    x = keep.astype(F32) + exchange(send, 1).astype(F32)
    for axes in GROUPS[1:]:
        count = lax.axis_size(axes)
        x = sum_group(swap(x.astype(BF), axes, count), count)
    return x


def gather_halves(x):
    for axes in reversed(GROUPS[1:]):
        count = lax.axis_size(axes)
        x = swap(copies(x, count), axes, count)
    return x, exchange(x, 1)


def reduce_with_tail(keep, send):
    cols = keep.shape[1]
    rows = keep.shape[0] - TAIL
    got = exchange(send, 1)
    count = lax.axis_size(GROUPS[1])
    part = rows // count
    main = pl.BlockSpec((part, cols), lambda i: (i, 0))
    tail = pl.BlockSpec((TAIL, cols), lambda i: (rows // TAIL, 0))
    x = pl.pallas_call(
        fold_pair_kernel,
        grid=(count,),
        in_specs=[main, main, tail, tail],
        out_specs=pl.BlockSpec((1, part + TAIL, cols), lambda i: (i, 0, 0)),
        out_shape=jax.ShapeDtypeStruct((count, part + TAIL, cols), BF),
        compiler_params=params("arbitrary"),
        name="fold_pair",
    )(keep, got, keep, got)
    got = swap(x.reshape(-1, cols), GROUPS[1], count).reshape(x.shape)
    rows, group = part, count
    count = lax.axis_size(GROUPS[2])
    part = rows // count
    at = rows // TAIL
    x = pl.pallas_call(
        fold_group_kernel,
        grid=(count,),
        in_specs=[
            pl.BlockSpec((group, part, cols), lambda i: (0, i, 0)),
            pl.BlockSpec((group, TAIL, cols), lambda i: (0, at, 0)),
        ],
        out_specs=pl.BlockSpec((1, part + TAIL, cols), lambda i: (i, 0, 0)),
        out_shape=jax.ShapeDtypeStruct((count, part + TAIL, cols), BF),
        compiler_params=params("arbitrary"),
        name="fold_group",
    )(got, got)
    x = sum_group(swap(x.reshape(-1, cols), GROUPS[2], count), count)
    return x[:part].astype(BF), x[part:]


def bit_masks(devices):
    slow = devices // lax.axis_size("z")
    order = [m for m in (1 << b for b in range(1, devices.bit_length())) if m < devices]
    return [m for m in order if m >= slow] + [m for m in order if m < slow]


def halving_sum(keep, send):
    devices = lax.axis_size(EVERYONE)
    masks = [1] + bit_masks(devices)
    place = lax.axis_index(EVERYONE)
    for mask, after in zip(masks, masks[1:]):
        rows, cols = keep.shape
        bit = ((place & after) > 0).astype(jnp.int32).reshape(1)
        keep, send = pl.pallas_call(
            fold_split_kernel,
            in_specs=[pl.BlockSpec(memory_space=pltpu.SMEM)]
            + [pl.BlockSpec(memory_space=pltpu.VMEM)] * 2,
            out_shape=(shape(rows // 2, cols, BF),) * 2,
            scratch_shapes=[pltpu.VMEM((rows, cols), F32)],
            compiler_params=params(),
            name="fold_split",
        )(bit, keep, exchange(send, mask))
    x = (keep.astype(F32) + exchange(send, masks[-1]).astype(F32)).astype(BF)
    for mask in reversed(masks):
        other = exchange(x, mask)
        x = jnp.where(
            (place & mask) > 0, jnp.concatenate([other, x], 0), jnp.concatenate([x, other], 0)
        )
    return x


def padded_rows(rows, devices):
    return -(-rows // (16 * devices)) * 16 * devices


def per_device(
    node, coarse, edge, up, w1, w2, gain, nw1, nw2, ngain, ncot, ccot, ecot, ucot,
    send_rows, edge_sender, edge_receiver, up_sender, up_receiver,
):
    n, lat = node.shape
    width = w2.shape[0]
    ccount = coarse.shape[0]
    ecount = edge.shape[0]
    ucount = up.shape[0]
    devices, slots = send_rows.shape[1], send_rows.shape[2]
    imports = devices * slots
    es, er = edge_sender.reshape(1, ecount), edge_receiver.reshape(1, ecount)
    us, ur = up_sender.reshape(1, ucount), up_receiver.reshape(1, ucount)
    gain_row, ngain_row = gain.reshape(1, lat), ngain.reshape(1, lat)
    own = owner_index()
    core = lax.axis_index("core").reshape(1)
    in_vmem = pl.BlockSpec(memory_space=pltpu.VMEM)
    in_smem = pl.BlockSpec(memory_space=pltpu.SMEM)

    table = send_rows.reshape(imports)
    hot_send = (table[:, None] == jnp.arange(n, dtype=jnp.int32)[None, :]).astype(BF)
    outgoing = dot(hot_send, node).astype(BF)
    halo = lax.all_to_all(
        outgoing.reshape(devices, slots, lat), EVERYONE, 0, 0, tiled=True
    ).reshape(imports, lat)

    up_pre, up_xs, up_xr, keep, send = pl.pallas_call(
        up_forward_kernel,
        in_specs=[in_vmem] * 2 + [in_smem] + [in_vmem] * 6,
        out_shape=(
            shape(ucount, width, F32), shape(ucount, lat, BF), shape(ucount, lat, BF),
            shape(ccount // 2, lat, BF), shape(ccount // 2, lat, BF),
        ),
        scratch_shapes=[pltpu.VMEM((ccount, lat), F32)],
        compiler_params=params(),
        cost_estimate=cost(5.0),
        name="up_forward",
    )(us, ur, core, up, node, coarse, w1, w2, gain_row)

    coarse_total = reduce_rows(keep, send)

    tile = math.gcd(ecount, 256)
    steps = ecount // tile
    rows_spec = pl.BlockSpec((tile, lat), lambda i: (i, 0))
    index_spec = pl.BlockSpec((1, tile), lambda i: (0, i))
    fixed = lambda r, c: pl.BlockSpec((r, c), lambda i: (0, 0))
    pre, xs, fine_total = pl.pallas_call(
        edge_forward_kernel,
        grid=(steps,),
        in_specs=[index_spec, index_spec, rows_spec]
        + [whole(a) for a in (node, halo, coarse, w1, w2, gain_row)],
        out_specs=[pl.BlockSpec((tile, width), lambda i: (i, 0)), rows_spec, fixed(n, lat)],
        out_shape=(shape(ecount, width, F32), shape(ecount, lat, BF), shape(n, lat, BF)),
        scratch_shapes=[pltpu.VMEM((n, lat), F32)],
        compiler_params=params("arbitrary"),
        cost_estimate=cost(9.0),
        name="edge_forward",
    )(es, er, edge, node, halo, coarse, w1, w2, gain_row)

    fine_grad, grad_n, ngw1, ngw2, ngg = pl.pallas_call(
        node_kernel,
        out_shape=(
            shape(n, lat, F32), shape(n, lat, F32), shape(2 * lat, width, BF),
            shape(width, lat, BF), shape(1, lat, F32),
        ),
        compiler_params=params(),
        cost_estimate=cost(5.0),
        name="node_mlp",
    )(node, fine_total, nw1, nw2, ngain_row, ncot)

    grad_e, d_pre, gw2, gg = pl.pallas_call(
        edge_cotangent_kernel,
        grid=(steps,),
        in_specs=[
            index_spec, rows_spec, pl.BlockSpec((tile, width), lambda i: (i, 0)), rows_spec,
        ]
        + [whole(a) for a in (fine_grad, w1, w2, gain_row)],
        out_specs=[
            rows_spec, pl.BlockSpec((tile, width), lambda i: (i, 0)), fixed(width, lat),
            fixed(1, lat),
        ],
        out_shape=(
            shape(ecount, lat, F32), shape(ecount, width, BF), shape(width, lat, BF),
            shape(1, lat, F32),
        ),
        scratch_shapes=[pltpu.VMEM((width, lat), F32)],
        compiler_params=params("arbitrary"),
        cost_estimate=cost(8.0),
        name="edge_cotangent",
    )(er, edge, pre, ecot, fine_grad, w1, w2, gain_row)

    gw1, node_part, returning, coarse_local = pl.pallas_call(
        edge_product_kernel,
        grid=(steps,),
        in_specs=[
            index_spec, index_spec, rows_spec, rows_spec,
            pl.BlockSpec((tile, width), lambda i: (i, 0)),
        ]
        + [whole(a) for a in (node, w1)],
        out_specs=[
            fixed(3 * lat, width), fixed(n, lat), fixed(imports, lat), fixed(ccount, lat),
        ],
        out_shape=(
            shape(3 * lat, width, BF), shape(n, lat, F32), shape(imports, lat, BF),
            shape(ccount, lat, BF),
        ),
        scratch_shapes=[
            pltpu.VMEM((n + imports + ccount, width), F32), pltpu.VMEM((n, width), F32),
            pltpu.VMEM((2 * lat, width), F32),
        ],
        compiler_params=params("arbitrary"),
        cost_estimate=cost(9.0),
        name="edge_product",
    )(es, er, edge, xs, d_pre, node, w1)

    returned = lax.all_to_all(
        returning.reshape(devices, slots, lat), EVERYONE, 0, 0, tiled=True
    ).reshape(imports, lat)

    mine = ccount // devices
    padded = -(-mine // 16) * 16
    pad = lambda a: jnp.pad(a, ((0, padded - mine), (0, 0))) if padded > mine else a
    own_coarse = pad(lax.dynamic_slice_in_dim(coarse, own * mine, mine, 0))
    own_cot = pad(lax.dynamic_slice_in_dim(ccot, own * mine, mine, 0))
    node_rows = padded_rows(2 * lat + width, devices)
    coarse_grad, coarse_after, node_keep, node_send, ngg_sum = pl.pallas_call(
        coarse_kernel,
        in_specs=[in_smem] + [in_vmem] * 9,
        out_shape=(
            shape(padded, lat, BF), shape(padded, lat, F32), shape(node_rows // 2, lat, BF),
            shape(node_rows // 2, lat, BF), shape(1, lat, F32),
        ),
        scratch_shapes=[pltpu.VMEM((node_rows, lat), F32)],
        compiler_params=params(),
        cost_estimate=cost(5.0),
        name="coarse_mlp",
    )(core, own_coarse, pad(coarse_total), own_cot, nw1, nw2, ngain_row, ngw1, ngw2, ngg)
    cg_own, cg_other = gather_halves(coarse_grad[:mine])

    node_total = halving_sum(node_keep, node_send)

    edge_rows = padded_rows(ccount + 3 * lat + width, devices)
    grad_u, up_node_part, keep, send = pl.pallas_call(
        up_backward_kernel,
        in_specs=[in_vmem] * 2 + [in_smem] + [in_vmem] * 16,
        out_shape=(
            shape(ucount, lat, F32), shape(n, lat, F32), shape(edge_rows // 2 + TAIL, lat, BF),
            shape(edge_rows // 2 + TAIL, lat, BF),
        ),
        scratch_shapes=[pltpu.VMEM((ccount, lat), F32), pltpu.VMEM((edge_rows, lat), BF)],
        compiler_params=params(),
        cost_estimate=cost(8.0),
        name="up_backward",
    )(
        us, ur, jnp.stack([own, core[0]]), up, up_xs, up_xr, up_pre, ucot, cg_own, cg_other,
        w1, w2, gain_row, gw1, gw2, gg, ngg_sum, coarse_local, coarse_after[:mine],
    )
    block, gains = reduce_with_tail(keep, send)
    own_half, other_half = gather_halves(block)
    first = core[0] == 0
    edge_total = jnp.concatenate(
        [jnp.where(first, own_half, other_half), jnp.where(first, other_half, own_half)], 0
    )

    grad_nodes = (
        grad_n
        + node_part
        + up_node_part
        + lax.dot_general(hot_send, returned, (((0,), (0,)), ((), ())), preferred_element_type=F32)
    )
    edge_scale = 1.0 / math.sqrt((ecount + ucount) * devices)
    node_scale = 1.0 / math.sqrt(n * devices + ccount)
    in_end = ccount + 3 * lat
    return (
        grad_nodes,
        edge_total[:ccount].astype(F32),
        grad_e,
        grad_u,
        edge_total[ccount:in_end].astype(F32) * edge_scale,
        edge_total[in_end : in_end + width].astype(F32) * edge_scale,
        gains[0] * edge_scale,
        node_total[: 2 * lat].astype(F32) * node_scale,
        node_total[2 * lat : 2 * lat + width].astype(F32) * node_scale,
        gains[1] * node_scale,
    )


def split_mesh(mesh):
    face, band = mesh.shape["face"], mesh.shape["band"]
    z = 1
    while z * z < face or face % z:
        z += 1
    core = 2 if band % 2 == 0 else 1
    return Mesh(
        mesh.devices.reshape(z, face // z, band // core, core), ("z", "x", "y", "core")
    )


def solution(mesh):
    rows, split = P(EVERYONE, None), P(EVERYONE)
    return jax.shard_map(
        per_device,
        mesh=split_mesh(mesh),
        in_specs=(
            rows, P(), rows, rows, P(), P(), P(), P(), P(), P(), rows, P(), rows, rows,
            P(EVERYONE, None, None), split, split, split, split,
        ),
        out_specs=(rows, P(), rows, rows, P(), P(), P(), P(), P(), P()),
        check_vma=False,
    )
```

```python
import math

import jax
import jax.numpy as jnp
from jax import lax
from jax.experimental import pallas as pl
from jax.experimental.pallas import tpu as pltpu
from jax.sharding import Mesh, PartitionSpec as P

EPSILON = 1e-05
BF = jnp.bfloat16
F32 = jnp.float32
TAIL = 16
EVERYONE = ("z", "x", "y", "core")
VMEM_LIMIT = 56 * 1024 * 1024


def dot(a, b):
    return lax.dot_general(a, b, (((1,), (0,)), ((), ())), preferred_element_type=F32)


def dot_lt(a, b):
    return lax.dot_general(a, b, (((0,), (0,)), ((), ())), preferred_element_type=F32)


def dot_rt(a, b):
    return lax.dot_general(a, b, (((1,), (1,)), ((), ())), preferred_element_type=F32)


def onehot_t(index_row, rows, offset=0):
    ids = lax.broadcasted_iota(jnp.int32, (rows, index_row.shape[1]), 0) + offset
    return jnp.where(ids == index_row, 1.0, 0.0).astype(BF)


def hidden_of(pre):
    return (pre * jax.nn.sigmoid(pre)).astype(BF)


def normalise(projected):
    center = projected - jnp.mean(projected, axis=1, keepdims=True)
    inv_std = lax.rsqrt(jnp.mean(center * center, axis=1, keepdims=True) + EPSILON)
    return center * inv_std, inv_std


def grad_to_pre(pre, normed, inv_std, cot, gain, w2):
    gain_part = jnp.sum(cot * normed, axis=0, keepdims=True)
    scaled = cot * gain
    d_proj = (
        inv_std
        * (
            scaled
            - jnp.mean(scaled, axis=1, keepdims=True)
            - normed * jnp.mean(scaled * normed, axis=1, keepdims=True)
        )
    ).astype(BF)
    d_hidden = dot_rt(d_proj, w2)
    logistic = jax.nn.sigmoid(pre)
    d_pre = (d_hidden * logistic * (1.0 + pre * (1.0 - logistic))).astype(BF)
    return gain_part, d_proj, d_pre


def gather_f32(onehot, table):
    high = table.astype(BF)
    low = (table - high.astype(F32)).astype(BF)
    return dot_lt(onehot, high) + dot_lt(onehot, low)


def split_rows(ref, bit, keep_ref, send_ref):
    half = keep_ref.shape[0]
    keep_ref[...] = ref[pl.ds(pl.multiple_of(bit * half, 16), half), :].astype(BF)
    send_ref[...] = ref[pl.ds(pl.multiple_of((1 - bit) * half, 16), half), :].astype(BF)


def fold_split_kernel(bit, keep, recv, keep_ref, send_ref):
    half = keep_ref.shape[0]
    for side, out_ref in ((bit[0], keep_ref), (1 - bit[0], send_ref)):
        rows = pl.ds(pl.multiple_of(side * half, 16), half)
        out_ref[...] = (keep[rows, :].astype(F32) + recv[rows, :].astype(F32)).astype(BF)


def fold_pair_kernel(keep, recv, out_ref):
    count, rows, _ = out_ref.shape
    rows -= TAIL
    tail = (keep[count * rows :].astype(F32) + recv[count * rows :].astype(F32)).astype(BF)
    for k in range(count):
        piece = slice(k * rows, (k + 1) * rows)
        out_ref[k, 0:rows] = (keep[piece].astype(F32) + recv[piece].astype(F32)).astype(BF)
        out_ref[k, rows:] = tail


def fold_group_kernel(got, out_ref):
    group = got.shape[0]
    count, rows, _ = out_ref.shape
    rows -= TAIL

    def total(at, size):
        piece = slice(at, at + size)
        acc = got[0, piece].astype(F32)
        for k in range(1, group):
            acc += got[k, piece].astype(F32)
        return acc.astype(BF)

    tail = total(count * rows, TAIL)
    for k in range(count):
        out_ref[k, 0:rows] = total(k * rows, rows)
        out_ref[k, rows:] = tail


def up_forward_kernel(
    us, ur, core, up, node, coarse, w1, w2, gain, p_ref, xs_ref, xr_ref, keep_ref, send_ref, part
):
    lat = up.shape[1]
    xs = dot_lt(onehot_t(us[...], node.shape[0]), node[...]).astype(BF)
    hot_r = onehot_t(ur[...], coarse.shape[0])
    xr = dot_lt(hot_r, coarse[...]).astype(BF)
    pre = dot(up[...], w1[0:lat]) + dot(xs, w1[lat : 2 * lat]) + dot(xr, w1[2 * lat :])
    normed, _ = normalise(dot(hidden_of(pre), w2[...]))
    new = (up[...].astype(F32) + normed * gain[...]).astype(BF)
    p_ref[...] = pre
    xs_ref[...] = xs
    xr_ref[...] = xr
    part[...] = dot(hot_r, new)
    split_rows(part, core[0], keep_ref, send_ref)


def edge_forward_kernel(
    es, er, edge, node, halo, coarse, w1, w2, gain, p_ref, xs_ref, total_ref, acc
):
    step = pl.program_id(0)
    lat = edge.shape[1]
    n = node.shape[0]
    imports = halo.shape[0]

    @pl.when(step == 0)
    def _():
        acc[...] = jnp.zeros_like(acc)

    sender = es[...]
    xs = (
        dot_lt(onehot_t(sender, n), node[...])
        + dot_lt(onehot_t(sender, imports, n), halo[...])
        + dot_lt(onehot_t(sender, coarse.shape[0], n + imports), coarse[...])
    ).astype(BF)
    hot_r = onehot_t(er[...], n)
    xr = dot_lt(hot_r, node[...]).astype(BF)
    pre = dot(edge[...], w1[0:lat]) + dot(xs, w1[lat : 2 * lat]) + dot(xr, w1[2 * lat :])
    normed, _ = normalise(dot(hidden_of(pre), w2[...]))
    new = (edge[...].astype(F32) + normed * gain[...]).astype(BF)
    p_ref[...] = pre
    xs_ref[...] = xs
    acc[...] += dot(hot_r, new)

    @pl.when(step == pl.num_programs(0) - 1)
    def _():
        total_ref[...] = acc[...].astype(BF)


def node_kernel(
    node, total_in, nw1, nw2, ngain, ncot, fg_ref, gn_ref, ngw1_ref, ngw2_ref, ngg_ref
):
    lat = node.shape[1]
    total = total_in[...]
    node_pre = dot(node[...], nw1[0:lat]) + dot(total, nw1[lat:])
    hidden = hidden_of(node_pre)
    node_normed, inv_std = normalise(dot(hidden, nw2[...]))
    cot = ncot[...].astype(F32)
    gain_part, d_proj, d_pre = grad_to_pre(
        node_pre, node_normed, inv_std, cot, ngain[...], nw2[...]
    )
    ngg_ref[...] = gain_part
    ngw2_ref[...] = dot_lt(hidden, d_proj).astype(BF)
    ngw1_ref[0:lat] = dot_lt(node[...], d_pre).astype(BF)
    ngw1_ref[lat:] = dot_lt(total, d_pre).astype(BF)
    gn_ref[...] = cot + dot_rt(d_pre, nw1[0:lat])
    fg_ref[...] = dot_rt(d_pre, nw1[lat:])


def edge_cotangent_kernel(
    er, edge, pre_ref, ecot, fg, w1, w2, gain, ge_ref, dp_ref, gw2_out, gg_ref, gw2
):
    step = pl.program_id(0)
    lat = edge.shape[1]

    @pl.when(step == 0)
    def _():
        gw2[...] = jnp.zeros_like(gw2)
        gg_ref[...] = jnp.zeros_like(gg_ref)

    cot = ecot[...].astype(F32) + gather_f32(onehot_t(er[...], fg.shape[0]), fg[...])
    pre = pre_ref[...]
    hidden = hidden_of(pre)
    normed, inv_std = normalise(dot(hidden, w2[...]))
    gain_part, d_proj, d_pre = grad_to_pre(pre, normed, inv_std, cot, gain[...], w2[...])
    gg_ref[...] += gain_part
    gw2[...] += dot_lt(hidden, d_proj)
    ge_ref[...] = cot + dot_rt(d_pre, w1[0:lat])
    dp_ref[...] = d_pre

    @pl.when(step == pl.num_programs(0) - 1)
    def _():
        gw2_out[...] = gw2[...].astype(BF)


def edge_product_kernel(
    es, er, edge, xs, dp, node, w1, gw1_out, np_ref, ret_ref, cp_ref, sum_s, sum_r, gw1
):
    step = pl.program_id(0)
    lat = edge.shape[1]
    n = node.shape[0]
    imports = ret_ref.shape[0]

    @pl.when(step == 0)
    def _():
        sum_s[...] = jnp.zeros_like(sum_s)
        sum_r[...] = jnp.zeros_like(sum_r)
        gw1[...] = jnp.zeros_like(gw1)

    d_pre = dp[...]
    gw1[0:lat] += dot_lt(edge[...], d_pre)
    gw1[lat:] += dot_lt(xs[...], d_pre)
    sum_r[...] += dot(onehot_t(er[...], n), d_pre)
    sum_s[...] += dot(onehot_t(es[...], sum_s.shape[0]), d_pre)

    @pl.when(step == pl.num_programs(0) - 1)
    def _():
        w_s = w1[lat : 2 * lat]
        recv = sum_r[...].astype(BF)
        gw1_out[0 : 2 * lat] = gw1[...].astype(BF)
        gw1_out[2 * lat :] = dot_lt(node[...], recv).astype(BF)
        np_ref[...] = dot_rt(sum_s[0:n].astype(BF), w_s) + dot_rt(recv, w1[2 * lat :])
        ret_ref[...] = dot_rt(sum_s[n : n + imports].astype(BF), w_s).astype(BF)
        cp_ref[...] = dot_rt(sum_s[n + imports :].astype(BF), w_s).astype(BF)


def coarse_kernel(
    core, rows, total_in, ccot, nw1, nw2, ngain, ngw1, ngw2, ngg,
    cg_ref, after_ref, keep_ref, send_ref, gg_ref, pay,
):
    lat = rows.shape[1]
    used = ngw1.shape[0] + ngw2.shape[0]
    total = total_in[...].astype(BF)
    pre = dot(rows[...], nw1[0:lat]) + dot(total, nw1[lat:])
    hidden = hidden_of(pre)
    normed, inv_std = normalise(dot(hidden, nw2[...]))
    cot = ccot[...].astype(F32)
    gain_part, d_proj, d_pre = grad_to_pre(pre, normed, inv_std, cot, ngain[...], nw2[...])
    cg_ref[...] = dot_rt(d_pre, nw1[lat:]).astype(BF)
    after_ref[...] = cot + dot_rt(d_pre, nw1[0:lat])
    pay[0:lat] = ngw1[0:lat].astype(F32) + dot_lt(rows[...], d_pre)
    pay[lat : 2 * lat] = ngw1[lat:].astype(F32) + dot_lt(total, d_pre)
    pay[2 * lat : used] = ngw2[...].astype(F32) + dot_lt(hidden, d_proj)
    if used < pay.shape[0]:
        pay[used:] = jnp.zeros((pay.shape[0] - used, lat), F32)
    split_rows(pay, core[0], keep_ref, send_ref)
    gg_ref[...] = ngg[...] + gain_part


def up_backward_kernel(
    us, ur, place, up, xs, xr, pre_ref, ucot, cg_own, cg_other, w1, w2, gain, gw1, gw2, gg, ngg,
    cp, after, gu_ref, np_ref, keep_ref, send_ref, csum, pay,
):
    lat = up.shape[1]
    half = cg_own.shape[0]
    coarse = csum.shape[0]
    core = place[1]
    hot_r = onehot_t(ur[...], coarse)
    turned = ur[...] - core * half
    turned = jnp.where(turned < 0, turned + coarse, turned)
    cot = (
        ucot[...].astype(F32)
        + dot_lt(onehot_t(turned, half), cg_own[...])
        + dot_lt(onehot_t(turned, half, half), cg_other[...])
    )
    pre = pre_ref[...]
    hidden = hidden_of(pre)
    normed, inv_std = normalise(dot(hidden, w2[...]))
    gain_part, d_proj, d_pre = grad_to_pre(pre, normed, inv_std, cot, gain[...], w2[...])
    gu_ref[...] = cot + dot_rt(d_pre, w1[0:lat])
    send = dot(onehot_t(us[...], np_ref.shape[0]), d_pre).astype(BF)
    np_ref[...] = dot_rt(send, w1[lat : 2 * lat])
    csum[...] = cp[...].astype(F32) + dot_rt(dot(hot_r, d_pre).astype(BF), w1[2 * lat :])
    count = after.shape[0]
    mine = pl.ds(pl.multiple_of(place[0] * count, 8), count)
    csum[mine, :] = csum[mine, :] + after[...]
    pay[0:coarse] = csum[...].astype(BF)
    start = coarse
    for x in (up, xs, xr):
        piece = slice(start - coarse, start - coarse + lat)
        pay[start : start + lat] = (gw1[piece].astype(F32) + dot_lt(x[...], d_pre)).astype(BF)
        start += lat
    end = start + gw2.shape[0]
    pay[start:end] = (gw2[...].astype(F32) + dot_lt(hidden, d_proj)).astype(BF)
    if end < pay.shape[0]:
        pay[end:] = jnp.zeros((pay.shape[0] - end, lat), BF)
    rows = pay.shape[0] // 2
    split_rows(pay, core, keep_ref.at[0:rows], send_ref.at[0:rows])
    ids = lax.broadcasted_iota(jnp.int32, (TAIL, lat), 0)
    edge_row = jnp.broadcast_to(gg[...] + gain_part, (TAIL, lat))
    node_row = jnp.broadcast_to(ngg[...], (TAIL, lat))
    tail = jnp.where(ids == 0, edge_row, jnp.where(ids == 1, node_row, 0.0)).astype(BF)
    keep_ref[rows:] = tail
    send_ref[rows:] = tail


def params(*semantics):
    return pltpu.CompilerParams(
        dimension_semantics=semantics or None, vmem_limit_bytes=VMEM_LIMIT
    )


def cost(micros):
    return pl.CostEstimate(
        flops=int(micros * 1.1e9), transcendentals=0, bytes_accessed=int(micros * 3.0e6)
    )


def shape(rows, cols, dtype):
    return jax.ShapeDtypeStruct((rows, cols), dtype)


def whole(arr):
    return pl.BlockSpec(arr.shape, lambda i: (0,) * len(arr.shape))


def swap(x, axes, count):
    if count == 1:
        return x
    return lax.all_to_all(x, axes, 0, 0, tiled=True)


GROUPS = ("core", ("x", "y"), "z")


def owner_index():
    index = jnp.int32(0)
    for axes in GROUPS:
        index = index * lax.axis_size(axes) + lax.axis_index(axes)
    return index


def exchange(x, mask):
    devices = lax.axis_size(EVERYONE)
    if devices == 1:
        return x
    return lax.ppermute(x, EVERYONE, [(i, i ^ mask) for i in range(devices)])


def sum_group(got, count):
    return jnp.sum(got.reshape(count, -1, got.shape[1]).astype(F32), axis=0)


def copies(x, count):
    return jnp.broadcast_to(x[None], (count,) + x.shape).reshape(-1, x.shape[1])


def reduce_rows(keep, send):
    x = keep.astype(F32) + exchange(send, 1).astype(F32)
    for axes in GROUPS[1:]:
        count = lax.axis_size(axes)
        x = sum_group(swap(x.astype(BF), axes, count), count)
    return x


def gather_halves(x):
    for axes in reversed(GROUPS[1:]):
        count = lax.axis_size(axes)
        x = swap(copies(x, count), axes, count)
    return x, exchange(x, 1)


def reduce_with_tail(keep, send, wait_for):
    cols = keep.shape[1]
    rows = keep.shape[0] - TAIL
    got = exchange(send, 1)
    got, wait_for = lax.optimization_barrier((got, wait_for))
    x = (keep, got)
    for axes, kernel in zip(GROUPS[1:], (fold_pair_kernel, fold_group_kernel)):
        count = lax.axis_size(axes)
        part = rows // count
        x = pl.pallas_call(
            kernel,
            out_shape=jax.ShapeDtypeStruct((count, part + TAIL, cols), BF),
            compiler_params=params(),
            cost_estimate=cost(3.0),
        )(*x)
        x = (swap(x.reshape(-1, cols), axes, count).reshape(x.shape),)
        rows = part
    x = jnp.sum(x[0].astype(F32), axis=0)
    return x[:rows].astype(BF), x[rows:], wait_for


def bit_masks(devices):
    slow = devices // lax.axis_size("z")
    order = [m for m in (1 << b for b in range(1, devices.bit_length())) if m < devices]
    return [m for m in order if m >= slow] + [m for m in order if m < slow]


def halving_sum(keep, send):
    devices = lax.axis_size(EVERYONE)
    masks = [1] + bit_masks(devices)
    place = lax.axis_index(EVERYONE)
    for mask, after in zip(masks, masks[1:]):
        rows, cols = keep.shape
        bit = ((place & after) > 0).astype(jnp.int32).reshape(1)
        got = exchange(send, mask)
        keep, send = pl.pallas_call(
            fold_split_kernel,
            in_specs=[pl.BlockSpec(memory_space=pltpu.SMEM)]
            + [pl.BlockSpec(memory_space=pltpu.VMEM)] * 2,
            out_shape=(shape(rows // 2, cols, BF),) * 2,
            compiler_params=params(),
            cost_estimate=cost(1.0),
            name="fold_split",
        )(bit, keep, got)
    got = exchange(send, masks[-1])
    x = (keep.astype(F32) + got.astype(F32)).astype(BF)
    for mask in reversed(masks):
        other = exchange(x, mask)
        x = jnp.where(
            (place & mask) > 0, jnp.concatenate([other, x], 0), jnp.concatenate([x, other], 0)
        )
    return x


def padded_rows(rows, devices):
    return -(-rows // (16 * devices)) * 16 * devices


def per_device(
    node, coarse, edge, up, w1, w2, gain, nw1, nw2, ngain, ncot, ccot, ecot, ucot,
    send_rows, edge_sender, edge_receiver, up_sender, up_receiver,
):
    n, lat = node.shape
    width = w2.shape[0]
    ccount = coarse.shape[0]
    ecount = edge.shape[0]
    ucount = up.shape[0]
    devices, slots = send_rows.shape[1], send_rows.shape[2]
    imports = devices * slots
    es, er = edge_sender.reshape(1, ecount), edge_receiver.reshape(1, ecount)
    us, ur = up_sender.reshape(1, ucount), up_receiver.reshape(1, ucount)
    gain_row, ngain_row = gain.reshape(1, lat), ngain.reshape(1, lat)
    own = owner_index()
    core = lax.axis_index("core").reshape(1)
    in_vmem = pl.BlockSpec(memory_space=pltpu.VMEM)
    in_smem = pl.BlockSpec(memory_space=pltpu.SMEM)

    table = send_rows.reshape(imports)
    hot_send = (table[:, None] == jnp.arange(n, dtype=jnp.int32)[None, :]).astype(BF)
    outgoing = dot(hot_send, node).astype(BF)
    halo = lax.all_to_all(
        outgoing.reshape(devices, slots, lat), EVERYONE, 0, 0, tiled=True
    ).reshape(imports, lat)

    up_pre, up_xs, up_xr, keep, send = pl.pallas_call(
        up_forward_kernel,
        in_specs=[in_vmem] * 2 + [in_smem] + [in_vmem] * 6,
        out_shape=(
            shape(ucount, width, F32), shape(ucount, lat, BF), shape(ucount, lat, BF),
            shape(ccount // 2, lat, BF), shape(ccount // 2, lat, BF),
        ),
        scratch_shapes=[pltpu.VMEM((ccount, lat), F32)],
        compiler_params=params(),
        cost_estimate=cost(5.0),
        name="up_forward",
    )(us, ur, core, up, node, coarse, w1, w2, gain_row)

    coarse_total = reduce_rows(keep, send)

    tile = math.gcd(ecount, 256)
    steps = ecount // tile
    rows_spec = pl.BlockSpec((tile, lat), lambda i: (i, 0))
    index_spec = pl.BlockSpec((1, tile), lambda i: (0, i))
    fixed = lambda r, c: pl.BlockSpec((r, c), lambda i: (0, 0))
    pre, xs, fine_total = pl.pallas_call(
        edge_forward_kernel,
        grid=(steps,),
        in_specs=[index_spec, index_spec, rows_spec]
        + [whole(a) for a in (node, halo, coarse, w1, w2, gain_row)],
        out_specs=[pl.BlockSpec((tile, width), lambda i: (i, 0)), rows_spec, fixed(n, lat)],
        out_shape=(shape(ecount, width, F32), shape(ecount, lat, BF), shape(n, lat, BF)),
        scratch_shapes=[pltpu.VMEM((n, lat), F32)],
        compiler_params=params("arbitrary"),
        cost_estimate=cost(9.0),
        name="edge_forward",
    )(es, er, edge, node, halo, coarse, w1, w2, gain_row)

    fine_grad, grad_n, ngw1, ngw2, ngg = pl.pallas_call(
        node_kernel,
        out_shape=(
            shape(n, lat, F32), shape(n, lat, F32), shape(2 * lat, width, BF),
            shape(width, lat, BF), shape(1, lat, F32),
        ),
        compiler_params=params(),
        cost_estimate=cost(5.0),
        name="node_mlp",
    )(node, fine_total, nw1, nw2, ngain_row, ncot)

    grad_e, d_pre, gw2, gg = pl.pallas_call(
        edge_cotangent_kernel,
        grid=(steps,),
        in_specs=[
            index_spec, rows_spec, pl.BlockSpec((tile, width), lambda i: (i, 0)), rows_spec,
        ]
        + [whole(a) for a in (fine_grad, w1, w2, gain_row)],
        out_specs=[
            rows_spec, pl.BlockSpec((tile, width), lambda i: (i, 0)), fixed(width, lat),
            fixed(1, lat),
        ],
        out_shape=(
            shape(ecount, lat, F32), shape(ecount, width, BF), shape(width, lat, BF),
            shape(1, lat, F32),
        ),
        scratch_shapes=[pltpu.VMEM((width, lat), F32)],
        compiler_params=params("arbitrary"),
        cost_estimate=cost(8.0),
        name="edge_cotangent",
    )(er, edge, pre, ecot, fine_grad, w1, w2, gain_row)

    gw1, node_part, returning, coarse_local = pl.pallas_call(
        edge_product_kernel,
        grid=(steps,),
        in_specs=[
            index_spec, index_spec, rows_spec, rows_spec,
            pl.BlockSpec((tile, width), lambda i: (i, 0)),
        ]
        + [whole(a) for a in (node, w1)],
        out_specs=[
            fixed(3 * lat, width), fixed(n, lat), fixed(imports, lat), fixed(ccount, lat),
        ],
        out_shape=(
            shape(3 * lat, width, BF), shape(n, lat, F32), shape(imports, lat, BF),
            shape(ccount, lat, BF),
        ),
        scratch_shapes=[
            pltpu.VMEM((n + imports + ccount, width), F32), pltpu.VMEM((n, width), F32),
            pltpu.VMEM((2 * lat, width), F32),
        ],
        compiler_params=params("arbitrary"),
        cost_estimate=cost(9.0),
        name="edge_product",
    )(es, er, edge, xs, d_pre, node, w1)

    returned = lax.all_to_all(
        returning.reshape(devices, slots, lat), EVERYONE, 0, 0, tiled=True
    ).reshape(imports, lat)

    mine = ccount // devices
    padded = -(-mine // 16) * 16
    pad = lambda a: jnp.pad(a, ((0, padded - mine), (0, 0))) if padded > mine else a
    own_coarse = pad(lax.dynamic_slice_in_dim(coarse, own * mine, mine, 0))
    own_cot = pad(lax.dynamic_slice_in_dim(ccot, own * mine, mine, 0))
    node_rows = padded_rows(2 * lat + width, devices)
    coarse_grad, coarse_after, node_keep, node_send, ngg_sum = pl.pallas_call(
        coarse_kernel,
        in_specs=[in_smem] + [in_vmem] * 9,
        out_shape=(
            shape(padded, lat, BF), shape(padded, lat, F32), shape(node_rows // 2, lat, BF),
            shape(node_rows // 2, lat, BF), shape(1, lat, F32),
        ),
        scratch_shapes=[pltpu.VMEM((node_rows, lat), F32)],
        compiler_params=params(),
        cost_estimate=cost(5.0),
        name="coarse_mlp",
    )(core, own_coarse, pad(coarse_total), own_cot, nw1, nw2, ngain_row, ngw1, ngw2, ngg)
    cg_own, cg_other = gather_halves(coarse_grad[:mine])

    node_total = halving_sum(node_keep, node_send)

    edge_rows = padded_rows(ccount + 3 * lat + width, devices)
    grad_u, up_node_part, keep, send = pl.pallas_call(
        up_backward_kernel,
        in_specs=[in_vmem] * 2 + [in_smem] + [in_vmem] * 16,
        out_shape=(
            shape(ucount, lat, F32), shape(n, lat, F32), shape(edge_rows // 2 + TAIL, lat, BF),
            shape(edge_rows // 2 + TAIL, lat, BF),
        ),
        scratch_shapes=[pltpu.VMEM((ccount, lat), F32), pltpu.VMEM((edge_rows, lat), BF)],
        compiler_params=params(),
        cost_estimate=cost(8.0),
        name="up_backward",
    )(
        us, ur, jnp.stack([own, core[0]]), up, up_xs, up_xr, up_pre, ucot, cg_own, cg_other,
        w1, w2, gain_row, gw1, gw2, gg, ngg_sum, coarse_local, coarse_after[:mine],
    )
    block, gains, returned = reduce_with_tail(keep, send, returned)
    own_half, other_half = gather_halves(block)
    first = core[0] == 0
    edge_total = jnp.concatenate(
        [jnp.where(first, own_half, other_half), jnp.where(first, other_half, own_half)], 0
    )

    grad_nodes = (
        grad_n
        + node_part
        + up_node_part
        + lax.dot_general(hot_send, returned, (((0,), (0,)), ((), ())), preferred_element_type=F32)
    )
    edge_scale = 1.0 / math.sqrt((ecount + ucount) * devices)
    node_scale = 1.0 / math.sqrt(n * devices + ccount)
    in_end = ccount + 3 * lat
    return (
        grad_nodes,
        edge_total[:ccount].astype(F32),
        grad_e,
        grad_u,
        edge_total[ccount:in_end].astype(F32) * edge_scale,
        edge_total[in_end : in_end + width].astype(F32) * edge_scale,
        gains[0] * edge_scale,
        node_total[: 2 * lat].astype(F32) * node_scale,
        node_total[2 * lat : 2 * lat + width].astype(F32) * node_scale,
        gains[1] * node_scale,
    )


def split_mesh(mesh):
    face, band = mesh.shape["face"], mesh.shape["band"]
    z = 1
    while z * z < face or face % z:
        z += 1
    core = 2 if band % 2 == 0 else 1
    return Mesh(
        mesh.devices.reshape(z, face // z, band // core, core), ("z", "x", "y", "core")
    )


def solution(mesh):
    rows, split = P(EVERYONE, None), P(EVERYONE)
    return jax.shard_map(
        per_device,
        mesh=split_mesh(mesh),
        in_specs=(
            rows, P(), rows, rows, P(), P(), P(), P(), P(), P(), rows, P(), rows, rows,
            P(EVERYONE, None, None), split, split, split, split,
        ),
        out_specs=(rows, P(), rows, rows, P(), P(), P(), P(), P(), P()),
        check_vma=False,
    )
```

```python
import functools
import math

import jax
import jax.numpy as jnp
from jax import lax
from jax.experimental import pallas as pl
from jax.experimental.pallas import tpu as pltpu
from jax.sharding import Mesh, PartitionSpec as P

EPSILON = 1e-05
BF = jnp.bfloat16
F32 = jnp.float32
TAIL = 16
EVERYONE = ("z", "x", "y", "core")
VMEM_LIMIT = 24 * 1024 * 1024


def dot(a, b):
    return lax.dot_general(a, b, (((1,), (0,)), ((), ())), preferred_element_type=F32)


def dot_lt(a, b):
    return lax.dot_general(a, b, (((0,), (0,)), ((), ())), preferred_element_type=F32)


def dot_rt(a, b):
    return lax.dot_general(a, b, (((1,), (1,)), ((), ())), preferred_element_type=F32)


def onehot_t(index_row, rows, offset=0):
    ids = lax.broadcasted_iota(jnp.int32, (rows, index_row.shape[1]), 0) + offset
    return jnp.where(ids == index_row, 1.0, 0.0).astype(BF)


def hidden_of(pre):
    return (pre * jax.nn.sigmoid(pre)).astype(BF)


def normalise(projected):
    center = projected - jnp.mean(projected, axis=1, keepdims=True)
    inv_std = lax.rsqrt(jnp.mean(center * center, axis=1, keepdims=True) + EPSILON)
    return center * inv_std, inv_std


def grad_to_pre(pre, normed, inv_std, cot, gain, w2):
    gain_part = jnp.sum(cot * normed, axis=0, keepdims=True)
    scaled = cot * gain
    d_proj = (
        inv_std
        * (
            scaled
            - jnp.mean(scaled, axis=1, keepdims=True)
            - normed * jnp.mean(scaled * normed, axis=1, keepdims=True)
        )
    ).astype(BF)
    d_hidden = dot_rt(d_proj, w2)
    logistic = jax.nn.sigmoid(pre)
    d_pre = (d_hidden * logistic * (1.0 + pre * (1.0 - logistic))).astype(BF)
    return gain_part, d_proj, d_pre


def gather_f32(onehot, table):
    high = table.astype(BF)
    low = (table - high.astype(F32)).astype(BF)
    return dot_lt(onehot, high) + dot_lt(onehot, low)


def split_rows(ref, bit, keep_ref, send_ref):
    half = keep_ref.shape[0]
    keep_ref[...] = ref[pl.ds(pl.multiple_of(bit * half, 16), half), :].astype(BF)
    send_ref[...] = ref[pl.ds(pl.multiple_of((1 - bit) * half, 16), half), :].astype(BF)


def fold_split_kernel(bit, keep, recv, keep_ref, send_ref):
    half = keep_ref.shape[0]
    for side, out_ref in ((bit[0], keep_ref), (1 - bit[0], send_ref)):
        rows = pl.ds(pl.multiple_of(side * half, 16), half)
        out_ref[...] = (keep[rows, :].astype(F32) + recv[rows, :].astype(F32)).astype(BF)


def fold_pair_kernel(keep, recv, out_ref):
    count, rows, _ = out_ref.shape
    rows -= TAIL
    tail = (keep[count * rows :].astype(F32) + recv[count * rows :].astype(F32)).astype(BF)
    for k in range(count):
        piece = slice(k * rows, (k + 1) * rows)
        out_ref[k, 0:rows] = (keep[piece].astype(F32) + recv[piece].astype(F32)).astype(BF)
        out_ref[k, rows:] = tail


def fold_group_kernel(got, out_ref):
    group = got.shape[0]
    count, rows, _ = out_ref.shape
    rows -= TAIL

    def total(at, size):
        piece = slice(at, at + size)
        acc = got[0, piece].astype(F32)
        for k in range(1, group):
            acc += got[k, piece].astype(F32)
        return acc.astype(BF)

    tail = total(count * rows, TAIL)
    for k in range(count):
        out_ref[k, 0:rows] = total(k * rows, rows)
        out_ref[k, rows:] = tail


def up_forward_kernel(
    us, ur, core, up, node, coarse, w1, w2, gain, p_ref, xs_ref, xr_ref, keep_ref, send_ref, part
):
    lat = up.shape[1]
    xs = dot_lt(onehot_t(us[...], node.shape[0]), node[...]).astype(BF)
    hot_r = onehot_t(ur[...], coarse.shape[0])
    xr = dot_lt(hot_r, coarse[...]).astype(BF)
    pre = dot(up[...], w1[0:lat]) + dot(xs, w1[lat : 2 * lat]) + dot(xr, w1[2 * lat :])
    normed, _ = normalise(dot(hidden_of(pre), w2[...]))
    new = (up[...].astype(F32) + normed * gain[...]).astype(BF)
    p_ref[...] = pre
    xs_ref[...] = xs
    xr_ref[...] = xr
    part[...] = dot(hot_r, new)
    split_rows(part, core[0], keep_ref, send_ref)


def edge_forward_kernel(
    es, er, edge, node, halo, coarse, w1, w2, gain, p_ref, xs_ref, total_ref, acc
):
    step = pl.program_id(0)
    lat = edge.shape[1]
    n = node.shape[0]
    imports = halo.shape[0]

    @pl.when(step == 0)
    def _():
        acc[...] = jnp.zeros_like(acc)

    sender = es[...]
    xs = (
        dot_lt(onehot_t(sender, n), node[...])
        + dot_lt(onehot_t(sender, imports, n), halo[...])
        + dot_lt(onehot_t(sender, coarse.shape[0], n + imports), coarse[...])
    ).astype(BF)
    hot_r = onehot_t(er[...], n)
    xr = dot_lt(hot_r, node[...]).astype(BF)
    pre = dot(edge[...], w1[0:lat]) + dot(xs, w1[lat : 2 * lat]) + dot(xr, w1[2 * lat :])
    normed, _ = normalise(dot(hidden_of(pre), w2[...]))
    new = (edge[...].astype(F32) + normed * gain[...]).astype(BF)
    p_ref[...] = pre
    xs_ref[...] = xs
    acc[...] += dot(hot_r, new)

    @pl.when(step == pl.num_programs(0) - 1)
    def _():
        total_ref[...] = acc[...].astype(BF)


def node_kernel(
    node, total_in, nw1, nw2, ngain, ncot, fg_ref, gn_ref, ngw1_ref, ngw2_ref, ngg_ref
):
    lat = node.shape[1]
    total = total_in[...]
    node_pre = dot(node[...], nw1[0:lat]) + dot(total, nw1[lat:])
    hidden = hidden_of(node_pre)
    node_normed, inv_std = normalise(dot(hidden, nw2[...]))
    cot = ncot[...].astype(F32)
    gain_part, d_proj, d_pre = grad_to_pre(
        node_pre, node_normed, inv_std, cot, ngain[...], nw2[...]
    )
    ngg_ref[...] = gain_part
    ngw2_ref[...] = dot_lt(hidden, d_proj).astype(BF)
    ngw1_ref[0:lat] = dot_lt(node[...], d_pre).astype(BF)
    ngw1_ref[lat:] = dot_lt(total, d_pre).astype(BF)
    gn_ref[...] = cot + dot_rt(d_pre, nw1[0:lat])
    fg_ref[...] = dot_rt(d_pre, nw1[lat:])


def edge_cotangent_kernel(
    er, edge, pre_ref, ecot, fg, w1, w2, gain, ge_ref, dp_ref, gw2_out, gg_ref, gw2
):
    step = pl.program_id(0)
    lat = edge.shape[1]

    @pl.when(step == 0)
    def _():
        gw2[...] = jnp.zeros_like(gw2)
        gg_ref[...] = jnp.zeros_like(gg_ref)

    cot = ecot[...].astype(F32) + gather_f32(onehot_t(er[...], fg.shape[0]), fg[...])
    pre = pre_ref[...]
    hidden = hidden_of(pre)
    normed, inv_std = normalise(dot(hidden, w2[...]))
    gain_part, d_proj, d_pre = grad_to_pre(pre, normed, inv_std, cot, gain[...], w2[...])
    gg_ref[...] += gain_part
    gw2[...] += dot_lt(hidden, d_proj)
    ge_ref[...] = cot + dot_rt(d_pre, w1[0:lat])
    dp_ref[...] = d_pre

    @pl.when(step == pl.num_programs(0) - 1)
    def _():
        gw2_out[...] = gw2[...].astype(BF)


def edge_product_kernel(
    es, er, edge, xs, dp, node, w1, gw1_out, np_ref, ret_ref, cp_ref, sum_s, sum_r, gw1
):
    step = pl.program_id(0)
    lat = edge.shape[1]
    n = node.shape[0]
    imports = ret_ref.shape[0]

    @pl.when(step == 0)
    def _():
        sum_s[...] = jnp.zeros_like(sum_s)
        sum_r[...] = jnp.zeros_like(sum_r)
        gw1[...] = jnp.zeros_like(gw1)

    d_pre = dp[...]
    gw1[0:lat] += dot_lt(edge[...], d_pre)
    gw1[lat:] += dot_lt(xs[...], d_pre)
    sum_r[...] += dot(onehot_t(er[...], n), d_pre)
    sum_s[...] += dot(onehot_t(es[...], sum_s.shape[0]), d_pre)

    @pl.when(step == pl.num_programs(0) - 1)
    def _():
        w_s = w1[lat : 2 * lat]
        recv = sum_r[...].astype(BF)
        gw1_out[0 : 2 * lat] = gw1[...].astype(BF)
        gw1_out[2 * lat :] = dot_lt(node[...], recv).astype(BF)
        np_ref[...] = dot_rt(sum_s[0:n].astype(BF), w_s) + dot_rt(recv, w1[2 * lat :])
        ret_ref[...] = dot_rt(sum_s[n : n + imports].astype(BF), w_s).astype(BF)
        cp_ref[...] = dot_rt(sum_s[n + imports :].astype(BF), w_s).astype(BF)


def coarse_kernel(
    core, rows, total_in, ccot, nw1, nw2, ngain, ngw1, ngw2, ngg,
    cg_ref, after_ref, keep_ref, send_ref, gg_ref, pay,
):
    lat = rows.shape[1]
    used = ngw1.shape[0] + ngw2.shape[0]
    total = total_in[...].astype(BF)
    pre = dot(rows[...], nw1[0:lat]) + dot(total, nw1[lat:])
    hidden = hidden_of(pre)
    normed, inv_std = normalise(dot(hidden, nw2[...]))
    cot = ccot[...].astype(F32)
    gain_part, d_proj, d_pre = grad_to_pre(pre, normed, inv_std, cot, ngain[...], nw2[...])
    cg_ref[...] = dot_rt(d_pre, nw1[lat:]).astype(BF)
    after_ref[...] = cot + dot_rt(d_pre, nw1[0:lat])
    pay[0:lat] = ngw1[0:lat].astype(F32) + dot_lt(rows[...], d_pre)
    pay[lat : 2 * lat] = ngw1[lat:].astype(F32) + dot_lt(total, d_pre)
    pay[2 * lat : used] = ngw2[...].astype(F32) + dot_lt(hidden, d_proj)
    if used < pay.shape[0]:
        pay[used:] = jnp.zeros((pay.shape[0] - used, lat), F32)
    split_rows(pay, core[0], keep_ref, send_ref)
    gg_ref[...] = ngg[...] + gain_part


def up_backward_kernel(
    us, ur, place, up, xs, xr, pre_ref, ucot, cg_own, cg_other, w1, w2, gain, gw1, gw2, gg, ngg,
    cp, after, gu_ref, np_ref, keep_ref, send_ref, csum, pay,
):
    lat = up.shape[1]
    half = cg_own.shape[0]
    coarse = csum.shape[0]
    core = place[1]
    hot_r = onehot_t(ur[...], coarse)
    turned = ur[...] - core * half
    turned = jnp.where(turned < 0, turned + coarse, turned)
    cot = (
        ucot[...].astype(F32)
        + dot_lt(onehot_t(turned, half), cg_own[...])
        + dot_lt(onehot_t(turned, half, half), cg_other[...])
    )
    pre = pre_ref[...]
    hidden = hidden_of(pre)
    normed, inv_std = normalise(dot(hidden, w2[...]))
    gain_part, d_proj, d_pre = grad_to_pre(pre, normed, inv_std, cot, gain[...], w2[...])
    gu_ref[...] = cot + dot_rt(d_pre, w1[0:lat])
    send = dot(onehot_t(us[...], np_ref.shape[0]), d_pre).astype(BF)
    np_ref[...] = dot_rt(send, w1[lat : 2 * lat])
    csum[...] = cp[...].astype(F32) + dot_rt(dot(hot_r, d_pre).astype(BF), w1[2 * lat :])
    count = after.shape[0]
    mine = pl.ds(pl.multiple_of(place[0] * count, 8), count)
    csum[mine, :] = csum[mine, :] + after[...]
    rows = pay.shape[0] // 2
    first = [csum[...]]
    second = [gw2[...].astype(F32) + dot_lt(hidden, d_proj)]
    for k, x in enumerate((up, xs, xr)):
        piece = slice(k * lat, (k + 1) * lat)
        second.insert(k, gw1[piece].astype(F32) + dot_lt(x[...], d_pre))
    w1_part = jnp.concatenate(second[:-1], axis=0)
    for h in range(2):
        start = h * rows
        for full in (first[0], w1_part, second[-1]):
            size = full.shape[0] // 2
            pay[start : start + size] = full[h * size : (h + 1) * size].astype(BF)
            start += size
        if start < (h + 1) * rows:
            pay[start : (h + 1) * rows] = jnp.zeros(((h + 1) * rows - start, lat), BF)
    split_rows(pay, core, keep_ref.at[0:rows], send_ref.at[0:rows])
    ids = lax.broadcasted_iota(jnp.int32, (TAIL, lat), 0)
    edge_row = jnp.broadcast_to(gg[...] + gain_part, (TAIL, lat))
    node_row = jnp.broadcast_to(ngg[...], (TAIL, lat))
    tail = jnp.where(ids == 0, edge_row, jnp.where(ids == 1, node_row, 0.0)).astype(BF)
    keep_ref[rows:] = tail
    send_ref[rows:] = tail


def widen_kernel(core, half, coarse_ref, first_ref, second_ref, *, scale):
    start = 0
    for out_ref, factor in ((coarse_ref, None), (first_ref, scale), (second_ref, scale)):
        rows = out_ref.shape[1]
        values = half[start : start + rows].astype(F32)
        out_ref[0] = values if factor is None else values * factor
        start += rows


def widen_other_kernel(core, half, c_in, f_in, s_in, coarse_ref, first_ref, second_ref, *, scale):
    widen_kernel(core, half, coarse_ref, first_ref, second_ref, scale=scale)


def params(*semantics):
    return pltpu.CompilerParams(
        dimension_semantics=semantics or None, vmem_limit_bytes=VMEM_LIMIT
    )


def cost(micros):
    return pl.CostEstimate(
        flops=int(micros * 1.1e9), transcendentals=0, bytes_accessed=int(micros * 3.0e6)
    )


def shape(rows, cols, dtype):
    return jax.ShapeDtypeStruct((rows, cols), dtype)


def whole(arr):
    return pl.BlockSpec(arr.shape, lambda i: (0,) * len(arr.shape))


def swap(x, axes, count):
    if count == 1:
        return x
    return lax.all_to_all(x, axes, 0, 0, tiled=True)


GROUPS = ("core", ("x", "y"), "z")


def owner_index():
    index = jnp.int32(0)
    for axes in GROUPS:
        index = index * lax.axis_size(axes) + lax.axis_index(axes)
    return index


def exchange(x, mask):
    devices = lax.axis_size(EVERYONE)
    if devices == 1:
        return x
    return lax.ppermute(x, EVERYONE, [(i, i ^ mask) for i in range(devices)])


def sum_group(got, count):
    return jnp.sum(got.reshape(count, -1, got.shape[1]).astype(F32), axis=0)


def copies(x, count):
    return jnp.broadcast_to(x[None], (count,) + x.shape).reshape(-1, x.shape[1])


def reduce_rows(keep, send):
    x = keep.astype(F32) + exchange(send, 1).astype(F32)
    for axes in GROUPS[1:]:
        count = lax.axis_size(axes)
        x = sum_group(swap(x.astype(BF), axes, count), count)
    return x


def gather_halves(x):
    for axes in reversed(GROUPS[1:]):
        count = lax.axis_size(axes)
        x = swap(copies(x, count), axes, count)
    return x, exchange(x, 1)


def reduce_with_tail(keep, send, wait_for):
    cols = keep.shape[1]
    rows = keep.shape[0] - TAIL
    got = exchange(send, 1)
    got, wait_for = lax.optimization_barrier((got, wait_for))
    x = (keep, got)
    for axes, kernel in zip(GROUPS[1:], (fold_pair_kernel, fold_group_kernel)):
        count = lax.axis_size(axes)
        part = rows // count
        x = pl.pallas_call(
            kernel,
            out_shape=jax.ShapeDtypeStruct((count, part + TAIL, cols), BF),
            compiler_params=params(),
            cost_estimate=cost(3.0),
        )(*x)
        x = (swap(x.reshape(-1, cols), axes, count).reshape(x.shape),)
        rows = part
    x = jnp.sum(x[0].astype(F32), axis=0)
    return x[:rows].astype(BF), x[rows:], wait_for


def bit_masks(devices):
    slow = devices // lax.axis_size("z")
    order = [1 << b for b in range(1, devices.bit_length() - 1)]
    return (
        [m for m in order if m == slow]
        + [m for m in reversed(order) if m < slow]
        + [m for m in order if m > slow]
    )


def halving_sum(keep, send):
    devices = lax.axis_size(EVERYONE)
    masks = [1] + bit_masks(devices)
    place = lax.axis_index(EVERYONE)
    for mask, after in zip(masks, masks[1:]):
        rows, cols = keep.shape
        bit = ((place & after) > 0).astype(jnp.int32).reshape(1)
        got = exchange(send, mask)
        keep, send = pl.pallas_call(
            fold_split_kernel,
            in_specs=[pl.BlockSpec(memory_space=pltpu.SMEM)]
            + [pl.BlockSpec(memory_space=pltpu.VMEM)] * 2,
            out_shape=(shape(rows // 2, cols, BF),) * 2,
            compiler_params=params(),
            cost_estimate=cost(1.0),
            name="fold_split",
        )(bit, keep, got)
    got = exchange(send, masks[-1])
    x = (keep.astype(F32) + got.astype(F32)).astype(BF)
    for mask in reversed(masks):
        other = exchange(x, mask)
        x = jnp.where(
            (place & mask) > 0, jnp.concatenate([other, x], 0), jnp.concatenate([x, other], 0)
        )
    return x


def padded_rows(rows, devices):
    return -(-rows // (16 * devices)) * 16 * devices


def per_device(
    node, coarse, edge, up, w1, w2, gain, nw1, nw2, ngain, ncot, ccot, ecot, ucot,
    send_rows, edge_sender, edge_receiver, up_sender, up_receiver,
):
    n, lat = node.shape
    width = w2.shape[0]
    ccount = coarse.shape[0]
    ecount = edge.shape[0]
    ucount = up.shape[0]
    devices, slots = send_rows.shape[1], send_rows.shape[2]
    imports = devices * slots
    es, er = edge_sender.reshape(1, ecount), edge_receiver.reshape(1, ecount)
    us, ur = up_sender.reshape(1, ucount), up_receiver.reshape(1, ucount)
    gain_row, ngain_row = gain.reshape(1, lat), ngain.reshape(1, lat)
    own = owner_index()
    core = lax.axis_index("core").reshape(1)
    in_vmem = pl.BlockSpec(memory_space=pltpu.VMEM)
    in_smem = pl.BlockSpec(memory_space=pltpu.SMEM)

    table = send_rows.reshape(imports)
    hot_send = (table[:, None] == jnp.arange(n, dtype=jnp.int32)[None, :]).astype(BF)
    outgoing = dot(hot_send, node).astype(BF)
    halo = lax.all_to_all(
        outgoing.reshape(devices, slots, lat), EVERYONE, 0, 0, tiled=True
    ).reshape(imports, lat)

    up_pre, up_xs, up_xr, keep, send = pl.pallas_call(
        up_forward_kernel,
        in_specs=[in_vmem] * 2 + [in_smem] + [in_vmem] * 6,
        out_shape=(
            shape(ucount, width, F32), shape(ucount, lat, BF), shape(ucount, lat, BF),
            shape(ccount // 2, lat, BF), shape(ccount // 2, lat, BF),
        ),
        scratch_shapes=[pltpu.VMEM((ccount, lat), F32)],
        compiler_params=params(),
        cost_estimate=cost(5.0),
        name="up_forward",
    )(us, ur, core, up, node, coarse, w1, w2, gain_row)

    coarse_total = reduce_rows(keep, send)

    tile = math.gcd(ecount, 256)
    steps = ecount // tile
    rows_spec = pl.BlockSpec((tile, lat), lambda i: (i, 0))
    index_spec = pl.BlockSpec((1, tile), lambda i: (0, i))
    fixed = lambda r, c: pl.BlockSpec((r, c), lambda i: (0, 0))
    pre, xs, fine_total = pl.pallas_call(
        edge_forward_kernel,
        grid=(steps,),
        in_specs=[index_spec, index_spec, rows_spec]
        + [whole(a) for a in (node, halo, coarse, w1, w2, gain_row)],
        out_specs=[pl.BlockSpec((tile, width), lambda i: (i, 0)), rows_spec, fixed(n, lat)],
        out_shape=(shape(ecount, width, F32), shape(ecount, lat, BF), shape(n, lat, BF)),
        scratch_shapes=[pltpu.VMEM((n, lat), F32)],
        compiler_params=params("arbitrary"),
        cost_estimate=cost(9.0),
        name="edge_forward",
    )(es, er, edge, node, halo, coarse, w1, w2, gain_row)

    fine_grad, grad_n, ngw1, ngw2, ngg = pl.pallas_call(
        node_kernel,
        out_shape=(
            shape(n, lat, F32), shape(n, lat, F32), shape(2 * lat, width, BF),
            shape(width, lat, BF), shape(1, lat, F32),
        ),
        compiler_params=params(),
        cost_estimate=cost(5.0),
        name="node_mlp",
    )(node, fine_total, nw1, nw2, ngain_row, ncot)

    grad_e, d_pre, gw2, gg = pl.pallas_call(
        edge_cotangent_kernel,
        grid=(steps,),
        in_specs=[
            index_spec, rows_spec, pl.BlockSpec((tile, width), lambda i: (i, 0)), rows_spec,
        ]
        + [whole(a) for a in (fine_grad, w1, w2, gain_row)],
        out_specs=[
            rows_spec, pl.BlockSpec((tile, width), lambda i: (i, 0)), fixed(width, lat),
            fixed(1, lat),
        ],
        out_shape=(
            shape(ecount, lat, F32), shape(ecount, width, BF), shape(width, lat, BF),
            shape(1, lat, F32),
        ),
        scratch_shapes=[pltpu.VMEM((width, lat), F32)],
        compiler_params=params("arbitrary"),
        cost_estimate=cost(8.0),
        name="edge_cotangent",
    )(er, edge, pre, ecot, fine_grad, w1, w2, gain_row)

    gw1, node_part, returning, coarse_local = pl.pallas_call(
        edge_product_kernel,
        grid=(steps,),
        in_specs=[
            index_spec, index_spec, rows_spec, rows_spec,
            pl.BlockSpec((tile, width), lambda i: (i, 0)),
        ]
        + [whole(a) for a in (node, w1)],
        out_specs=[
            fixed(3 * lat, width), fixed(n, lat), fixed(imports, lat), fixed(ccount, lat),
        ],
        out_shape=(
            shape(3 * lat, width, BF), shape(n, lat, F32), shape(imports, lat, BF),
            shape(ccount, lat, BF),
        ),
        scratch_shapes=[
            pltpu.VMEM((n + imports + ccount, width), F32), pltpu.VMEM((n, width), F32),
            pltpu.VMEM((2 * lat, width), F32),
        ],
        compiler_params=params("arbitrary"),
        cost_estimate=cost(9.0),
        name="edge_product",
    )(es, er, edge, xs, d_pre, node, w1)

    returned = lax.all_to_all(
        returning.reshape(devices, slots, lat), EVERYONE, 0, 0, tiled=True
    ).reshape(imports, lat)

    mine = ccount // devices
    padded = -(-mine // 16) * 16
    pad = lambda a: jnp.pad(a, ((0, padded - mine), (0, 0))) if padded > mine else a
    own_coarse = pad(lax.dynamic_slice_in_dim(coarse, own * mine, mine, 0))
    own_cot = pad(lax.dynamic_slice_in_dim(ccot, own * mine, mine, 0))
    node_rows = padded_rows(2 * lat + width, devices)
    coarse_grad, coarse_after, node_keep, node_send, ngg_sum = pl.pallas_call(
        coarse_kernel,
        in_specs=[in_smem] + [in_vmem] * 9,
        out_shape=(
            shape(padded, lat, BF), shape(padded, lat, F32), shape(node_rows // 2, lat, BF),
            shape(node_rows // 2, lat, BF), shape(1, lat, F32),
        ),
        scratch_shapes=[pltpu.VMEM((node_rows, lat), F32)],
        compiler_params=params(),
        cost_estimate=cost(5.0),
        name="coarse_mlp",
    )(core, own_coarse, pad(coarse_total), own_cot, nw1, nw2, ngain_row, ngw1, ngw2, ngg)
    cg_own, cg_other = gather_halves(coarse_grad[:mine])

    node_total = halving_sum(node_keep, node_send)

    edge_rows = padded_rows(ccount + 3 * lat + width, devices)
    grad_u, up_node_part, keep, send = pl.pallas_call(
        up_backward_kernel,
        in_specs=[in_vmem] * 2 + [in_smem] + [in_vmem] * 16,
        out_shape=(
            shape(ucount, lat, F32), shape(n, lat, F32), shape(edge_rows // 2 + TAIL, lat, BF),
            shape(edge_rows // 2 + TAIL, lat, BF),
        ),
        scratch_shapes=[pltpu.VMEM((ccount, lat), F32), pltpu.VMEM((edge_rows, lat), BF)],
        compiler_params=params(),
        cost_estimate=cost(8.0),
        name="up_backward",
    )(
        us, ur, jnp.stack([own, core[0]]), up, up_xs, up_xr, up_pre, ucot, cg_own, cg_other,
        w1, w2, gain_row, gw1, gw2, gg, ngg_sum, coarse_local, coarse_after[:mine],
    )
    block, gains, returned = reduce_with_tail(keep, send, returned)
    own_half, other_half = gather_halves(block)
    edge_scale = 1.0 / math.sqrt((ecount + ucount) * devices)
    node_scale = 1.0 / math.sqrt(n * devices + ccount)
    halves = [ccount // 2, 3 * lat // 2, width // 2]
    outs = tuple(jax.ShapeDtypeStruct((2, rows, lat), F32) for rows in halves)

    def place_of(flip):
        return [
            pl.BlockSpec((1, rows, lat), lambda i, c: (c[0] ^ flip, 0, 0)) for rows in halves
        ]

    half_spec = pl.BlockSpec(own_half.shape, lambda i, c: (0, 0))
    written = pl.pallas_call(
        functools.partial(widen_kernel, scale=edge_scale),
        grid_spec=pltpu.PrefetchScalarGridSpec(
            num_scalar_prefetch=1, grid=(1,), in_specs=[half_spec], out_specs=place_of(0)
        ),
        out_shape=outs,
        compiler_params=params("arbitrary"),
        cost_estimate=cost(2.5),
        name="widen_own",
    )(core, own_half)
    written = pl.pallas_call(
        functools.partial(widen_other_kernel, scale=edge_scale),
        grid_spec=pltpu.PrefetchScalarGridSpec(
            num_scalar_prefetch=1,
            grid=(1,),
            in_specs=[half_spec] + [pl.BlockSpec(memory_space=pl.ANY)] * 3,
            out_specs=place_of(1),
        ),
        out_shape=outs,
        input_output_aliases={2: 0, 3: 1, 4: 2},
        compiler_params=params("arbitrary"),
        cost_estimate=cost(2.5),
        name="widen_other",
    )(core, other_half, *written)
    grad_coarse, grad_edge_in, grad_edge_out = (a.reshape(-1, lat) for a in written)

    grad_nodes = (
        grad_n
        + node_part
        + up_node_part
        + lax.dot_general(hot_send, returned, (((0,), (0,)), ((), ())), preferred_element_type=F32)
    )
    grad_node_in = node_total[: 2 * lat].astype(F32) * node_scale
    grad_node_out = node_total[2 * lat : 2 * lat + width].astype(F32) * node_scale
    return (
        grad_nodes,
        grad_coarse,
        grad_e,
        grad_u,
        grad_edge_in,
        grad_edge_out,
        gains[0] * edge_scale,
        grad_node_in,
        grad_node_out,
        gains[1] * node_scale,
    )


def split_mesh(mesh):
    face, band = mesh.shape["face"], mesh.shape["band"]
    z = 1
    while z * z < face or face % z:
        z += 1
    core = 2 if band % 2 == 0 else 1
    return Mesh(
        mesh.devices.reshape(z, face // z, band // core, core), ("z", "x", "y", "core")
    )


def solution(mesh):
    rows, split = P(EVERYONE, None), P(EVERYONE)
    return jax.shard_map(
        per_device,
        mesh=split_mesh(mesh),
        in_specs=(
            rows, P(), rows, rows, P(), P(), P(), P(), P(), P(), rows, P(), rows, rows,
            P(EVERYONE, None, None), split, split, split, split,
        ),
        out_specs=(rows, P(), rows, rows, P(), P(), P(), P(), P(), P()),
        check_vma=False,
    )
```

```python
import functools
import math

import jax
import jax.numpy as jnp
from jax import lax
from jax.experimental import pallas as pl
from jax.experimental.pallas import tpu as pltpu
from jax.sharding import Mesh, PartitionSpec as P

EPSILON = 1e-05
BF = jnp.bfloat16
F32 = jnp.float32
TAIL = 16
EVERYONE = ("z", "x", "y", "core")
VMEM_LIMIT = 24 * 1024 * 1024


def dot(a, b):
    return lax.dot_general(a, b, (((1,), (0,)), ((), ())), preferred_element_type=F32)


def dot_lt(a, b):
    return lax.dot_general(a, b, (((0,), (0,)), ((), ())), preferred_element_type=F32)


def dot_rt(a, b):
    return lax.dot_general(a, b, (((1,), (1,)), ((), ())), preferred_element_type=F32)


def onehot_t(index_row, rows, offset=0):
    ids = lax.broadcasted_iota(jnp.int32, (rows, index_row.shape[1]), 0) + offset
    return jnp.where(ids == index_row, 1.0, 0.0).astype(BF)


def hidden_of(pre):
    return (pre * jax.nn.sigmoid(pre)).astype(BF)


def normalise(projected):
    center = projected - jnp.mean(projected, axis=1, keepdims=True)
    inv_std = lax.rsqrt(jnp.mean(center * center, axis=1, keepdims=True) + EPSILON)
    return center * inv_std, inv_std


def grad_to_pre(pre, normed, inv_std, cot, gain, w2):
    gain_part = jnp.sum(cot * normed, axis=0, keepdims=True)
    scaled = cot * gain
    d_proj = (
        inv_std
        * (
            scaled
            - jnp.mean(scaled, axis=1, keepdims=True)
            - normed * jnp.mean(scaled * normed, axis=1, keepdims=True)
        )
    ).astype(BF)
    d_hidden = dot_rt(d_proj, w2)
    logistic = jax.nn.sigmoid(pre)
    d_pre = (d_hidden * logistic * (1.0 + pre * (1.0 - logistic))).astype(BF)
    return gain_part, d_proj, d_pre


def gather_f32(onehot, table):
    high = table.astype(BF)
    low = (table - high.astype(F32)).astype(BF)
    return dot_lt(onehot, high) + dot_lt(onehot, low)


def split_rows(ref, bit, keep_ref, send_ref):
    half = keep_ref.shape[0]
    keep_ref[...] = ref[pl.ds(pl.multiple_of(bit * half, 16), half), :].astype(BF)
    send_ref[...] = ref[pl.ds(pl.multiple_of((1 - bit) * half, 16), half), :].astype(BF)


def fold_split_kernel(bit, keep, recv, keep_ref, send_ref):
    half = keep_ref.shape[0]
    for side, out_ref in ((bit[0], keep_ref), (1 - bit[0], send_ref)):
        rows = pl.ds(pl.multiple_of(side * half, 16), half)
        out_ref[...] = (keep[rows, :].astype(F32) + recv[rows, :].astype(F32)).astype(BF)


def fold_pair_kernel(keep, recv, out_ref):
    count, rows, _ = out_ref.shape
    rows -= TAIL
    tail = (keep[count * rows :].astype(F32) + recv[count * rows :].astype(F32)).astype(BF)
    for k in range(count):
        piece = slice(k * rows, (k + 1) * rows)
        out_ref[k, 0:rows] = (keep[piece].astype(F32) + recv[piece].astype(F32)).astype(BF)
        out_ref[k, rows:] = tail


def fold_group_kernel(got, out_ref):
    group = got.shape[0]
    count, rows, _ = out_ref.shape
    rows -= TAIL

    def total(at, size):
        piece = slice(at, at + size)
        acc = got[0, piece].astype(F32)
        for k in range(1, group):
            acc += got[k, piece].astype(F32)
        return acc.astype(BF)

    tail = total(count * rows, TAIL)
    for k in range(count):
        out_ref[k, 0:rows] = total(k * rows, rows)
        out_ref[k, rows:] = tail


def up_forward_kernel(
    us, ur, core, up, gain, node_far, coarse_far, w1_far, w2_far,
    p_ref, xs_ref, xr_ref, keep_ref, send_ref, part, node, coarse, w1, w2, sems,
):
    loads = loads_of((node_far, coarse_far, w1_far, w2_far), (node, coarse, w1, w2), sems)
    for load in loads:
        load.start()
    lat = up.shape[1]
    hot_s = onehot_t(us[...], node.shape[0])
    hot_r = onehot_t(ur[...], coarse.shape[0])
    loads[0].wait()
    xs = dot_lt(hot_s, node[...]).astype(BF)
    loads[1].wait()
    xr = dot_lt(hot_r, coarse[...]).astype(BF)
    loads[2].wait()
    pre = dot(up[...], w1[0:lat]) + dot(xs, w1[lat : 2 * lat]) + dot(xr, w1[2 * lat :])
    loads[3].wait()
    normed, _ = normalise(dot(hidden_of(pre), w2[...]))
    new = (up[...].astype(F32) + normed * gain[...]).astype(BF)
    p_ref[...] = pre
    xs_ref[...] = xs
    xr_ref[...] = xr
    part[...] = dot(hot_r, new)
    split_rows(part, core[0], keep_ref, send_ref)


def edge_forward_kernel(
    es, er, edge, halo, gain, node_far, coarse_far, w1_far, w2_far, p_ref, xs_ref, total_ref,
    acc, node, coarse, w1, w2, sems,
):
    step = pl.program_id(0)
    lat = edge.shape[1]
    n = node.shape[0]
    imports = halo.shape[0]
    loads = loads_of((node_far, coarse_far, w1_far, w2_far), (node, coarse, w1, w2), sems)

    @pl.when(step == 0)
    def _():
        for load in loads:
            load.start()
        acc[...] = jnp.zeros_like(acc)
        for load in loads[:3]:
            load.wait()

    sender = es[...]
    xs = (
        dot_lt(onehot_t(sender, n), node[...])
        + dot_lt(onehot_t(sender, imports, n), halo[...])
        + dot_lt(onehot_t(sender, coarse.shape[0], n + imports), coarse[...])
    ).astype(BF)
    hot_r = onehot_t(er[...], n)
    xr = dot_lt(hot_r, node[...]).astype(BF)
    pre = dot(edge[...], w1[0:lat]) + dot(xs, w1[lat : 2 * lat]) + dot(xr, w1[2 * lat :])
    p_ref[...] = pre

    @pl.when(step == 0)
    def _():
        loads[3].wait()

    normed, _ = normalise(dot(hidden_of(pre), w2[...]))
    new = (edge[...].astype(F32) + normed * gain[...]).astype(BF)
    xs_ref[...] = xs
    acc[...] += dot(hot_r, new)

    @pl.when(step == pl.num_programs(0) - 1)
    def _():
        total_ref[...] = acc[...].astype(BF)


def node_kernel(
    node, total_in, ngain, ncot, nw1_far, nw2_far, fg_ref, gn_ref, ngw1_ref, ngw2_ref, ngg_ref,
    nw1, nw2, sems,
):
    loads = loads_of((nw1_far, nw2_far), (nw1, nw2), sems)
    for load in loads:
        load.start()
    lat = node.shape[1]
    total = total_in[...]
    loads[0].wait()
    node_pre = dot(node[...], nw1[0:lat]) + dot(total, nw1[lat:])
    hidden = hidden_of(node_pre)
    loads[1].wait()
    node_normed, inv_std = normalise(dot(hidden, nw2[...]))
    cot = ncot[...].astype(F32)
    gain_part, d_proj, d_pre = grad_to_pre(
        node_pre, node_normed, inv_std, cot, ngain[...], nw2[...]
    )
    ngg_ref[...] = gain_part
    ngw2_ref[...] = dot_lt(hidden, d_proj).astype(BF)
    ngw1_ref[0:lat] = dot_lt(node[...], d_pre).astype(BF)
    ngw1_ref[lat:] = dot_lt(total, d_pre).astype(BF)
    gn_ref[...] = cot + dot_rt(d_pre, nw1[0:lat])
    fg_ref[...] = dot_rt(d_pre, nw1[lat:])


def edge_cotangent_kernel(
    er, pre_ref, ecot, fg, gain, w1_far, w2_far, ge_ref, dp_ref, gw2_out, gg_ref,
    gw2, w1, w2, sems,
):
    step = pl.program_id(0)
    lat = ecot.shape[1]
    loads = loads_of((w1_far.at[0:lat], w2_far), (w1, w2), sems)

    @pl.when(step == 0)
    def _():
        for load in loads:
            load.start()
        gw2[...] = jnp.zeros_like(gw2)
        gg_ref[...] = jnp.zeros_like(gg_ref)

    cot = ecot[...].astype(F32) + gather_f32(onehot_t(er[...], fg.shape[0]), fg[...])
    pre = pre_ref[...]
    hidden = hidden_of(pre)

    @pl.when(step == 0)
    def _():
        for load in loads:
            load.wait()

    normed, inv_std = normalise(dot(hidden, w2[...]))
    gain_part, d_proj, d_pre = grad_to_pre(pre, normed, inv_std, cot, gain[...], w2[...])
    gg_ref[...] += gain_part
    gw2[...] += dot_lt(hidden, d_proj)
    ge_ref[...] = cot + dot_rt(d_pre, w1[...])
    dp_ref[...] = d_pre

    @pl.when(step == pl.num_programs(0) - 1)
    def _():
        gw2_out[...] = gw2[...].astype(BF)


def edge_product_kernel(
    es, er, edge, xs, dp, node_far, w1_far, gw1_out, np_ref, ret_ref, cp_ref,
    sum_s, sum_r, gw1, node, w1, sems,
):
    step = pl.program_id(0)
    lat = edge.shape[1]
    n = node.shape[0]
    imports = ret_ref.shape[0]
    loads = loads_of((node_far, w1_far.at[lat : 3 * lat]), (node, w1), sems)

    @pl.when(step == 0)
    def _():
        for load in loads:
            load.start()
        sum_s[...] = jnp.zeros_like(sum_s)
        sum_r[...] = jnp.zeros_like(sum_r)
        gw1[...] = jnp.zeros_like(gw1)

    d_pre = dp[...]
    gw1[0:lat] += dot_lt(edge[...], d_pre)
    gw1[lat:] += dot_lt(xs[...], d_pre)
    sum_r[...] += dot(onehot_t(er[...], n), d_pre)
    sum_s[...] += dot(onehot_t(es[...], sum_s.shape[0]), d_pre)

    @pl.when(step == pl.num_programs(0) - 1)
    def _():
        for load in loads:
            load.wait()
        w_s = w1[0:lat]
        recv = sum_r[...].astype(BF)
        gw1_out[0 : 2 * lat] = gw1[...].astype(BF)
        gw1_out[2 * lat :] = dot_lt(node[...], recv).astype(BF)
        np_ref[...] = dot_rt(sum_s[0:n].astype(BF), w_s) + dot_rt(recv, w1[lat:])
        ret_ref[...] = dot_rt(sum_s[n : n + imports].astype(BF), w_s).astype(BF)
        cp_ref[...] = dot_rt(sum_s[n + imports :].astype(BF), w_s).astype(BF)


def coarse_kernel(
    core, rows, total_in, ccot, ngain, ngg, nw1_far, nw2_far, ngw1_far, ngw2_far,
    cg_ref, after_ref, keep_ref, send_ref, gg_ref, pay, nw1, nw2, ngw1, ngw2, sems,
):
    loads = loads_of(
        (nw1_far, nw2_far, ngw1_far, ngw2_far), (nw1, nw2, ngw1, ngw2), sems
    )
    for load in loads:
        load.start()
    lat = rows.shape[1]
    used = ngw1.shape[0] + ngw2.shape[0]
    total = total_in[...].astype(BF)
    loads[0].wait()
    pre = dot(rows[...], nw1[0:lat]) + dot(total, nw1[lat:])
    hidden = hidden_of(pre)
    loads[1].wait()
    normed, inv_std = normalise(dot(hidden, nw2[...]))
    cot = ccot[...].astype(F32)
    gain_part, d_proj, d_pre = grad_to_pre(pre, normed, inv_std, cot, ngain[...], nw2[...])
    cg_ref[...] = dot_rt(d_pre, nw1[lat:]).astype(BF)
    after_ref[...] = cot + dot_rt(d_pre, nw1[0:lat])
    loads[2].wait()
    loads[3].wait()
    pay[0:lat] = ngw1[0:lat].astype(F32) + dot_lt(rows[...], d_pre)
    pay[lat : 2 * lat] = ngw1[lat:].astype(F32) + dot_lt(total, d_pre)
    pay[2 * lat : used] = ngw2[...].astype(F32) + dot_lt(hidden, d_proj)
    if used < pay.shape[0]:
        pay[used:] = jnp.zeros((pay.shape[0] - used, lat), F32)
    split_rows(pay, core[0], keep_ref, send_ref)
    gg_ref[...] = ngg[...] + gain_part


def up_backward_kernel(
    us, ur, place, up, xs, xr, pre_ref, ucot, cg_own, cg_other, gain, gg, ngg, after,
    w2_far, w1_far, cp_far, gw2_far, gw1_far, gu_ref, np_ref, keep_far, send_far,
    csum, pay, w2, w1, cp, gw2, gw1, sems, out_sems,
):
    loads = loads_of(
        (w2_far, w1_far, cp_far, gw2_far, gw1_far), (w2, w1, cp, gw2, gw1), sems
    )
    for load in loads:
        load.start()
    lat = up.shape[1]
    half = cg_own.shape[0]
    coarse = csum.shape[0]
    core = place[1]
    hot_r = onehot_t(ur[...], coarse)
    turned = ur[...] - core * half
    turned = jnp.where(turned < 0, turned + coarse, turned)
    cot = (
        ucot[...].astype(F32)
        + dot_lt(onehot_t(turned, half), cg_own[...])
        + dot_lt(onehot_t(turned, half, half), cg_other[...])
    )
    pre = pre_ref[...]
    hidden = hidden_of(pre)
    loads[0].wait()
    normed, inv_std = normalise(dot(hidden, w2[...]))
    gain_part, d_proj, d_pre = grad_to_pre(pre, normed, inv_std, cot, gain[...], w2[...])
    loads[1].wait()
    gu_ref[...] = cot + dot_rt(d_pre, w1[0:lat])
    send = dot(onehot_t(us[...], np_ref.shape[0]), d_pre).astype(BF)
    np_ref[...] = dot_rt(send, w1[lat : 2 * lat])
    loads[2].wait()
    csum[...] = cp[...].astype(F32) + dot_rt(dot(hot_r, d_pre).astype(BF), w1[2 * lat :])
    count = after.shape[0]
    mine = pl.ds(pl.multiple_of(place[0] * count, 8), count)
    csum[mine, :] = csum[mine, :] + after[...]
    rows = pay.shape[0] // 2 - TAIL
    c_half, h_half, w_half = coarse // 2, gw1.shape[0] // 2, gw2.shape[0] // 2

    def send_piece(start, size):
        for h in range(2):
            src = pay.at[pl.ds(h * (rows + TAIL) + start, size)]

            @pl.when(core == h)
            def _():
                pltpu.make_async_copy(
                    src, keep_far.at[pl.ds(start, size)], out_sems.at[0]
                ).start()

            @pl.when(core != h)
            def _():
                pltpu.make_async_copy(
                    src, send_far.at[pl.ds(start, size)], out_sems.at[1]
                ).start()

    def put(start, size, full):
        for h in range(2):
            at = h * (rows + TAIL) + start
            pay[at : at + size] = full[h * size : (h + 1) * size].astype(BF)

    put(0, c_half, csum)
    send_piece(0, c_half)
    loads[3].wait()
    put(c_half + h_half, w_half, gw2[...].astype(F32) + dot_lt(hidden, d_proj))
    send_piece(c_half + h_half, w_half)
    loads[4].wait()
    w1_part = jnp.concatenate(
        [
            gw1[k * lat : (k + 1) * lat].astype(F32) + dot_lt(x[...], d_pre)
            for k, x in enumerate((up, xs, xr))
        ],
        axis=0,
    )
    put(c_half, h_half, w1_part)
    send_piece(c_half, h_half)
    used = c_half + h_half + w_half
    ids = lax.broadcasted_iota(jnp.int32, (TAIL, lat), 0)
    edge_row = jnp.broadcast_to(gg[...] + gain_part, (TAIL, lat))
    node_row = jnp.broadcast_to(ngg[...], (TAIL, lat))
    tail = jnp.where(ids == 0, edge_row, jnp.where(ids == 1, node_row, 0.0)).astype(BF)
    for h in range(2):
        at = h * (rows + TAIL)
        if used < rows:
            pay[at + used : at + rows] = jnp.zeros((rows - used, lat), BF)
        pay[at + rows : at + rows + TAIL] = tail
    send_piece(used, rows + TAIL - used)
    for k, out_far in enumerate((keep_far, send_far)):
        pltpu.make_async_copy(pay.at[pl.ds(0, rows + TAIL)], out_far, out_sems.at[k]).wait()


def widen_kernel(core, half, coarse_ref, first_ref, second_ref, *, scale):
    start = 0
    for out_ref, factor in ((coarse_ref, None), (first_ref, scale), (second_ref, scale)):
        rows = out_ref.shape[1]
        values = half[start : start + rows].astype(F32)
        out_ref[0] = values if factor is None else values * factor
        start += rows


def widen_other_kernel(core, half, c_in, f_in, s_in, coarse_ref, first_ref, second_ref, *, scale):
    widen_kernel(core, half, coarse_ref, first_ref, second_ref, scale=scale)


def params(*semantics):
    return pltpu.CompilerParams(
        dimension_semantics=semantics or None, vmem_limit_bytes=VMEM_LIMIT
    )


def cost(micros):
    return pl.CostEstimate(
        flops=int(micros * 1.1e9), transcendentals=0, bytes_accessed=int(micros * 3.0e6)
    )


def shape(rows, cols, dtype):
    return jax.ShapeDtypeStruct((rows, cols), dtype)


def far(rows, cols, dtype):
    return pltpu.HBM((rows, cols), dtype)


def in_far(*arrays):
    return [pltpu.with_memory_space_constraint(a, pltpu.HBM) for a in arrays]


IN_VMEM = pl.BlockSpec(memory_space=pltpu.VMEM)
IN_SMEM = pl.BlockSpec(memory_space=pltpu.SMEM)
IN_HBM = pl.BlockSpec(memory_space=pl.ANY)


def loads_of(sources, targets, sems):
    return [
        pltpu.make_async_copy(src, dst, sems.at[k])
        for k, (src, dst) in enumerate(zip(sources, targets))
    ]


def buffers(*arrays):
    return [pltpu.VMEM(a.shape, a.dtype) for a in arrays] + [
        pltpu.SemaphoreType.DMA((len(arrays),))
    ]


def swap(x, axes, count):
    if count == 1:
        return x
    return lax.all_to_all(x, axes, 0, 0, tiled=True)


GROUPS = ("core", ("x", "y"), "z")


def owner_index():
    index = jnp.int32(0)
    for axes in GROUPS:
        index = index * lax.axis_size(axes) + lax.axis_index(axes)
    return index


def exchange(x, mask):
    devices = lax.axis_size(EVERYONE)
    if devices == 1:
        return x
    return lax.ppermute(x, EVERYONE, [(i, i ^ mask) for i in range(devices)])


def sum_group(got, count):
    return jnp.sum(got.reshape(count, -1, got.shape[1]).astype(F32), axis=0)


def copies(x, count):
    return jnp.broadcast_to(x[None], (count,) + x.shape).reshape(-1, x.shape[1])


def reduce_rows(keep, send):
    x = keep.astype(F32) + exchange(send, 1).astype(F32)
    for axes in GROUPS[1:]:
        count = lax.axis_size(axes)
        x = sum_group(swap(x.astype(BF), axes, count), count)
    return x


def gather_halves(x):
    for axes in reversed(GROUPS[1:]):
        count = lax.axis_size(axes)
        x = swap(copies(x, count), axes, count)
    return x, exchange(x, 1)


def reduce_with_tail(keep, send, wait_for):
    cols = keep.shape[1]
    rows = keep.shape[0] - TAIL
    got = exchange(send, 1)
    got, wait_for = lax.optimization_barrier((got, wait_for))
    x = (*in_far(keep), got)
    for axes, kernel in zip(GROUPS[1:], (fold_pair_kernel, fold_group_kernel)):
        count = lax.axis_size(axes)
        part = rows // count
        x = pl.pallas_call(
            kernel,
            out_shape=pltpu.HBM((count, part + TAIL, cols), BF),
            compiler_params=params(),
            cost_estimate=cost(3.0),
        )(*x)
        x = (swap(x.reshape(-1, cols), axes, count).reshape(x.shape),)
        rows = part
    x = jnp.sum(x[0].astype(F32), axis=0)
    return x[:rows].astype(BF), x[rows:], wait_for


def bit_masks(devices):
    slow = devices // lax.axis_size("z")
    order = [1 << b for b in range(1, devices.bit_length() - 1)]
    return (
        [m for m in order if m == slow]
        + [m for m in reversed(order) if m < slow]
        + [m for m in order if m > slow]
    )


def halving_sum(keep, send):
    devices = lax.axis_size(EVERYONE)
    masks = [1] + bit_masks(devices)
    place = lax.axis_index(EVERYONE)
    for mask, after in zip(masks, masks[1:]):
        rows, cols = keep.shape
        bit = ((place & after) > 0).astype(jnp.int32).reshape(1)
        got = exchange(send, mask)
        keep, send = pl.pallas_call(
            fold_split_kernel,
            in_specs=[pl.BlockSpec(memory_space=pltpu.SMEM)]
            + [pl.BlockSpec(memory_space=pltpu.VMEM)] * 2,
            out_shape=(far(rows // 2, cols, BF), shape(rows // 2, cols, BF)),
            compiler_params=params(),
            cost_estimate=cost(1.0),
            name="fold_split",
        )(bit, *in_far(keep), got)
    got = exchange(send, masks[-1])
    x = (keep.astype(F32) + got.astype(F32)).astype(BF)
    for mask in reversed(masks):
        other = exchange(x, mask)
        x = jnp.where(
            (place & mask) > 0, jnp.concatenate([other, x], 0), jnp.concatenate([x, other], 0)
        )
    return x


def padded_rows(rows, devices):
    return -(-rows // (16 * devices)) * 16 * devices


def per_device(
    node, coarse, edge, up, w1, w2, gain, nw1, nw2, ngain, ncot, ccot, ecot, ucot,
    send_rows, edge_sender, edge_receiver, up_sender, up_receiver,
):
    n, lat = node.shape
    width = w2.shape[0]
    ccount = coarse.shape[0]
    ecount = edge.shape[0]
    ucount = up.shape[0]
    devices, slots = send_rows.shape[1], send_rows.shape[2]
    imports = devices * slots
    es, er = in_far(edge_sender.reshape(1, ecount), edge_receiver.reshape(1, ecount))
    us, ur = in_far(up_sender.reshape(1, ucount), up_receiver.reshape(1, ucount))
    gain_row, ngain_row = in_far(gain.reshape(1, lat), ngain.reshape(1, lat))
    own = owner_index()
    core = lax.axis_index("core").reshape(1)

    table = send_rows.reshape(imports)
    hot_send = (table[:, None] == jnp.arange(n, dtype=jnp.int32)[None, :]).astype(BF)
    outgoing = dot(hot_send, node).astype(BF)
    halo = lax.all_to_all(
        outgoing.reshape(devices, slots, lat), EVERYONE, 0, 0, tiled=True
    ).reshape(imports, lat)

    up_pre, up_xs, up_xr, keep, send = pl.pallas_call(
        up_forward_kernel,
        in_specs=[IN_VMEM] * 2 + [IN_SMEM] + [IN_VMEM] * 2 + [IN_HBM] * 4,
        out_shape=(
            far(ucount, width, F32), far(ucount, lat, BF), far(ucount, lat, BF),
            far(ccount // 2, lat, BF), shape(ccount // 2, lat, BF),
        ),
        scratch_shapes=[pltpu.VMEM((ccount, lat), F32)] + buffers(node, coarse, w1, w2),
        compiler_params=params(),
        cost_estimate=cost(5.0),
        name="up_forward",
    )(us, ur, core, *in_far(up), gain_row, *in_far(node, coarse, w1, w2))

    coarse_total = reduce_rows(keep, send)

    tile = math.gcd(ecount, 256)
    steps = ecount // tile
    rows_spec = pl.BlockSpec((tile, lat), lambda i: (i, 0))
    index_spec = pl.BlockSpec((1, tile), lambda i: (0, i))
    fixed = lambda r, c: pl.BlockSpec((r, c), lambda i: (0, 0))
    pre, xs, fine_total = pl.pallas_call(
        edge_forward_kernel,
        grid=(steps,),
        in_specs=[index_spec, index_spec, rows_spec] + [IN_VMEM] * 2 + [IN_HBM] * 4,
        out_specs=[pl.BlockSpec((tile, width), lambda i: (i, 0)), rows_spec, fixed(n, lat)],
        out_shape=(far(ecount, width, F32), far(ecount, lat, BF), far(n, lat, BF)),
        scratch_shapes=[pltpu.VMEM((n, lat), F32)] + buffers(node, coarse, w1, w2),
        compiler_params=params("arbitrary"),
        cost_estimate=cost(9.0),
        name="edge_forward",
    )(es, er, *in_far(edge), halo, gain_row, *in_far(node, coarse, w1, w2))

    fine_grad, grad_n, ngw1, ngw2, ngg = pl.pallas_call(
        node_kernel,
        in_specs=[IN_VMEM] * 4 + [IN_HBM] * 2,
        scratch_shapes=buffers(nw1, nw2),
        out_shape=(
            far(n, lat, F32), far(n, lat, F32), far(2 * lat, width, BF),
            far(width, lat, BF), shape(1, lat, F32),
        ),
        compiler_params=params(),
        cost_estimate=cost(5.0),
        name="node_mlp",
    )(*in_far(node, fine_total), ngain_row, *in_far(ncot, nw1, nw2))

    grad_e, d_pre, gw2, gg = pl.pallas_call(
        edge_cotangent_kernel,
        grid=(steps,),
        in_specs=[index_spec, pl.BlockSpec((tile, width), lambda i: (i, 0)), rows_spec]
        + [IN_VMEM] * 2
        + [IN_HBM] * 2,
        out_specs=[
            rows_spec, pl.BlockSpec((tile, width), lambda i: (i, 0)), fixed(width, lat),
            fixed(1, lat),
        ],
        out_shape=(
            far(ecount, lat, F32), far(ecount, width, BF), far(width, lat, BF),
            shape(1, lat, F32),
        ),
        scratch_shapes=[pltpu.VMEM((width, lat), F32)] + buffers(far(lat, width, BF), w2),
        compiler_params=params("arbitrary"),
        cost_estimate=cost(8.0),
        name="edge_cotangent",
    )(
        er, *in_far(pre, ecot, fine_grad), gain_row, *in_far(w1, w2)
    )

    gw1, node_part, returning, coarse_local = pl.pallas_call(
        edge_product_kernel,
        grid=(steps,),
        in_specs=[
            index_spec, index_spec, rows_spec, rows_spec,
            pl.BlockSpec((tile, width), lambda i: (i, 0)),
        ]
        + [IN_HBM] * 2,
        out_specs=[
            fixed(3 * lat, width), fixed(n, lat), fixed(imports, lat), fixed(ccount, lat),
        ],
        out_shape=(
            far(3 * lat, width, BF), far(n, lat, F32), shape(imports, lat, BF),
            far(ccount, lat, BF),
        ),
        scratch_shapes=[
            pltpu.VMEM((n + imports + ccount, width), F32), pltpu.VMEM((n, width), F32),
            pltpu.VMEM((2 * lat, width), F32),
        ]
        + buffers(node, far(2 * lat, width, BF)),
        compiler_params=params("arbitrary"),
        cost_estimate=cost(9.0),
        name="edge_product",
    )(es, er, *in_far(edge, xs, d_pre, node, w1))

    returned = lax.all_to_all(
        returning.reshape(devices, slots, lat), EVERYONE, 0, 0, tiled=True
    ).reshape(imports, lat)

    mine = ccount // devices
    padded = -(-mine // 16) * 16
    pad = lambda a: jnp.pad(a, ((0, padded - mine), (0, 0))) if padded > mine else a
    own_coarse = pad(lax.dynamic_slice_in_dim(coarse, own * mine, mine, 0))
    own_cot = pad(lax.dynamic_slice_in_dim(ccot, own * mine, mine, 0))
    node_rows = padded_rows(2 * lat + width, devices)
    coarse_grad, coarse_after, node_keep, node_send, ngg_sum = pl.pallas_call(
        coarse_kernel,
        in_specs=[IN_SMEM] + [IN_VMEM] * 5 + [IN_HBM] * 4,
        out_shape=(
            shape(padded, lat, BF), far(padded, lat, F32), far(node_rows // 2, lat, BF),
            shape(node_rows // 2, lat, BF), shape(1, lat, F32),
        ),
        scratch_shapes=[pltpu.VMEM((node_rows, lat), F32)] + buffers(nw1, nw2, ngw1, ngw2),
        compiler_params=params(),
        cost_estimate=cost(5.0),
        name="coarse_mlp",
    )(
        core, own_coarse, pad(coarse_total), own_cot, ngain_row, ngg,
        *in_far(nw1, nw2, ngw1, ngw2),
    )
    cg_own, cg_other = gather_halves(coarse_grad[:mine])

    node_total = halving_sum(node_keep, node_send)

    edge_rows = padded_rows(ccount + 3 * lat + width, devices)
    grad_u, up_node_part, keep, send = pl.pallas_call(
        up_backward_kernel,
        in_specs=[IN_VMEM] * 2 + [IN_SMEM] + [IN_VMEM] * 11 + [IN_HBM] * 5,
        out_specs=[IN_VMEM] * 2 + [IN_HBM] * 2,
        out_shape=(
            far(ucount, lat, F32), far(n, lat, F32), far(edge_rows // 2 + TAIL, lat, BF),
            far(edge_rows // 2 + TAIL, lat, BF),
        ),
        scratch_shapes=[
            pltpu.VMEM((ccount, lat), F32), pltpu.VMEM((edge_rows + 2 * TAIL, lat), BF),
        ]
        + buffers(w2, w1, coarse_local, gw2, gw1)
        + [pltpu.SemaphoreType.DMA((2,))],
        compiler_params=params(),
        cost_estimate=cost(8.0),
        name="up_backward",
    )(
        us, ur, jnp.stack([own, core[0]]), *in_far(up, up_xs, up_xr, up_pre, ucot), cg_own,
        cg_other, gain_row, gg, ngg_sum, *in_far(coarse_after[:mine]),
        *in_far(w2, w1, coarse_local, gw2, gw1),
    )
    block, gains, returned = reduce_with_tail(keep, send, returned)
    own_half, other_half = gather_halves(block)
    edge_scale = 1.0 / math.sqrt((ecount + ucount) * devices)
    node_scale = 1.0 / math.sqrt(n * devices + ccount)
    halves = [ccount // 2, 3 * lat // 2, width // 2]
    outs = tuple(pltpu.HBM((2, rows, lat), F32) for rows in halves)

    def place_of(flip):
        return [
            pl.BlockSpec((1, rows, lat), lambda i, c: (c[0] ^ flip, 0, 0)) for rows in halves
        ]

    half_spec = pl.BlockSpec(own_half.shape, lambda i, c: (0, 0))
    written = pl.pallas_call(
        functools.partial(widen_kernel, scale=edge_scale),
        grid_spec=pltpu.PrefetchScalarGridSpec(
            num_scalar_prefetch=1, grid=(1,), in_specs=[half_spec], out_specs=place_of(0)
        ),
        out_shape=outs,
        compiler_params=params("arbitrary"),
        cost_estimate=cost(2.5),
        name="widen_own",
    )(core, own_half)
    written = pl.pallas_call(
        functools.partial(widen_other_kernel, scale=edge_scale),
        grid_spec=pltpu.PrefetchScalarGridSpec(
            num_scalar_prefetch=1,
            grid=(1,),
            in_specs=[half_spec] + [pl.BlockSpec(memory_space=pl.ANY)] * 3,
            out_specs=place_of(1),
        ),
        out_shape=outs,
        input_output_aliases={2: 0, 3: 1, 4: 2},
        compiler_params=params("arbitrary"),
        cost_estimate=cost(2.5),
        name="widen_other",
    )(core, other_half, *in_far(*written))
    grad_coarse, grad_edge_in, grad_edge_out = (a.reshape(-1, lat) for a in written)

    grad_nodes = (
        grad_n
        + node_part
        + up_node_part
        + lax.dot_general(hot_send, returned, (((0,), (0,)), ((), ())), preferred_element_type=F32)
    )
    grad_node_in = node_total[: 2 * lat].astype(F32) * node_scale
    grad_node_out = node_total[2 * lat : 2 * lat + width].astype(F32) * node_scale
    return (
        grad_nodes,
        grad_coarse,
        grad_e,
        grad_u,
        grad_edge_in,
        grad_edge_out,
        gains[0] * edge_scale,
        grad_node_in,
        grad_node_out,
        gains[1] * node_scale,
    )


def split_mesh(mesh):
    face, band = mesh.shape["face"], mesh.shape["band"]
    z = 1
    while z * z < face or face % z:
        z += 1
    core = 2 if band % 2 == 0 else 1
    return Mesh(
        mesh.devices.reshape(z, face // z, band // core, core), ("z", "x", "y", "core")
    )


def solution(mesh):
    rows, split = P(EVERYONE, None), P(EVERYONE)
    return jax.shard_map(
        per_device,
        mesh=split_mesh(mesh),
        in_specs=(
            rows, P(), rows, rows, P(), P(), P(), P(), P(), P(), rows, P(), rows, rows,
            P(EVERYONE, None, None), split, split, split, split,
        ),
        out_specs=(rows, P(), rows, rows, P(), P(), P(), P(), P(), P()),
        check_vma=False,
    )
```

```python
import functools
import math

import jax
import jax.numpy as jnp
from jax import lax
from jax.experimental import pallas as pl
from jax.experimental.pallas import tpu as pltpu
from jax.sharding import Mesh, PartitionSpec as P

EPSILON = 1e-05
BF = jnp.bfloat16
F32 = jnp.float32
TAIL = 16
EVERYONE = ("z", "x", "y", "core")
VMEM_LIMIT = 24 * 1024 * 1024


def dot(a, b):
    return lax.dot_general(a, b, (((1,), (0,)), ((), ())), preferred_element_type=F32)


def dot_lt(a, b):
    return lax.dot_general(a, b, (((0,), (0,)), ((), ())), preferred_element_type=F32)


def dot_rt(a, b):
    return lax.dot_general(a, b, (((1,), (1,)), ((), ())), preferred_element_type=F32)


def onehot_t(index_row, rows, offset=0):
    ids = lax.broadcasted_iota(jnp.int32, (rows, index_row.shape[1]), 0) + offset
    return jnp.where(ids == index_row, 1.0, 0.0).astype(BF)


def hidden_of(pre):
    return (pre * jax.nn.sigmoid(pre)).astype(BF)


def normalise(projected):
    center = projected - jnp.mean(projected, axis=1, keepdims=True)
    inv_std = lax.rsqrt(jnp.mean(center * center, axis=1, keepdims=True) + EPSILON)
    return center * inv_std, inv_std


def grad_to_pre(pre, normed, inv_std, cot, gain, w2):
    gain_part = jnp.sum(cot * normed, axis=0, keepdims=True)
    scaled = cot * gain
    d_proj = (
        inv_std
        * (
            scaled
            - jnp.mean(scaled, axis=1, keepdims=True)
            - normed * jnp.mean(scaled * normed, axis=1, keepdims=True)
        )
    ).astype(BF)
    d_hidden = dot_rt(d_proj, w2)
    logistic = jax.nn.sigmoid(pre)
    d_pre = (d_hidden * logistic * (1.0 + pre * (1.0 - logistic))).astype(BF)
    return gain_part, d_proj, d_pre


def gather_f32(onehot, table):
    high = table.astype(BF)
    low = (table - high.astype(F32)).astype(BF)
    return dot_lt(onehot, high) + dot_lt(onehot, low)


def split_rows(ref, bit, keep_ref, send_ref):
    half = keep_ref.shape[0]
    keep_ref[...] = ref[pl.ds(pl.multiple_of(bit * half, 16), half), :].astype(BF)
    send_ref[...] = ref[pl.ds(pl.multiple_of((1 - bit) * half, 16), half), :].astype(BF)


def fold_split_kernel(bit, keep, recv, keep_ref, send_ref):
    half = keep_ref.shape[0]
    for side, out_ref in ((bit[0], keep_ref), (1 - bit[0], send_ref)):
        rows = pl.ds(pl.multiple_of(side * half, 16), half)
        out_ref[...] = (keep[rows, :].astype(F32) + recv[rows, :].astype(F32)).astype(BF)


def fold_pair_kernel(keep, recv, out_ref):
    count, rows, _ = out_ref.shape
    rows -= TAIL
    tail = (keep[count * rows :].astype(F32) + recv[count * rows :].astype(F32)).astype(BF)
    for k in range(count):
        piece = slice(k * rows, (k + 1) * rows)
        out_ref[k, 0:rows] = (keep[piece].astype(F32) + recv[piece].astype(F32)).astype(BF)
        out_ref[k, rows:] = tail


def fold_group_kernel(got, out_ref):
    group = got.shape[0]
    count, rows, _ = out_ref.shape
    rows -= TAIL

    def total(at, size):
        piece = slice(at, at + size)
        acc = got[0, piece].astype(F32)
        for k in range(1, group):
            acc += got[k, piece].astype(F32)
        return acc.astype(BF)

    tail = total(count * rows, TAIL)
    for k in range(count):
        out_ref[k, 0:rows] = total(k * rows, rows)
        out_ref[k, rows:] = tail


def up_forward_kernel(
    us, ur, core, up, gain, node_far, coarse_far, w1_far, w2_far,
    p_ref, xs_ref, xr_ref, keep_ref, send_ref, part, node, coarse, w1, w2, sems,
):
    loads = loads_of((node_far, coarse_far, w1_far, w2_far), (node, coarse, w1, w2), sems)
    for load in loads:
        load.start()
    lat = up.shape[1]
    hot_s = onehot_t(us[...], node.shape[0])
    hot_r = onehot_t(ur[...], coarse.shape[0])
    loads[0].wait()
    xs = dot_lt(hot_s, node[...]).astype(BF)
    loads[1].wait()
    xr = dot_lt(hot_r, coarse[...]).astype(BF)
    loads[2].wait()
    pre = dot(up[...], w1[0:lat]) + dot(xs, w1[lat : 2 * lat]) + dot(xr, w1[2 * lat :])
    loads[3].wait()
    normed, _ = normalise(dot(hidden_of(pre), w2[...]))
    new = (up[...].astype(F32) + normed * gain[...]).astype(BF)
    p_ref[...] = pre
    xs_ref[...] = xs
    xr_ref[...] = xr
    part[...] = dot(hot_r, new)
    split_rows(part, core[0], keep_ref, send_ref)


def edge_forward_kernel(
    es, er, edge, halo, gain, w1_far, w2_far, node_far, coarse_far, p_ref, xs_ref, total_ref,
    acc, w1, w2, node, coarse, sems,
):
    step = pl.program_id(0)
    lat = edge.shape[1]
    n = node.shape[0]
    imports = halo.shape[0]
    parts = [slice(k * lat, (k + 1) * lat) for k in (0, 2, 1)]
    first, last, middle = (
        pltpu.make_async_copy(w1_far.at[part], w1.at[part], sems.at[k])
        for k, part in enumerate(parts)
    )
    node_load = pltpu.make_async_copy(node_far, node, sems.at[3])
    coarse_load = pltpu.make_async_copy(coarse_far, coarse, sems.at[4])
    w2_load = pltpu.make_async_copy(w2_far, w2, sems.at[5])

    @pl.when(step == 0)
    def _():
        for load in (first, node_load, last, coarse_load, middle, w2_load):
            load.start()
        acc[...] = jnp.zeros_like(acc)

    sender = es[...]
    hot_r = onehot_t(er[...], n)

    @pl.when(step == 0)
    def _():
        first.wait()

    pre = dot(edge[...], w1[0:lat])

    @pl.when(step == 0)
    def _():
        node_load.wait()
        last.wait()

    pre += dot(dot_lt(hot_r, node[...]).astype(BF), w1[2 * lat :])
    xs = dot_lt(onehot_t(sender, n), node[...]) + dot_lt(
        onehot_t(sender, imports, n), halo[...]
    )
    hot_c = onehot_t(sender, coarse.shape[0], n + imports)

    @pl.when(step == 0)
    def _():
        coarse_load.wait()
        middle.wait()
        w2_load.wait()

    xs = (xs + dot_lt(hot_c, coarse[...])).astype(BF)
    pre += dot(xs, w1[lat : 2 * lat])
    normed, _ = normalise(dot(hidden_of(pre), w2[...]))
    new = (edge[...].astype(F32) + normed * gain[...]).astype(BF)
    p_ref[...] = pre
    xs_ref[...] = xs
    acc[...] += dot(hot_r, new)

    @pl.when(step == pl.num_programs(0) - 1)
    def _():
        total_ref[...] = acc[...].astype(BF)


def node_kernel(
    node, total_in, ngain, ncot, nw1_far, nw2_far, fg_ref, gn_ref, ngw1_ref, ngw2_ref, ngg_ref,
    nw1, nw2, sems,
):
    loads = loads_of((nw1_far, nw2_far), (nw1, nw2), sems)
    for load in loads:
        load.start()
    lat = node.shape[1]
    total = total_in[...]
    loads[0].wait()
    node_pre = dot(node[...], nw1[0:lat]) + dot(total, nw1[lat:])
    hidden = hidden_of(node_pre)
    loads[1].wait()
    node_normed, inv_std = normalise(dot(hidden, nw2[...]))
    cot = ncot[...].astype(F32)
    gain_part, d_proj, d_pre = grad_to_pre(
        node_pre, node_normed, inv_std, cot, ngain[...], nw2[...]
    )
    ngg_ref[...] = gain_part
    ngw2_ref[...] = dot_lt(hidden, d_proj).astype(BF)
    ngw1_ref[0:lat] = dot_lt(node[...], d_pre).astype(BF)
    ngw1_ref[lat:] = dot_lt(total, d_pre).astype(BF)
    gn_ref[...] = cot + dot_rt(d_pre, nw1[0:lat])
    fg_ref[...] = dot_rt(d_pre, nw1[lat:])


def edge_backward_kernel(
    es, er, edge, xs, pre_ref, ecot, gain, w2_far, fg_far, w1_far, node_far,
    ge_ref, gw1_out, gw2_out, gg_ref, np_ref, ret_ref, cp_ref,
    sum_s, sum_r, gw1, gw2, w2, fg, w1, node, sems,
):
    step = pl.program_id(0)
    lat = edge.shape[1]
    n = node.shape[0]
    imports = ret_ref.shape[0]
    loads = loads_of((w2_far, fg_far, w1_far, node_far), (w2, fg, w1, node), sems)

    @pl.when(step == 0)
    def _():
        for load in loads:
            load.start()
        for ref in (sum_s, sum_r, gw1, gw2, gg_ref):
            ref[...] = jnp.zeros_like(ref)

    hot_r = onehot_t(er[...], n)
    pre = pre_ref[...]
    hidden = hidden_of(pre)

    @pl.when(step == 0)
    def _():
        loads[0].wait()

    normed, inv_std = normalise(dot(hidden, w2[...]))

    @pl.when(step == 0)
    def _():
        loads[1].wait()
        loads[2].wait()

    cot = ecot[...].astype(F32) + gather_f32(hot_r, fg[...])
    gain_part, d_proj, d_pre = grad_to_pre(pre, normed, inv_std, cot, gain[...], w2[...])
    gg_ref[...] += gain_part
    ge_ref[...] = cot + dot_rt(d_pre, w1[0:lat])
    gw2[...] += dot_lt(hidden, d_proj)
    gw1[0:lat] += dot_lt(edge[...], d_pre)
    gw1[lat:] += dot_lt(xs[...], d_pre)
    sum_r[...] += dot(hot_r, d_pre)
    sum_s[...] += dot(onehot_t(es[...], sum_s.shape[0]), d_pre)

    @pl.when(step == pl.num_programs(0) - 1)
    def _():
        loads[3].wait()
        w_s = w1[lat : 2 * lat]
        recv = sum_r[...].astype(BF)
        gw2_out[...] = gw2[...].astype(BF)
        gw1_out[0 : 2 * lat] = gw1[...].astype(BF)
        gw1_out[2 * lat :] = dot_lt(node[...], recv).astype(BF)
        np_ref[...] = dot_rt(sum_s[0:n].astype(BF), w_s) + dot_rt(recv, w1[2 * lat :])
        ret_ref[...] = dot_rt(sum_s[n : n + imports].astype(BF), w_s).astype(BF)
        cp_ref[...] = dot_rt(sum_s[n + imports :].astype(BF), w_s).astype(BF)


def coarse_kernel(
    core, rows, total_in, ccot, ngain, ngg, nw1_far, nw2_far, ngw1_far, ngw2_far,
    cg_ref, after_ref, keep_ref, send_ref, gg_ref, pay, nw1, nw2, ngw1, ngw2, sems,
):
    loads = loads_of(
        (nw1_far, nw2_far, ngw1_far, ngw2_far), (nw1, nw2, ngw1, ngw2), sems
    )
    for load in loads:
        load.start()
    lat = rows.shape[1]
    used = ngw1.shape[0] + ngw2.shape[0]
    total = total_in[...].astype(BF)
    loads[0].wait()
    pre = dot(rows[...], nw1[0:lat]) + dot(total, nw1[lat:])
    hidden = hidden_of(pre)
    loads[1].wait()
    normed, inv_std = normalise(dot(hidden, nw2[...]))
    cot = ccot[...].astype(F32)
    gain_part, d_proj, d_pre = grad_to_pre(pre, normed, inv_std, cot, ngain[...], nw2[...])
    cg_ref[...] = dot_rt(d_pre, nw1[lat:]).astype(BF)
    after_ref[...] = cot + dot_rt(d_pre, nw1[0:lat])
    loads[2].wait()
    loads[3].wait()
    pay[0:lat] = ngw1[0:lat].astype(F32) + dot_lt(rows[...], d_pre)
    pay[lat : 2 * lat] = ngw1[lat:].astype(F32) + dot_lt(total, d_pre)
    pay[2 * lat : used] = ngw2[...].astype(F32) + dot_lt(hidden, d_proj)
    if used < pay.shape[0]:
        pay[used:] = jnp.zeros((pay.shape[0] - used, lat), F32)
    split_rows(pay, core[0], keep_ref, send_ref)
    gg_ref[...] = ngg[...] + gain_part


def up_backward_kernel(
    us, ur, place, up, xs, xr, pre_ref, ucot, cg_own, cg_other, gain, gg, ngg, after,
    w2_far, w1_far, cp_far, gw2_far, gw1_far, gu_ref, np_ref, keep_far, send_far,
    csum, pay, w2, w1, cp, gw2, gw1, sems, out_sems,
):
    loads = loads_of(
        (w2_far, w1_far, cp_far, gw2_far, gw1_far), (w2, w1, cp, gw2, gw1), sems
    )
    for load in loads:
        load.start()
    lat = up.shape[1]
    half = cg_own.shape[0]
    coarse = csum.shape[0]
    core = place[1]
    hot_r = onehot_t(ur[...], coarse)
    turned = ur[...] - core * half
    turned = jnp.where(turned < 0, turned + coarse, turned)
    cot = (
        ucot[...].astype(F32)
        + dot_lt(onehot_t(turned, half), cg_own[...])
        + dot_lt(onehot_t(turned, half, half), cg_other[...])
    )
    pre = pre_ref[...]
    hidden = hidden_of(pre)
    loads[0].wait()
    normed, inv_std = normalise(dot(hidden, w2[...]))
    gain_part, d_proj, d_pre = grad_to_pre(pre, normed, inv_std, cot, gain[...], w2[...])
    loads[1].wait()
    gu_ref[...] = cot + dot_rt(d_pre, w1[0:lat])
    send = dot(onehot_t(us[...], np_ref.shape[0]), d_pre).astype(BF)
    np_ref[...] = dot_rt(send, w1[lat : 2 * lat])
    loads[2].wait()
    csum[...] = cp[...].astype(F32) + dot_rt(dot(hot_r, d_pre).astype(BF), w1[2 * lat :])
    count = after.shape[0]
    mine = pl.ds(pl.multiple_of(place[0] * count, 8), count)
    csum[mine, :] = csum[mine, :] + after[...]
    rows = pay.shape[0] // 2 - TAIL
    c_half, h_half, w_half = coarse // 2, gw1.shape[0] // 2, gw2.shape[0] // 2

    def send_piece(start, size):
        for h in range(2):
            src = pay.at[pl.ds(h * (rows + TAIL) + start, size)]

            @pl.when(core == h)
            def _():
                pltpu.make_async_copy(
                    src, keep_far.at[pl.ds(start, size)], out_sems.at[0]
                ).start()

            @pl.when(core != h)
            def _():
                pltpu.make_async_copy(
                    src, send_far.at[pl.ds(start, size)], out_sems.at[1]
                ).start()

    def put(start, size, full):
        for h in range(2):
            at = h * (rows + TAIL) + start
            pay[at : at + size] = full[h * size : (h + 1) * size].astype(BF)

    put(0, c_half, csum)
    send_piece(0, c_half)
    loads[3].wait()
    put(c_half + h_half, w_half, gw2[...].astype(F32) + dot_lt(hidden, d_proj))
    send_piece(c_half + h_half, w_half)
    loads[4].wait()
    w1_part = jnp.concatenate(
        [
            gw1[k * lat : (k + 1) * lat].astype(F32) + dot_lt(x[...], d_pre)
            for k, x in enumerate((up, xs, xr))
        ],
        axis=0,
    )
    put(c_half, h_half, w1_part)
    send_piece(c_half, h_half)
    used = c_half + h_half + w_half
    ids = lax.broadcasted_iota(jnp.int32, (TAIL, lat), 0)
    edge_row = jnp.broadcast_to(gg[...] + gain_part, (TAIL, lat))
    node_row = jnp.broadcast_to(ngg[...], (TAIL, lat))
    tail = jnp.where(ids == 0, edge_row, jnp.where(ids == 1, node_row, 0.0)).astype(BF)
    for h in range(2):
        at = h * (rows + TAIL)
        if used < rows:
            pay[at + used : at + rows] = jnp.zeros((rows - used, lat), BF)
        pay[at + rows : at + rows + TAIL] = tail
    send_piece(used, rows + TAIL - used)
    for k, out_far in enumerate((keep_far, send_far)):
        pltpu.make_async_copy(pay.at[pl.ds(0, rows + TAIL)], out_far, out_sems.at[k]).wait()


def widen_kernel(core, half, coarse_ref, first_ref, second_ref, *, scale):
    start = 0
    for out_ref, factor in ((coarse_ref, None), (first_ref, scale), (second_ref, scale)):
        rows = out_ref.shape[1]
        values = half[start : start + rows].astype(F32)
        out_ref[0] = values if factor is None else values * factor
        start += rows


def widen_other_kernel(core, half, c_in, f_in, s_in, coarse_ref, first_ref, second_ref, *, scale):
    widen_kernel(core, half, coarse_ref, first_ref, second_ref, scale=scale)


def params(*semantics):
    return pltpu.CompilerParams(
        dimension_semantics=semantics or None, vmem_limit_bytes=VMEM_LIMIT
    )


def cost(micros):
    return pl.CostEstimate(
        flops=int(micros * 1.1e9), transcendentals=0, bytes_accessed=int(micros * 3.0e6)
    )


def shape(rows, cols, dtype):
    return jax.ShapeDtypeStruct((rows, cols), dtype)


def far(rows, cols, dtype):
    return pltpu.HBM((rows, cols), dtype)


def in_far(*arrays):
    return [pltpu.with_memory_space_constraint(a, pltpu.HBM) for a in arrays]


IN_VMEM = pl.BlockSpec(memory_space=pltpu.VMEM)
IN_SMEM = pl.BlockSpec(memory_space=pltpu.SMEM)
IN_HBM = pl.BlockSpec(memory_space=pl.ANY)


def loads_of(sources, targets, sems):
    return [
        pltpu.make_async_copy(src, dst, sems.at[k])
        for k, (src, dst) in enumerate(zip(sources, targets))
    ]


def buffers(*arrays):
    return [pltpu.VMEM(a.shape, a.dtype) for a in arrays] + [
        pltpu.SemaphoreType.DMA((len(arrays),))
    ]


def swap(x, axes, count):
    if count == 1:
        return x
    return lax.all_to_all(x, axes, 0, 0, tiled=True)


GROUPS = ("core", ("x", "y"), "z")


def owner_index():
    index = jnp.int32(0)
    for axes in GROUPS:
        index = index * lax.axis_size(axes) + lax.axis_index(axes)
    return index


def exchange(x, mask):
    devices = lax.axis_size(EVERYONE)
    if devices == 1:
        return x
    return lax.ppermute(x, EVERYONE, [(i, i ^ mask) for i in range(devices)])


def sum_group(got, count):
    return jnp.sum(got.reshape(count, -1, got.shape[1]).astype(F32), axis=0)


def copies(x, count):
    return jnp.broadcast_to(x[None], (count,) + x.shape).reshape(-1, x.shape[1])


def reduce_rows(keep, send):
    x = keep.astype(F32) + exchange(send, 1).astype(F32)
    for axes in GROUPS[1:]:
        count = lax.axis_size(axes)
        x = sum_group(swap(x.astype(BF), axes, count), count)
    return x


def gather_halves(x):
    for axes in reversed(GROUPS[1:]):
        count = lax.axis_size(axes)
        x = swap(copies(x, count), axes, count)
    return x, exchange(x, 1)


def reduce_with_tail(keep, send, wait_for):
    cols = keep.shape[1]
    rows = keep.shape[0] - TAIL
    got = exchange(send, 1)
    got, wait_for = lax.optimization_barrier((got, wait_for))
    x = (*in_far(keep), got)
    for axes, kernel in zip(GROUPS[1:], (fold_pair_kernel, fold_group_kernel)):
        count = lax.axis_size(axes)
        part = rows // count
        x = pl.pallas_call(
            kernel,
            out_shape=pltpu.HBM((count, part + TAIL, cols), BF),
            compiler_params=params(),
            cost_estimate=cost(3.0),
        )(*x)
        x = (swap(x.reshape(-1, cols), axes, count).reshape(x.shape),)
        rows = part
    x = jnp.sum(x[0].astype(F32), axis=0)
    return x[:rows].astype(BF), x[rows:], wait_for


def bit_masks(devices):
    slow = devices // lax.axis_size("z")
    order = [1 << b for b in range(1, devices.bit_length() - 1)]
    return (
        [m for m in order if m == slow]
        + [m for m in reversed(order) if m < slow]
        + [m for m in order if m > slow]
    )


def halving_sum(keep, send):
    devices = lax.axis_size(EVERYONE)
    masks = [1] + bit_masks(devices)
    place = lax.axis_index(EVERYONE)
    for mask, after in zip(masks, masks[1:]):
        rows, cols = keep.shape
        bit = ((place & after) > 0).astype(jnp.int32).reshape(1)
        got = exchange(send, mask)
        keep, send = pl.pallas_call(
            fold_split_kernel,
            in_specs=[pl.BlockSpec(memory_space=pltpu.SMEM)]
            + [pl.BlockSpec(memory_space=pltpu.VMEM)] * 2,
            out_shape=(far(rows // 2, cols, BF), shape(rows // 2, cols, BF)),
            compiler_params=params(),
            cost_estimate=cost(1.0),
            name="fold_split",
        )(bit, *in_far(keep), got)
    got = exchange(send, masks[-1])
    x = (keep.astype(F32) + got.astype(F32)).astype(BF)
    for mask in reversed(masks):
        other = exchange(x, mask)
        x = jnp.where(
            (place & mask) > 0, jnp.concatenate([other, x], 0), jnp.concatenate([x, other], 0)
        )
    return x


def padded_rows(rows, devices):
    return -(-rows // (16 * devices)) * 16 * devices


def per_device(
    node, coarse, edge, up, w1, w2, gain, nw1, nw2, ngain, ncot, ccot, ecot, ucot,
    send_rows, edge_sender, edge_receiver, up_sender, up_receiver,
):
    n, lat = node.shape
    width = w2.shape[0]
    ccount = coarse.shape[0]
    ecount = edge.shape[0]
    ucount = up.shape[0]
    devices, slots = send_rows.shape[1], send_rows.shape[2]
    imports = devices * slots
    es, er = in_far(edge_sender.reshape(1, ecount), edge_receiver.reshape(1, ecount))
    us, ur = in_far(up_sender.reshape(1, ucount), up_receiver.reshape(1, ucount))
    gain_row, ngain_row = in_far(gain.reshape(1, lat), ngain.reshape(1, lat))
    own = owner_index()
    core = lax.axis_index("core").reshape(1)

    table = send_rows.reshape(imports)
    hot_send = (table[:, None] == jnp.arange(n, dtype=jnp.int32)[None, :]).astype(BF)
    outgoing = dot(hot_send, node).astype(BF)
    halo = lax.all_to_all(
        outgoing.reshape(devices, slots, lat), EVERYONE, 0, 0, tiled=True
    ).reshape(imports, lat)

    up_pre, up_xs, up_xr, keep, send = pl.pallas_call(
        up_forward_kernel,
        in_specs=[IN_VMEM] * 2 + [IN_SMEM] + [IN_VMEM] * 2 + [IN_HBM] * 4,
        out_shape=(
            far(ucount, width, F32), far(ucount, lat, BF), far(ucount, lat, BF),
            far(ccount // 2, lat, BF), shape(ccount // 2, lat, BF),
        ),
        scratch_shapes=[pltpu.VMEM((ccount, lat), F32)] + buffers(node, coarse, w1, w2),
        compiler_params=params(),
        cost_estimate=cost(5.0),
        name="up_forward",
    )(us, ur, core, *in_far(up), gain_row, *in_far(node, coarse, w1, w2))

    coarse_total = reduce_rows(keep, send)

    tile = math.gcd(ecount, 256)
    steps = ecount // tile
    rows_spec = pl.BlockSpec((tile, lat), lambda i: (i, 0))
    index_spec = pl.BlockSpec((1, tile), lambda i: (0, i))
    fixed = lambda r, c: pl.BlockSpec((r, c), lambda i: (0, 0))
    pre, xs, fine_total = pl.pallas_call(
        edge_forward_kernel,
        grid=(steps,),
        in_specs=[index_spec, index_spec, rows_spec] + [IN_VMEM] * 2 + [IN_HBM] * 4,
        out_specs=[pl.BlockSpec((tile, width), lambda i: (i, 0)), rows_spec, fixed(n, lat)],
        out_shape=(far(ecount, width, F32), far(ecount, lat, BF), far(n, lat, BF)),
        scratch_shapes=[pltpu.VMEM((n, lat), F32)]
        + buffers(w1, w2, node, coarse)[:-1]
        + [pltpu.SemaphoreType.DMA((6,))],
        compiler_params=params("arbitrary"),
        cost_estimate=cost(9.0),
        name="edge_forward",
    )(es, er, *in_far(edge), halo, gain_row, *in_far(w1, w2, node, coarse))

    fine_grad, grad_n, ngw1, ngw2, ngg = pl.pallas_call(
        node_kernel,
        in_specs=[IN_VMEM] * 4 + [IN_HBM] * 2,
        scratch_shapes=buffers(nw1, nw2),
        out_shape=(
            far(n, lat, F32), far(n, lat, F32), far(2 * lat, width, BF),
            far(width, lat, BF), shape(1, lat, F32),
        ),
        compiler_params=params(),
        cost_estimate=cost(5.0),
        name="node_mlp",
    )(*in_far(node, fine_total), ngain_row, *in_far(ncot, nw1, nw2))

    grad_e, gw1, gw2, gg, node_part, returning, coarse_local = pl.pallas_call(
        edge_backward_kernel,
        grid=(steps,),
        in_specs=[
            index_spec, index_spec, rows_spec, rows_spec,
            pl.BlockSpec((tile, width), lambda i: (i, 0)), rows_spec,
        ]
        + [IN_VMEM]
        + [IN_HBM] * 4,
        out_specs=[
            rows_spec, fixed(3 * lat, width), fixed(width, lat), fixed(1, lat), fixed(n, lat),
            fixed(imports, lat), fixed(ccount, lat),
        ],
        out_shape=(
            far(ecount, lat, F32), far(3 * lat, width, BF), far(width, lat, BF),
            shape(1, lat, F32), far(n, lat, F32), shape(imports, lat, BF),
            far(ccount, lat, BF),
        ),
        scratch_shapes=[
            pltpu.VMEM((n + imports + ccount, width), F32), pltpu.VMEM((n, width), F32),
            pltpu.VMEM((2 * lat, width), F32), pltpu.VMEM((width, lat), F32),
        ]
        + buffers(w2, fine_grad, w1, node),
        compiler_params=params("arbitrary"),
        cost_estimate=cost(15.0),
        name="edge_backward",
    )(es, er, *in_far(edge, xs, pre, ecot), gain_row, *in_far(w2, fine_grad, w1, node))

    returned = lax.all_to_all(
        returning.reshape(devices, slots, lat), EVERYONE, 0, 0, tiled=True
    ).reshape(imports, lat)

    mine = ccount // devices
    padded = -(-mine // 16) * 16
    pad = lambda a: jnp.pad(a, ((0, padded - mine), (0, 0))) if padded > mine else a
    own_coarse = pad(lax.dynamic_slice_in_dim(coarse, own * mine, mine, 0))
    own_cot = pad(lax.dynamic_slice_in_dim(ccot, own * mine, mine, 0))
    node_rows = padded_rows(2 * lat + width, devices)
    coarse_grad, coarse_after, node_keep, node_send, ngg_sum = pl.pallas_call(
        coarse_kernel,
        in_specs=[IN_SMEM] + [IN_VMEM] * 5 + [IN_HBM] * 4,
        out_shape=(
            shape(padded, lat, BF), far(padded, lat, F32), far(node_rows // 2, lat, BF),
            shape(node_rows // 2, lat, BF), shape(1, lat, F32),
        ),
        scratch_shapes=[pltpu.VMEM((node_rows, lat), F32)] + buffers(nw1, nw2, ngw1, ngw2),
        compiler_params=params(),
        cost_estimate=cost(5.0),
        name="coarse_mlp",
    )(
        core, own_coarse, pad(coarse_total), own_cot, ngain_row, ngg,
        *in_far(nw1, nw2, ngw1, ngw2),
    )
    cg_own, cg_other = gather_halves(coarse_grad[:mine])

    node_total = halving_sum(node_keep, node_send)

    edge_rows = padded_rows(ccount + 3 * lat + width, devices)
    grad_u, up_node_part, keep, send = pl.pallas_call(
        up_backward_kernel,
        in_specs=[IN_VMEM] * 2 + [IN_SMEM] + [IN_VMEM] * 11 + [IN_HBM] * 5,
        out_specs=[IN_VMEM] * 2 + [IN_HBM] * 2,
        out_shape=(
            far(ucount, lat, F32), far(n, lat, F32), far(edge_rows // 2 + TAIL, lat, BF),
            far(edge_rows // 2 + TAIL, lat, BF),
        ),
        scratch_shapes=[
            pltpu.VMEM((ccount, lat), F32), pltpu.VMEM((edge_rows + 2 * TAIL, lat), BF),
        ]
        + buffers(w2, w1, coarse_local, gw2, gw1)
        + [pltpu.SemaphoreType.DMA((2,))],
        compiler_params=params(),
        cost_estimate=cost(8.0),
        name="up_backward",
    )(
        us, ur, jnp.stack([own, core[0]]), *in_far(up, up_xs, up_xr, up_pre, ucot), cg_own,
        cg_other, gain_row, gg, ngg_sum, *in_far(coarse_after[:mine]),
        *in_far(w2, w1, coarse_local, gw2, gw1),
    )
    block, gains, returned = reduce_with_tail(keep, send, returned)
    own_half, other_half = gather_halves(block)
    edge_scale = 1.0 / math.sqrt((ecount + ucount) * devices)
    node_scale = 1.0 / math.sqrt(n * devices + ccount)
    halves = [ccount // 2, 3 * lat // 2, width // 2]
    outs = tuple(pltpu.HBM((2, rows, lat), F32) for rows in halves)

    def place_of(flip):
        return [
            pl.BlockSpec((1, rows, lat), lambda i, c: (c[0] ^ flip, 0, 0)) for rows in halves
        ]

    half_spec = pl.BlockSpec(own_half.shape, lambda i, c: (0, 0))
    written = pl.pallas_call(
        functools.partial(widen_kernel, scale=edge_scale),
        grid_spec=pltpu.PrefetchScalarGridSpec(
            num_scalar_prefetch=1, grid=(1,), in_specs=[half_spec], out_specs=place_of(0)
        ),
        out_shape=outs,
        compiler_params=params("arbitrary"),
        cost_estimate=cost(2.5),
        name="widen_own",
    )(core, own_half)
    written = pl.pallas_call(
        functools.partial(widen_other_kernel, scale=edge_scale),
        grid_spec=pltpu.PrefetchScalarGridSpec(
            num_scalar_prefetch=1,
            grid=(1,),
            in_specs=[half_spec] + [pl.BlockSpec(memory_space=pl.ANY)] * 3,
            out_specs=place_of(1),
        ),
        out_shape=outs,
        input_output_aliases={2: 0, 3: 1, 4: 2},
        compiler_params=params("arbitrary"),
        cost_estimate=cost(2.5),
        name="widen_other",
    )(core, other_half, *in_far(*written))
    grad_coarse, grad_edge_in, grad_edge_out = (a.reshape(-1, lat) for a in written)

    grad_nodes = (
        grad_n
        + node_part
        + up_node_part
        + lax.dot_general(hot_send, returned, (((0,), (0,)), ((), ())), preferred_element_type=F32)
    )
    grad_node_in = node_total[: 2 * lat].astype(F32) * node_scale
    grad_node_out = node_total[2 * lat : 2 * lat + width].astype(F32) * node_scale
    return (
        grad_nodes,
        grad_coarse,
        grad_e,
        grad_u,
        grad_edge_in,
        grad_edge_out,
        gains[0] * edge_scale,
        grad_node_in,
        grad_node_out,
        gains[1] * node_scale,
    )


def split_mesh(mesh):
    face, band = mesh.shape["face"], mesh.shape["band"]
    z = 1
    while z * z < face or face % z:
        z += 1
    core = 2 if band % 2 == 0 else 1
    return Mesh(
        mesh.devices.reshape(z, face // z, band // core, core), ("z", "x", "y", "core")
    )


def solution(mesh):
    rows, split = P(EVERYONE, None), P(EVERYONE)
    return jax.shard_map(
        per_device,
        mesh=split_mesh(mesh),
        in_specs=(
            rows, P(), rows, rows, P(), P(), P(), P(), P(), P(), rows, P(), rows, rows,
            P(EVERYONE, None, None), split, split, split, split,
        ),
        out_specs=(rows, P(), rows, rows, P(), P(), P(), P(), P(), P()),
        check_vma=False,
    )
```

```python
import functools
import math

import jax
import jax.numpy as jnp
from jax import lax
from jax.experimental import pallas as pl
from jax.experimental.pallas import tpu as pltpu
from jax.sharding import Mesh, PartitionSpec as P

EPSILON = 1e-05
BF = jnp.bfloat16
F32 = jnp.float32
TAIL = 16
EVERYONE = ("z", "x", "y", "core")
VMEM_LIMIT = 24 * 1024 * 1024
BIG_VMEM_LIMIT = 50 * 1024 * 1024


def dot(a, b):
    return lax.dot_general(a, b, (((1,), (0,)), ((), ())), preferred_element_type=F32)


def dot_lt(a, b):
    return lax.dot_general(a, b, (((0,), (0,)), ((), ())), preferred_element_type=F32)


def dot_rt(a, b):
    return lax.dot_general(a, b, (((1,), (1,)), ((), ())), preferred_element_type=F32)


def onehot_t(index_row, rows, offset=0):
    ids = lax.broadcasted_iota(jnp.int32, (rows, index_row.shape[1]), 0) + offset
    return jnp.where(ids == index_row, 1.0, 0.0).astype(BF)


def hidden_of(pre):
    return (pre * jax.nn.sigmoid(pre)).astype(BF)


def normalise(projected):
    center = projected - jnp.mean(projected, axis=1, keepdims=True)
    inv_std = lax.rsqrt(jnp.mean(center * center, axis=1, keepdims=True) + EPSILON)
    return center * inv_std, inv_std


def grad_to_pre(pre, normed, inv_std, cot, gain, w2):
    gain_part = jnp.sum(cot * normed, axis=0, keepdims=True)
    scaled = cot * gain
    d_proj = (
        inv_std
        * (
            scaled
            - jnp.mean(scaled, axis=1, keepdims=True)
            - normed * jnp.mean(scaled * normed, axis=1, keepdims=True)
        )
    ).astype(BF)
    d_hidden = dot_rt(d_proj, w2)
    logistic = jax.nn.sigmoid(pre)
    d_pre = (d_hidden * logistic * (1.0 + pre * (1.0 - logistic))).astype(BF)
    return gain_part, d_proj, d_pre


def gather_f32(onehot, table):
    high = table.astype(BF)
    low = (table - high.astype(F32)).astype(BF)
    return dot_lt(onehot, high) + dot_lt(onehot, low)


def split_rows(ref, bit, keep_ref, send_ref):
    half = keep_ref.shape[0]
    keep_ref[...] = ref[pl.ds(pl.multiple_of(bit * half, 16), half), :].astype(BF)
    send_ref[...] = ref[pl.ds(pl.multiple_of((1 - bit) * half, 16), half), :].astype(BF)


def fold_split_kernel(bit, keep, recv, keep_ref, send_ref):
    half = keep_ref.shape[0]
    for side, out_ref in ((bit[0], keep_ref), (1 - bit[0], send_ref)):
        rows = pl.ds(pl.multiple_of(side * half, 16), half)
        out_ref[...] = (keep[rows, :].astype(F32) + recv[rows, :].astype(F32)).astype(BF)


def fold_pair_kernel(keep, recv, out_ref):
    count, rows, _ = out_ref.shape
    rows -= TAIL
    tail = (keep[count * rows :].astype(F32) + recv[count * rows :].astype(F32)).astype(BF)
    for k in range(count):
        piece = slice(k * rows, (k + 1) * rows)
        out_ref[k, 0:rows] = (keep[piece].astype(F32) + recv[piece].astype(F32)).astype(BF)
        out_ref[k, rows:] = tail


def fold_group_kernel(got, out_ref):
    group = got.shape[0]
    count, rows, _ = out_ref.shape
    rows -= TAIL

    def total(at, size):
        piece = slice(at, at + size)
        acc = got[0, piece].astype(F32)
        for k in range(1, group):
            acc += got[k, piece].astype(F32)
        return acc.astype(BF)

    tail = total(count * rows, TAIL)
    for k in range(count):
        out_ref[k, 0:rows] = total(k * rows, rows)
        out_ref[k, rows:] = tail


def up_forward_kernel(
    us, ur, core, up, gain, node_far, coarse_far, w1_far, w2_far,
    p_ref, xs_ref, xr_ref, keep_ref, send_ref, part, node, coarse, w1, w2, sems,
):
    loads = loads_of((node_far, coarse_far, w1_far, w2_far), (node, coarse, w1, w2), sems)
    for load in loads:
        load.start()
    lat = up.shape[1]
    hot_s = onehot_t(us[...], node.shape[0])
    hot_r = onehot_t(ur[...], coarse.shape[0])
    loads[0].wait()
    xs = dot_lt(hot_s, node[...]).astype(BF)
    loads[1].wait()
    xr = dot_lt(hot_r, coarse[...]).astype(BF)
    loads[2].wait()
    pre = dot(up[...], w1[0:lat]) + dot(xs, w1[lat : 2 * lat]) + dot(xr, w1[2 * lat :])
    loads[3].wait()
    normed, _ = normalise(dot(hidden_of(pre), w2[...]))
    new = (up[...].astype(F32) + normed * gain[...]).astype(BF)
    p_ref[...] = pre
    xs_ref[...] = xs
    xr_ref[...] = xr
    part[...] = dot(hot_r, new)
    split_rows(part, core[0], keep_ref, send_ref)


def store_out(staging, target, sem):
    copy = pltpu.make_async_copy(staging, target, sem)
    copy.start()
    return copy


def edge_forward_kernel(
    es, er, halo, gain, w1_far, edge_far, node_far, coarse_far, w2_far,
    p_far, xs_far, total_ref, w1, edge, node, coarse, w2, pre_out, xs_out, sems, out_sems,
):
    lat = edge.shape[1]
    n = node.shape[0]
    imports = halo.shape[0]
    first, last, middle = (
        pltpu.make_async_copy(
            w1_far.at[k * lat : (k + 1) * lat], w1.at[k * lat : (k + 1) * lat], sems.at[5 + k]
        )
        for k in (0, 2, 1)
    )
    edge_load, node_load, coarse_load, w2_load = loads_of(
        (edge_far, node_far, coarse_far, w2_far), (edge, node, coarse, w2), sems
    )
    for load in (node_load, last, edge_load, first, coarse_load, middle, w2_load):
        load.start()
    sender = es[...]
    hot_r = onehot_t(er[...], n)
    hot_n = onehot_t(sender, n)
    node_load.wait()
    xr = dot_lt(hot_r, node[...]).astype(BF)
    xs = dot_lt(hot_n, node[...]) + dot_lt(onehot_t(sender, imports, n), halo[...])
    last.wait()
    pre = dot(xr, w1[2 * lat :])
    edge_load.wait()
    first.wait()
    pre += dot(edge[...], w1[0:lat])
    hot_c = onehot_t(sender, coarse.shape[0], n + imports)
    coarse_load.wait()
    xs = (xs + dot_lt(hot_c, coarse[...])).astype(BF)
    xs_out[...] = xs
    outs = [store_out(xs_out, xs_far, out_sems.at[0])]
    middle.wait()
    pre += dot(xs, w1[lat : 2 * lat])
    pre_out[...] = pre
    outs.append(store_out(pre_out, p_far, out_sems.at[1]))
    hidden = hidden_of(pre)
    w2_load.wait()
    normed, _ = normalise(dot(hidden, w2[...]))
    new = (edge[...].astype(F32) + normed * gain[...]).astype(BF)
    total_ref[...] = dot(hot_r, new).astype(BF)
    for out in outs:
        out.wait()


def node_kernel(
    node, total_in, ngain, ncot, nw1_far, nw2_far, fg_ref, gn_ref, ngw1_ref, ngw2_ref, ngg_ref,
    nw1, nw2, sems,
):
    loads = loads_of((nw1_far, nw2_far), (nw1, nw2), sems)
    for load in loads:
        load.start()
    lat = node.shape[1]
    total = total_in[...]
    loads[0].wait()
    node_pre = dot(node[...], nw1[0:lat]) + dot(total, nw1[lat:])
    hidden = hidden_of(node_pre)
    loads[1].wait()
    node_normed, inv_std = normalise(dot(hidden, nw2[...]))
    cot = ncot[...].astype(F32)
    gain_part, d_proj, d_pre = grad_to_pre(
        node_pre, node_normed, inv_std, cot, ngain[...], nw2[...]
    )
    ngg_ref[...] = gain_part
    ngw2_ref[...] = dot_lt(hidden, d_proj).astype(BF)
    ngw1_ref[0:lat] = dot_lt(node[...], d_pre).astype(BF)
    ngw1_ref[lat:] = dot_lt(total, d_pre).astype(BF)
    gn_ref[...] = cot + dot_rt(d_pre, nw1[0:lat])
    fg_ref[...] = dot_rt(d_pre, nw1[lat:])


def edge_backward_kernel(
    es, er, gain, pre_far, w2_far, ecot_far, fg_far, w1_far, edge_far, xs_far, node_far,
    gg_ref, ret_ref, ge_far, gw1_far, gw2_far, np_far, cp_far,
    pre, w2, ecot, fg, w1, edge, xs, node, sems, ge, gw1, gw2, np_out, cp, out_sems,
):
    lat = edge.shape[1]
    n = node.shape[0]
    imports = ret_ref.shape[0]
    loads = loads_of(
        (pre_far, w2_far, ecot_far, fg_far, w1_far, edge_far, xs_far, node_far),
        (pre, w2, ecot, fg, w1, edge, xs, node),
        sems,
    )
    for load in loads:
        load.start()
    hot_r = onehot_t(er[...], n)
    loads[0].wait()
    hidden = hidden_of(pre[...])
    loads[1].wait()
    normed, inv_std = normalise(dot(hidden, w2[...]))
    loads[2].wait()
    loads[3].wait()
    cot = ecot[...].astype(F32) + gather_f32(hot_r, fg[...])
    gain_part, d_proj, d_pre = grad_to_pre(pre[...], normed, inv_std, cot, gain[...], w2[...])
    gg_ref[...] = gain_part
    loads[4].wait()
    ge[...] = cot + dot_rt(d_pre, w1[0:lat])
    outs = [store_out(ge, ge_far, out_sems.at[0])]
    loads[5].wait()
    gw1[0:lat] = dot_lt(edge[...], d_pre).astype(BF)
    loads[6].wait()
    gw1[lat : 2 * lat] = dot_lt(xs[...], d_pre).astype(BF)
    recv = dot(hot_r, d_pre).astype(BF)
    loads[7].wait()
    gw1[2 * lat :] = dot_lt(node[...], recv).astype(BF)
    outs.append(store_out(gw1, gw1_far, out_sems.at[1]))
    gw2[...] = dot_lt(hidden, d_proj).astype(BF)
    outs.append(store_out(gw2, gw2_far, out_sems.at[2]))
    w_s = w1[lat : 2 * lat]
    sender = es[...]
    count = cp.shape[0]
    sums = dot(onehot_t(sender, count, n + imports), d_pre).astype(BF)
    cp[...] = dot_rt(sums, w_s).astype(BF)
    outs.append(store_out(cp, cp_far, out_sems.at[3]))
    sums = dot(onehot_t(sender, n), d_pre).astype(BF)
    np_out[...] = dot_rt(sums, w_s) + dot_rt(recv, w1[2 * lat :])
    outs.append(store_out(np_out, np_far, out_sems.at[4]))
    sums = dot(onehot_t(sender, imports, n), d_pre).astype(BF)
    ret_ref[...] = dot_rt(sums, w_s).astype(BF)
    for out in outs:
        out.wait()


def coarse_kernel(
    core, rows, total_in, ccot, ngain, ngg, nw1_far, nw2_far, ngw1_far, ngw2_far,
    cg_ref, after_ref, keep_ref, send_ref, gg_ref, pay, nw1, nw2, ngw1, ngw2, sems,
):
    loads = loads_of(
        (nw1_far, nw2_far, ngw1_far, ngw2_far), (nw1, nw2, ngw1, ngw2), sems
    )
    for load in loads:
        load.start()
    lat = rows.shape[1]
    used = ngw1.shape[0] + ngw2.shape[0]
    total = total_in[...].astype(BF)
    loads[0].wait()
    pre = dot(rows[...], nw1[0:lat]) + dot(total, nw1[lat:])
    hidden = hidden_of(pre)
    loads[1].wait()
    normed, inv_std = normalise(dot(hidden, nw2[...]))
    cot = ccot[...].astype(F32)
    gain_part, d_proj, d_pre = grad_to_pre(pre, normed, inv_std, cot, ngain[...], nw2[...])
    cg_ref[...] = dot_rt(d_pre, nw1[lat:]).astype(BF)
    after_ref[...] = cot + dot_rt(d_pre, nw1[0:lat])
    loads[2].wait()
    loads[3].wait()
    pay[0:lat] = ngw1[0:lat].astype(F32) + dot_lt(rows[...], d_pre)
    pay[lat : 2 * lat] = ngw1[lat:].astype(F32) + dot_lt(total, d_pre)
    pay[2 * lat : used] = ngw2[...].astype(F32) + dot_lt(hidden, d_proj)
    if used < pay.shape[0]:
        pay[used:] = jnp.zeros((pay.shape[0] - used, lat), F32)
    split_rows(pay, core[0], keep_ref, send_ref)
    gg_ref[...] = ngg[...] + gain_part


def up_backward_kernel(
    us, ur, place, up, xs, xr, pre_ref, ucot, cg_own, cg_other, gain, gg, ngg, after,
    w2_far, w1_far, cp_far, gw2_far, gw1_far, gu_ref, np_ref, keep_far, send_far,
    csum, pay, w2, w1, cp, gw2, gw1, sems, out_sems,
):
    loads = loads_of(
        (w2_far, w1_far, cp_far, gw2_far, gw1_far), (w2, w1, cp, gw2, gw1), sems
    )
    for load in loads:
        load.start()
    lat = up.shape[1]
    half = cg_own.shape[0]
    coarse = csum.shape[0]
    core = place[1]
    hot_r = onehot_t(ur[...], coarse)
    turned = ur[...] - core * half
    turned = jnp.where(turned < 0, turned + coarse, turned)
    cot = (
        ucot[...].astype(F32)
        + dot_lt(onehot_t(turned, half), cg_own[...])
        + dot_lt(onehot_t(turned, half, half), cg_other[...])
    )
    pre = pre_ref[...]
    hidden = hidden_of(pre)
    loads[0].wait()
    normed, inv_std = normalise(dot(hidden, w2[...]))
    gain_part, d_proj, d_pre = grad_to_pre(pre, normed, inv_std, cot, gain[...], w2[...])
    loads[1].wait()
    gu_ref[...] = cot + dot_rt(d_pre, w1[0:lat])
    send = dot(onehot_t(us[...], np_ref.shape[0]), d_pre).astype(BF)
    np_ref[...] = dot_rt(send, w1[lat : 2 * lat])
    loads[2].wait()
    csum[...] = cp[...].astype(F32) + dot_rt(dot(hot_r, d_pre).astype(BF), w1[2 * lat :])
    count = after.shape[0]
    mine = pl.ds(pl.multiple_of(place[0] * count, 8), count)
    csum[mine, :] = csum[mine, :] + after[...]
    rows = pay.shape[0] // 2 - TAIL
    c_half, h_half, w_half = coarse // 2, gw1.shape[0] // 2, gw2.shape[0] // 2

    def send_piece(start, size):
        for h in range(2):
            src = pay.at[pl.ds(h * (rows + TAIL) + start, size)]

            @pl.when(core == h)
            def _():
                pltpu.make_async_copy(
                    src, keep_far.at[pl.ds(start, size)], out_sems.at[0]
                ).start()

            @pl.when(core != h)
            def _():
                pltpu.make_async_copy(
                    src, send_far.at[pl.ds(start, size)], out_sems.at[1]
                ).start()

    def put(start, size, full):
        for h in range(2):
            at = h * (rows + TAIL) + start
            pay[at : at + size] = full[h * size : (h + 1) * size].astype(BF)

    put(0, c_half, csum)
    send_piece(0, c_half)
    loads[3].wait()
    put(c_half + h_half, w_half, gw2[...].astype(F32) + dot_lt(hidden, d_proj))
    send_piece(c_half + h_half, w_half)
    loads[4].wait()
    w1_part = jnp.concatenate(
        [
            gw1[k * lat : (k + 1) * lat].astype(F32) + dot_lt(x[...], d_pre)
            for k, x in enumerate((up, xs, xr))
        ],
        axis=0,
    )
    put(c_half, h_half, w1_part)
    send_piece(c_half, h_half)
    used = c_half + h_half + w_half
    ids = lax.broadcasted_iota(jnp.int32, (TAIL, lat), 0)
    edge_row = jnp.broadcast_to(gg[...] + gain_part, (TAIL, lat))
    node_row = jnp.broadcast_to(ngg[...], (TAIL, lat))
    tail = jnp.where(ids == 0, edge_row, jnp.where(ids == 1, node_row, 0.0)).astype(BF)
    for h in range(2):
        at = h * (rows + TAIL)
        if used < rows:
            pay[at + used : at + rows] = jnp.zeros((rows - used, lat), BF)
        pay[at + rows : at + rows + TAIL] = tail
    send_piece(used, rows + TAIL - used)
    for k, out_far in enumerate((keep_far, send_far)):
        pltpu.make_async_copy(pay.at[pl.ds(0, rows + TAIL)], out_far, out_sems.at[k]).wait()


def widen_kernel(core, half, coarse_ref, first_ref, second_ref, *, scale):
    start = 0
    for out_ref, factor in ((coarse_ref, None), (first_ref, scale), (second_ref, scale)):
        rows = out_ref.shape[1]
        values = half[start : start + rows].astype(F32)
        out_ref[0] = values if factor is None else values * factor
        start += rows


def widen_other_kernel(core, half, c_in, f_in, s_in, coarse_ref, first_ref, second_ref, *, scale):
    widen_kernel(core, half, coarse_ref, first_ref, second_ref, scale=scale)


def params(*semantics, limit=VMEM_LIMIT):
    return pltpu.CompilerParams(dimension_semantics=semantics or None, vmem_limit_bytes=limit)


def cost(micros):
    return pl.CostEstimate(
        flops=int(micros * 1.1e9), transcendentals=0, bytes_accessed=int(micros * 3.0e6)
    )


def shape(rows, cols, dtype):
    return jax.ShapeDtypeStruct((rows, cols), dtype)


def far(rows, cols, dtype):
    return pltpu.HBM((rows, cols), dtype)


def in_far(*arrays):
    return [pltpu.with_memory_space_constraint(a, pltpu.HBM) for a in arrays]


IN_VMEM = pl.BlockSpec(memory_space=pltpu.VMEM)
IN_SMEM = pl.BlockSpec(memory_space=pltpu.SMEM)
IN_HBM = pl.BlockSpec(memory_space=pl.ANY)


def loads_of(sources, targets, sems):
    return [
        pltpu.make_async_copy(src, dst, sems.at[k])
        for k, (src, dst) in enumerate(zip(sources, targets))
    ]


def buffers(*arrays):
    return [pltpu.VMEM(a.shape, a.dtype) for a in arrays] + [
        pltpu.SemaphoreType.DMA((len(arrays),))
    ]


def swap(x, axes, count):
    if count == 1:
        return x
    return lax.all_to_all(x, axes, 0, 0, tiled=True)


GROUPS = ("core", ("x", "y"), "z")


def owner_index():
    index = jnp.int32(0)
    for axes in GROUPS:
        index = index * lax.axis_size(axes) + lax.axis_index(axes)
    return index


def exchange(x, mask):
    devices = lax.axis_size(EVERYONE)
    if devices == 1:
        return x
    return lax.ppermute(x, EVERYONE, [(i, i ^ mask) for i in range(devices)])


def sum_group(got, count):
    return jnp.sum(got.reshape(count, -1, got.shape[1]).astype(F32), axis=0)


def copies(x, count):
    return jnp.broadcast_to(x[None], (count,) + x.shape).reshape(-1, x.shape[1])


def reduce_rows(keep, send):
    x = keep.astype(F32) + exchange(send, 1).astype(F32)
    for axes in GROUPS[1:]:
        count = lax.axis_size(axes)
        x = sum_group(swap(x.astype(BF), axes, count), count)
    return x


def gather_halves(x):
    for axes in reversed(GROUPS[1:]):
        count = lax.axis_size(axes)
        x = swap(copies(x, count), axes, count)
    return x, exchange(x, 1)


def reduce_with_tail(keep, send, wait_for):
    cols = keep.shape[1]
    rows = keep.shape[0] - TAIL
    got = exchange(send, 1)
    got, wait_for = lax.optimization_barrier((got, wait_for))
    x = (*in_far(keep), got)
    for axes, kernel in zip(GROUPS[1:], (fold_pair_kernel, fold_group_kernel)):
        count = lax.axis_size(axes)
        part = rows // count
        x = pl.pallas_call(
            kernel,
            out_shape=pltpu.HBM((count, part + TAIL, cols), BF),
            compiler_params=params(),
            cost_estimate=cost(3.0),
        )(*x)
        x = (swap(x.reshape(-1, cols), axes, count).reshape(x.shape),)
        rows = part
    x = jnp.sum(x[0].astype(F32), axis=0)
    return x[:rows].astype(BF), x[rows:], wait_for


def bit_masks(devices):
    slow = devices // lax.axis_size("z")
    order = [1 << b for b in range(1, devices.bit_length() - 1)]
    return (
        [m for m in order if m == slow]
        + [m for m in reversed(order) if m < slow]
        + [m for m in order if m > slow]
    )


def halving_sum(keep, send):
    devices = lax.axis_size(EVERYONE)
    masks = [1] + bit_masks(devices)
    place = lax.axis_index(EVERYONE)
    for mask, after in zip(masks, masks[1:]):
        rows, cols = keep.shape
        bit = ((place & after) > 0).astype(jnp.int32).reshape(1)
        got = exchange(send, mask)
        keep, send = pl.pallas_call(
            fold_split_kernel,
            in_specs=[pl.BlockSpec(memory_space=pltpu.SMEM)]
            + [pl.BlockSpec(memory_space=pltpu.VMEM)] * 2,
            out_shape=(far(rows // 2, cols, BF), shape(rows // 2, cols, BF)),
            compiler_params=params(),
            cost_estimate=cost(1.0),
            name="fold_split",
        )(bit, *in_far(keep), got)
    got = exchange(send, masks[-1])
    x = (keep.astype(F32) + got.astype(F32)).astype(BF)
    for mask in reversed(masks):
        other = exchange(x, mask)
        x = jnp.where(
            (place & mask) > 0, jnp.concatenate([other, x], 0), jnp.concatenate([x, other], 0)
        )
    return x


def padded_rows(rows, devices):
    return -(-rows // (16 * devices)) * 16 * devices


def per_device(
    node, coarse, edge, up, w1, w2, gain, nw1, nw2, ngain, ncot, ccot, ecot, ucot,
    send_rows, edge_sender, edge_receiver, up_sender, up_receiver,
):
    n, lat = node.shape
    width = w2.shape[0]
    ccount = coarse.shape[0]
    ecount = edge.shape[0]
    ucount = up.shape[0]
    devices, slots = send_rows.shape[1], send_rows.shape[2]
    imports = devices * slots
    es, er = in_far(edge_sender.reshape(1, ecount), edge_receiver.reshape(1, ecount))
    us, ur = in_far(up_sender.reshape(1, ucount), up_receiver.reshape(1, ucount))
    gain_row, ngain_row = in_far(gain.reshape(1, lat), ngain.reshape(1, lat))
    own = owner_index()
    core = lax.axis_index("core").reshape(1)

    table = send_rows.reshape(imports)
    hot_send = (table[:, None] == jnp.arange(n, dtype=jnp.int32)[None, :]).astype(BF)
    outgoing = dot(hot_send, node).astype(BF)
    halo = lax.all_to_all(
        outgoing.reshape(devices, slots, lat), EVERYONE, 0, 0, tiled=True
    ).reshape(imports, lat)

    up_pre, up_xs, up_xr, keep, send = pl.pallas_call(
        up_forward_kernel,
        in_specs=[IN_VMEM] * 2 + [IN_SMEM] + [IN_VMEM] * 2 + [IN_HBM] * 4,
        out_shape=(
            far(ucount, width, F32), far(ucount, lat, BF), far(ucount, lat, BF),
            far(ccount // 2, lat, BF), shape(ccount // 2, lat, BF),
        ),
        scratch_shapes=[pltpu.VMEM((ccount, lat), F32)] + buffers(node, coarse, w1, w2),
        compiler_params=params(),
        cost_estimate=cost(5.0),
        name="up_forward",
    )(us, ur, core, *in_far(up), gain_row, *in_far(node, coarse, w1, w2))

    coarse_total = reduce_rows(keep, send)

    edge_args = (w1, edge, node, coarse, w2)
    staging = [far(ecount, width, F32), far(ecount, lat, BF)]
    pre, xs, fine_total = pl.pallas_call(
        edge_forward_kernel,
        in_specs=[IN_VMEM] * 4 + [IN_HBM] * 5,
        out_specs=[IN_HBM] * 2 + [IN_VMEM],
        out_shape=(*staging, far(n, lat, BF)),
        scratch_shapes=buffers(*edge_args, *staging)[:-1]
        + [pltpu.SemaphoreType.DMA((8,)), pltpu.SemaphoreType.DMA((2,))],
        compiler_params=params(limit=BIG_VMEM_LIMIT),
        cost_estimate=cost(9.0),
        name="edge_forward",
    )(es, er, halo, gain_row, *in_far(*edge_args))

    fine_grad, grad_n, ngw1, ngw2, ngg = pl.pallas_call(
        node_kernel,
        in_specs=[IN_VMEM] * 4 + [IN_HBM] * 2,
        scratch_shapes=buffers(nw1, nw2),
        out_shape=(
            far(n, lat, F32), far(n, lat, F32), far(2 * lat, width, BF),
            far(width, lat, BF), shape(1, lat, F32),
        ),
        compiler_params=params(),
        cost_estimate=cost(5.0),
        name="node_mlp",
    )(*in_far(node, fine_total), ngain_row, *in_far(ncot, nw1, nw2))

    edge_args = (pre, w2, ecot, fine_grad, w1, edge, xs, node)
    staging = [
        far(ecount, lat, F32), far(3 * lat, width, BF), far(width, lat, BF), far(n, lat, F32),
        far(ccount, lat, BF),
    ]
    gg, returning, grad_e, gw1, gw2, node_part, coarse_local = pl.pallas_call(
        edge_backward_kernel,
        in_specs=[IN_VMEM] * 3 + [IN_HBM] * 8,
        out_specs=[IN_VMEM] * 2 + [IN_HBM] * 5,
        out_shape=(shape(1, lat, F32), shape(imports, lat, BF), *staging),
        scratch_shapes=buffers(*edge_args) + buffers(*staging),
        compiler_params=params(limit=BIG_VMEM_LIMIT),
        cost_estimate=cost(15.0),
        name="edge_backward",
    )(es, er, gain_row, *in_far(*edge_args))

    returned = lax.all_to_all(
        returning.reshape(devices, slots, lat), EVERYONE, 0, 0, tiled=True
    ).reshape(imports, lat)

    mine = ccount // devices
    padded = -(-mine // 16) * 16
    pad = lambda a: jnp.pad(a, ((0, padded - mine), (0, 0))) if padded > mine else a
    own_coarse = pad(lax.dynamic_slice_in_dim(coarse, own * mine, mine, 0))
    own_cot = pad(lax.dynamic_slice_in_dim(ccot, own * mine, mine, 0))
    node_rows = padded_rows(2 * lat + width, devices)
    coarse_grad, coarse_after, node_keep, node_send, ngg_sum = pl.pallas_call(
        coarse_kernel,
        in_specs=[IN_SMEM] + [IN_VMEM] * 5 + [IN_HBM] * 4,
        out_shape=(
            shape(padded, lat, BF), far(padded, lat, F32), far(node_rows // 2, lat, BF),
            shape(node_rows // 2, lat, BF), shape(1, lat, F32),
        ),
        scratch_shapes=[pltpu.VMEM((node_rows, lat), F32)] + buffers(nw1, nw2, ngw1, ngw2),
        compiler_params=params(),
        cost_estimate=cost(5.0),
        name="coarse_mlp",
    )(
        core, own_coarse, pad(coarse_total), own_cot, ngain_row, ngg,
        *in_far(nw1, nw2, ngw1, ngw2),
    )
    cg_own, cg_other = gather_halves(coarse_grad[:mine])

    node_total = halving_sum(node_keep, node_send)

    edge_rows = padded_rows(ccount + 3 * lat + width, devices)
    grad_u, up_node_part, keep, send = pl.pallas_call(
        up_backward_kernel,
        in_specs=[IN_VMEM] * 2 + [IN_SMEM] + [IN_VMEM] * 11 + [IN_HBM] * 5,
        out_specs=[IN_VMEM] * 2 + [IN_HBM] * 2,
        out_shape=(
            far(ucount, lat, F32), far(n, lat, F32), far(edge_rows // 2 + TAIL, lat, BF),
            far(edge_rows // 2 + TAIL, lat, BF),
        ),
        scratch_shapes=[
            pltpu.VMEM((ccount, lat), F32), pltpu.VMEM((edge_rows + 2 * TAIL, lat), BF),
        ]
        + buffers(w2, w1, coarse_local, gw2, gw1)
        + [pltpu.SemaphoreType.DMA((2,))],
        compiler_params=params(),
        cost_estimate=cost(8.0),
        name="up_backward",
    )(
        us, ur, jnp.stack([own, core[0]]), *in_far(up, up_xs, up_xr, up_pre, ucot), cg_own,
        cg_other, gain_row, gg, ngg_sum, *in_far(coarse_after[:mine]),
        *in_far(w2, w1, coarse_local, gw2, gw1),
    )
    block, gains, returned = reduce_with_tail(keep, send, returned)
    own_half, other_half = gather_halves(block)
    edge_scale = 1.0 / math.sqrt((ecount + ucount) * devices)
    node_scale = 1.0 / math.sqrt(n * devices + ccount)
    halves = [ccount // 2, 3 * lat // 2, width // 2]
    outs = tuple(pltpu.HBM((2, rows, lat), F32) for rows in halves)

    def place_of(flip):
        return [
            pl.BlockSpec((1, rows, lat), lambda i, c: (c[0] ^ flip, 0, 0)) for rows in halves
        ]

    half_spec = pl.BlockSpec(own_half.shape, lambda i, c: (0, 0))
    written = pl.pallas_call(
        functools.partial(widen_kernel, scale=edge_scale),
        grid_spec=pltpu.PrefetchScalarGridSpec(
            num_scalar_prefetch=1, grid=(1,), in_specs=[half_spec], out_specs=place_of(0)
        ),
        out_shape=outs,
        compiler_params=params("arbitrary"),
        cost_estimate=cost(2.5),
        name="widen_own",
    )(core, own_half)
    written = pl.pallas_call(
        functools.partial(widen_other_kernel, scale=edge_scale),
        grid_spec=pltpu.PrefetchScalarGridSpec(
            num_scalar_prefetch=1,
            grid=(1,),
            in_specs=[half_spec] + [pl.BlockSpec(memory_space=pl.ANY)] * 3,
            out_specs=place_of(1),
        ),
        out_shape=outs,
        input_output_aliases={2: 0, 3: 1, 4: 2},
        compiler_params=params("arbitrary"),
        cost_estimate=cost(2.5),
        name="widen_other",
    )(core, other_half, *in_far(*written))
    grad_coarse, grad_edge_in, grad_edge_out = (a.reshape(-1, lat) for a in written)

    grad_nodes = (
        grad_n
        + node_part
        + up_node_part
        + lax.dot_general(hot_send, returned, (((0,), (0,)), ((), ())), preferred_element_type=F32)
    )
    grad_node_in = node_total[: 2 * lat].astype(F32) * node_scale
    grad_node_out = node_total[2 * lat : 2 * lat + width].astype(F32) * node_scale
    return (
        grad_nodes,
        grad_coarse,
        grad_e,
        grad_u,
        grad_edge_in,
        grad_edge_out,
        gains[0] * edge_scale,
        grad_node_in,
        grad_node_out,
        gains[1] * node_scale,
    )


def split_mesh(mesh):
    face, band = mesh.shape["face"], mesh.shape["band"]
    z = 1
    while z * z < face or face % z:
        z += 1
    core = 2 if band % 2 == 0 else 1
    return Mesh(
        mesh.devices.reshape(z, face // z, band // core, core), ("z", "x", "y", "core")
    )


def solution(mesh):
    rows, split = P(EVERYONE, None), P(EVERYONE)
    return jax.shard_map(
        per_device,
        mesh=split_mesh(mesh),
        in_specs=(
            rows, P(), rows, rows, P(), P(), P(), P(), P(), P(), rows, P(), rows, rows,
            P(EVERYONE, None, None), split, split, split, split,
        ),
        out_specs=(rows, P(), rows, rows, P(), P(), P(), P(), P(), P()),
        check_vma=False,
    )
```

```python
import functools
import math

import jax
import jax.numpy as jnp
from jax import lax
from jax.experimental import pallas as pl
from jax.experimental.pallas import tpu as pltpu
from jax.sharding import Mesh, PartitionSpec as P

EPSILON = 1e-05
BF = jnp.bfloat16
F32 = jnp.float32
TAIL = 16
EVERYONE = ("z", "x", "y", "core")
VMEM_LIMIT = 24 * 1024 * 1024
BIG_VMEM_LIMIT = 50 * 1024 * 1024


def dot(a, b):
    return lax.dot_general(a, b, (((1,), (0,)), ((), ())), preferred_element_type=F32)


def dot_lt(a, b):
    return lax.dot_general(a, b, (((0,), (0,)), ((), ())), preferred_element_type=F32)


def dot_rt(a, b):
    return lax.dot_general(a, b, (((1,), (1,)), ((), ())), preferred_element_type=F32)


def onehot_t(index_row, rows, offset=0):
    ids = lax.broadcasted_iota(jnp.int32, (rows, index_row.shape[1]), 0) + offset
    return jnp.where(ids == index_row, 1.0, 0.0).astype(BF)


def hidden_of(pre):
    return (pre * jax.nn.sigmoid(pre)).astype(BF)


def normalise(projected):
    center = projected - jnp.mean(projected, axis=1, keepdims=True)
    inv_std = lax.rsqrt(jnp.mean(center * center, axis=1, keepdims=True) + EPSILON)
    return center * inv_std, inv_std


def grad_to_pre(pre, normed, inv_std, cot, gain, w2):
    gain_part = jnp.sum(cot * normed, axis=0, keepdims=True)
    scaled = cot * gain
    d_proj = (
        inv_std
        * (
            scaled
            - jnp.mean(scaled, axis=1, keepdims=True)
            - normed * jnp.mean(scaled * normed, axis=1, keepdims=True)
        )
    ).astype(BF)
    d_hidden = dot_rt(d_proj, w2)
    logistic = jax.nn.sigmoid(pre)
    d_pre = (d_hidden * logistic * (1.0 + pre * (1.0 - logistic))).astype(BF)
    return gain_part, d_proj, d_pre


def gather_f32(onehot, table):
    high = table.astype(BF)
    low = (table - high.astype(F32)).astype(BF)
    return dot_lt(onehot, high) + dot_lt(onehot, low)


def split_rows(ref, bit, keep_ref, send_ref):
    half = keep_ref.shape[0]
    keep_ref[...] = ref[pl.ds(pl.multiple_of(bit * half, 16), half), :].astype(BF)
    send_ref[...] = ref[pl.ds(pl.multiple_of((1 - bit) * half, 16), half), :].astype(BF)


def fold_split_kernel(bit, keep, recv, keep_ref, send_ref):
    half = keep_ref.shape[0]
    for side, out_ref in ((bit[0], keep_ref), (1 - bit[0], send_ref)):
        rows = pl.ds(pl.multiple_of(side * half, 16), half)
        out_ref[...] = (keep[rows, :].astype(F32) + recv[rows, :].astype(F32)).astype(BF)


def fold_pair_kernel(keep_far, recv, out_far, keep, out, sems, out_sems):
    count, rows, _ = out.shape
    rows -= TAIL
    spans = [(count * rows, TAIL)] + [(k * rows, rows) for k in range(count)]
    loads = [
        pltpu.make_async_copy(
            keep_far.at[pl.ds(at, size)], keep.at[pl.ds(at, size)], sems.at[k]
        )
        for k, (at, size) in enumerate(spans)
    ]
    for load in loads:
        load.start()
    sums = []
    outs = []
    for k, (at, size) in enumerate(spans):
        loads[k].wait()
        piece = slice(at, at + size)
        total = (keep[piece].astype(F32) + recv[piece].astype(F32)).astype(BF)
        if k == 0:
            sums.append(total)
            continue
        out[k - 1, 0:rows] = total
        out[k - 1, rows:] = sums[0]
        outs.append(store_out(out.at[k - 1], out_far.at[k - 1], out_sems.at[k - 1]))
    for copy in outs:
        copy.wait()


def fold_group_kernel(got, out_ref):
    group = got.shape[0]
    count, rows, _ = out_ref.shape
    rows -= TAIL

    def total(at, size):
        piece = slice(at, at + size)
        acc = got[0, piece].astype(F32)
        for k in range(1, group):
            acc += got[k, piece].astype(F32)
        return acc.astype(BF)

    tail = total(count * rows, TAIL)
    for k in range(count):
        out_ref[k, 0:rows] = total(k * rows, rows)
        out_ref[k, rows:] = tail


def up_forward_kernel(
    us, ur, core, up, gain, node_far, coarse_far, w1_far, w2_far,
    p_ref, xs_ref, xr_ref, keep_ref, send_ref, part, node, coarse, w1, w2, sems,
):
    loads = loads_of((node_far, coarse_far, w1_far, w2_far), (node, coarse, w1, w2), sems)
    for load in loads:
        load.start()
    lat = up.shape[1]
    hot_s = onehot_t(us[...], node.shape[0])
    hot_r = onehot_t(ur[...], coarse.shape[0])
    loads[0].wait()
    xs = dot_lt(hot_s, node[...]).astype(BF)
    loads[1].wait()
    xr = dot_lt(hot_r, coarse[...]).astype(BF)
    loads[2].wait()
    pre = dot(up[...], w1[0:lat]) + dot(xs, w1[lat : 2 * lat]) + dot(xr, w1[2 * lat :])
    loads[3].wait()
    normed, _ = normalise(dot(hidden_of(pre), w2[...]))
    new = (up[...].astype(F32) + normed * gain[...]).astype(BF)
    p_ref[...] = pre
    xs_ref[...] = xs
    xr_ref[...] = xr
    part[...] = dot(hot_r, new)
    split_rows(part, core[0], keep_ref, send_ref)


def store_out(staging, target, sem):
    copy = pltpu.make_async_copy(staging, target, sem)
    copy.start()
    return copy


def edge_forward_kernel(
    es, er, halo, gain, w1_far, edge_far, node_far, coarse_far, w2_far,
    p_far, xs_far, total_ref, w1, edge, node, coarse, w2, pre_out, xs_out, sems, out_sems,
):
    lat = edge.shape[1]
    n = node.shape[0]
    imports = halo.shape[0]
    first, last, middle = (
        pltpu.make_async_copy(
            w1_far.at[k * lat : (k + 1) * lat], w1.at[k * lat : (k + 1) * lat], sems.at[5 + k]
        )
        for k in (0, 2, 1)
    )
    edge_load, node_load, coarse_load, w2_load = loads_of(
        (edge_far, node_far, coarse_far, w2_far), (edge, node, coarse, w2), sems
    )
    for load in (node_load, last, edge_load, first, coarse_load, middle, w2_load):
        load.start()
    sender = es[...]
    hot_r = onehot_t(er[...], n)
    hot_n = onehot_t(sender, n)
    node_load.wait()
    xr = dot_lt(hot_r, node[...]).astype(BF)
    xs = dot_lt(hot_n, node[...]) + dot_lt(onehot_t(sender, imports, n), halo[...])
    last.wait()
    pre = dot(xr, w1[2 * lat :])
    edge_load.wait()
    first.wait()
    pre += dot(edge[...], w1[0:lat])
    hot_c = onehot_t(sender, coarse.shape[0], n + imports)
    coarse_load.wait()
    xs = (xs + dot_lt(hot_c, coarse[...])).astype(BF)
    xs_out[...] = xs
    outs = [store_out(xs_out, xs_far, out_sems.at[0])]
    middle.wait()
    pre += dot(xs, w1[lat : 2 * lat])
    pre_out[...] = pre
    outs.append(store_out(pre_out, p_far, out_sems.at[1]))
    hidden = hidden_of(pre)
    w2_load.wait()
    normed, _ = normalise(dot(hidden, w2[...]))
    new = (edge[...].astype(F32) + normed * gain[...]).astype(BF)
    total_ref[...] = dot(hot_r, new).astype(BF)
    for out in outs:
        out.wait()


def node_kernel(
    ngain, node_far, total_far, nw1_far, nw2_far, ncot_far,
    ngg_ref, dp_far, fg_far, gn_far, hidden_far, dy_far,
    node, total, nw1, nw2, ncot, sems, dp, fg, gn, hidden_out, dy, out_sems,
):
    loads = loads_of(
        (node_far, total_far, nw1_far, nw2_far, ncot_far), (node, total, nw1, nw2, ncot), sems
    )
    for load in loads:
        load.start()
    lat = node.shape[1]
    for load in loads[:3]:
        load.wait()
    pre = dot(node[...], nw1[0:lat]) + dot(total[...], nw1[lat:])
    hidden = hidden_of(pre)
    hidden_out[...] = hidden
    outs = [store_out(hidden_out, hidden_far, out_sems.at[0])]
    loads[3].wait()
    normed, inv_std = normalise(dot(hidden, nw2[...]))
    loads[4].wait()
    cot = ncot[...].astype(F32)
    gain_part, d_proj, d_pre = grad_to_pre(pre, normed, inv_std, cot, ngain[...], nw2[...])
    ngg_ref[...] = gain_part
    dy[...] = d_proj
    outs.append(store_out(dy, dy_far, out_sems.at[1]))
    dp[...] = d_pre
    outs.append(store_out(dp, dp_far, out_sems.at[2]))
    fg[...] = dot_rt(d_pre, nw1[lat:])
    outs.append(store_out(fg, fg_far, out_sems.at[3]))
    gn[...] = cot + dot_rt(d_pre, nw1[0:lat])
    outs.append(store_out(gn, gn_far, out_sems.at[4]))
    for out in outs:
        out.wait()


def edge_backward_kernel(
    es, er, gain, pre_far, w2_far, ecot_far, fg_far, w1_far, edge_far, xs_far, node_far,
    gg_ref, ret_ref, ge_far, gw1_far, gw2_far, np_far, cp_far,
    pre, w2, ecot, fg, w1, edge, xs, node, sems, ge, gw1, gw2, np_out, cp, out_sems,
):
    lat = edge.shape[1]
    n = node.shape[0]
    imports = ret_ref.shape[0]
    loads = loads_of(
        (pre_far, w2_far, ecot_far, fg_far, w1_far, edge_far, xs_far, node_far),
        (pre, w2, ecot, fg, w1, edge, xs, node),
        sems,
    )
    for load in loads:
        load.start()
    hot_r = onehot_t(er[...], n)
    loads[0].wait()
    hidden = hidden_of(pre[...])
    loads[1].wait()
    normed, inv_std = normalise(dot(hidden, w2[...]))
    loads[2].wait()
    loads[3].wait()
    cot = ecot[...].astype(F32) + gather_f32(hot_r, fg[...])
    gain_part, d_proj, d_pre = grad_to_pre(pre[...], normed, inv_std, cot, gain[...], w2[...])
    gg_ref[...] = gain_part
    loads[4].wait()
    ge[...] = cot + dot_rt(d_pre, w1[0:lat])
    outs = [store_out(ge, ge_far, out_sems.at[0])]
    loads[5].wait()
    gw1[0:lat] = dot_lt(edge[...], d_pre).astype(BF)
    loads[6].wait()
    gw1[lat : 2 * lat] = dot_lt(xs[...], d_pre).astype(BF)
    recv = dot(hot_r, d_pre).astype(BF)
    loads[7].wait()
    gw1[2 * lat :] = dot_lt(node[...], recv).astype(BF)
    outs.append(store_out(gw1, gw1_far, out_sems.at[1]))
    gw2[...] = dot_lt(hidden, d_proj).astype(BF)
    outs.append(store_out(gw2, gw2_far, out_sems.at[2]))
    w_s = w1[lat : 2 * lat]
    sender = es[...]
    count = cp.shape[0]
    sums = dot(onehot_t(sender, count, n + imports), d_pre).astype(BF)
    cp[...] = dot_rt(sums, w_s).astype(BF)
    outs.append(store_out(cp, cp_far, out_sems.at[3]))
    sums = dot(onehot_t(sender, n), d_pre).astype(BF)
    np_out[...] = dot_rt(sums, w_s) + dot_rt(recv, w1[2 * lat :])
    outs.append(store_out(np_out, np_far, out_sems.at[4]))
    sums = dot(onehot_t(sender, imports, n), d_pre).astype(BF)
    ret_ref[...] = dot_rt(sums, w_s).astype(BF)
    for out in outs:
        out.wait()


def coarse_kernel(
    core, rows, total_in, ccot, ngain, ngg,
    nw1_far, nw2_far, node_far, dp_far, fine_far, hidden_far, dy_far,
    cg_ref, after_ref, keep_ref, send_ref, gg_ref,
    pay, nw1, nw2, node, dp, fine, node_hidden, dy, sems,
):
    loads = loads_of(
        (nw1_far, nw2_far, node_far, dp_far, fine_far, hidden_far, dy_far),
        (nw1, nw2, node, dp, fine, node_hidden, dy),
        sems,
    )
    for load in loads:
        load.start()
    lat = rows.shape[1]
    width = nw2.shape[0]
    used = 2 * lat + width
    total = total_in[...].astype(BF)
    loads[0].wait()
    pre = dot(rows[...], nw1[0:lat]) + dot(total, nw1[lat:])
    hidden = hidden_of(pre)
    loads[1].wait()
    normed, inv_std = normalise(dot(hidden, nw2[...]))
    cot = ccot[...].astype(F32)
    gain_part, d_proj, d_pre = grad_to_pre(pre, normed, inv_std, cot, ngain[...], nw2[...])
    cg_ref[...] = dot_rt(d_pre, nw1[lat:]).astype(BF)
    after_ref[...] = cot + dot_rt(d_pre, nw1[0:lat])
    gg_ref[...] = ngg[...] + gain_part
    for load in loads[2:]:
        load.wait()
    pay[0:lat] = dot_lt(node[...], dp[...]) + dot_lt(rows[...], d_pre)
    pay[lat : 2 * lat] = dot_lt(fine[...], dp[...]) + dot_lt(total, d_pre)
    pay[2 * lat : used] = dot_lt(node_hidden[...], dy[...]) + dot_lt(hidden, d_proj)
    if used < pay.shape[0]:
        pay[used:] = jnp.zeros((pay.shape[0] - used, lat), F32)
    split_rows(pay, core[0], keep_ref, send_ref)


def up_backward_kernel(
    us, ur, place, cg_own, cg_other, gain, gg, ngg, after,
    pre_far, w2_far, ucot_far, w1_far, cp_far, gw2_far, gw1_far, up_far, xs_far, xr_far,
    gu_far, np_far, keep_far, send_far,
    csum, pay, gu, np_out, pre_ref, w2, ucot, w1, cp, gw2, gw1, up, xs, xr, sems, out_sems,
):
    loads = loads_of(
        (pre_far, w2_far, ucot_far, w1_far, cp_far, gw2_far, gw1_far, up_far, xs_far, xr_far),
        (pre_ref, w2, ucot, w1, cp, gw2, gw1, up, xs, xr),
        sems,
    )
    for load in loads:
        load.start()
    lat = up.shape[1]
    half = cg_own.shape[0]
    coarse = csum.shape[0]
    core = place[1]
    hot_r = onehot_t(ur[...], coarse)
    turned = ur[...] - core * half
    turned = jnp.where(turned < 0, turned + coarse, turned)
    loads[2].wait()
    cot = (
        ucot[...].astype(F32)
        + dot_lt(onehot_t(turned, half), cg_own[...])
        + dot_lt(onehot_t(turned, half, half), cg_other[...])
    )
    loads[0].wait()
    pre = pre_ref[...]
    hidden = hidden_of(pre)
    loads[1].wait()
    normed, inv_std = normalise(dot(hidden, w2[...]))
    gain_part, d_proj, d_pre = grad_to_pre(pre, normed, inv_std, cot, gain[...], w2[...])
    loads[3].wait()
    gu[...] = cot + dot_rt(d_pre, w1[0:lat])
    outs = [store_out(gu, gu_far, out_sems.at[2])]
    send = dot(onehot_t(us[...], np_out.shape[0]), d_pre).astype(BF)
    np_out[...] = dot_rt(send, w1[lat : 2 * lat])
    outs.append(store_out(np_out, np_far, out_sems.at[3]))
    loads[4].wait()
    csum[...] = cp[...].astype(F32) + dot_rt(dot(hot_r, d_pre).astype(BF), w1[2 * lat :])
    count = after.shape[0]
    mine = pl.ds(pl.multiple_of(place[0] * count, 8), count)
    csum[mine, :] = csum[mine, :] + after[...]
    rows = pay.shape[0] // 2 - TAIL
    c_half, h_half, w_half = coarse // 2, gw1.shape[0] // 2, gw2.shape[0] // 2

    def send_piece(start, size):
        for h in range(2):
            src = pay.at[pl.ds(h * (rows + TAIL) + start, size)]

            @pl.when(core == h)
            def _():
                pltpu.make_async_copy(
                    src, keep_far.at[pl.ds(start, size)], out_sems.at[0]
                ).start()

            @pl.when(core != h)
            def _():
                pltpu.make_async_copy(
                    src, send_far.at[pl.ds(start, size)], out_sems.at[1]
                ).start()

    def put(start, size, full):
        for h in range(2):
            at = h * (rows + TAIL) + start
            pay[at : at + size] = full[h * size : (h + 1) * size].astype(BF)

    put(0, c_half, csum)
    send_piece(0, c_half)
    loads[5].wait()
    put(c_half + h_half, w_half, gw2[...].astype(F32) + dot_lt(hidden, d_proj))
    send_piece(c_half + h_half, w_half)
    for load in loads[6:]:
        load.wait()
    w1_part = jnp.concatenate(
        [
            gw1[k * lat : (k + 1) * lat].astype(F32) + dot_lt(x[...], d_pre)
            for k, x in enumerate((up, xs, xr))
        ],
        axis=0,
    )
    put(c_half, h_half, w1_part)
    send_piece(c_half, h_half)
    used = c_half + h_half + w_half
    ids = lax.broadcasted_iota(jnp.int32, (TAIL, lat), 0)
    edge_row = jnp.broadcast_to(gg[...] + gain_part, (TAIL, lat))
    node_row = jnp.broadcast_to(ngg[...], (TAIL, lat))
    tail = jnp.where(ids == 0, edge_row, jnp.where(ids == 1, node_row, 0.0)).astype(BF)
    for h in range(2):
        at = h * (rows + TAIL)
        if used < rows:
            pay[at + used : at + rows] = jnp.zeros((rows - used, lat), BF)
        pay[at + rows : at + rows + TAIL] = tail
    send_piece(used, rows + TAIL - used)
    for k, out_far in enumerate((keep_far, send_far)):
        pltpu.make_async_copy(pay.at[pl.ds(0, rows + TAIL)], out_far, out_sems.at[k]).wait()
    for out in outs:
        out.wait()


def widen_kernel(core, half, coarse_ref, first_ref, second_ref, *, scale):
    start = 0
    for out_ref, factor in ((coarse_ref, None), (first_ref, scale), (second_ref, scale)):
        rows = out_ref.shape[1]
        values = half[start : start + rows].astype(F32)
        out_ref[0] = values if factor is None else values * factor
        start += rows


def widen_other_kernel(core, half, c_in, f_in, s_in, coarse_ref, first_ref, second_ref, *, scale):
    widen_kernel(core, half, coarse_ref, first_ref, second_ref, scale=scale)


def params(*semantics, limit=VMEM_LIMIT):
    return pltpu.CompilerParams(dimension_semantics=semantics or None, vmem_limit_bytes=limit)


def cost(micros):
    return pl.CostEstimate(
        flops=int(micros * 1.1e9), transcendentals=0, bytes_accessed=int(micros * 3.0e6)
    )


def shape(rows, cols, dtype):
    return jax.ShapeDtypeStruct((rows, cols), dtype)


def far(rows, cols, dtype):
    return pltpu.HBM((rows, cols), dtype)


def in_far(*arrays):
    return [pltpu.with_memory_space_constraint(a, pltpu.HBM) for a in arrays]


IN_VMEM = pl.BlockSpec(memory_space=pltpu.VMEM)
IN_SMEM = pl.BlockSpec(memory_space=pltpu.SMEM)
IN_HBM = pl.BlockSpec(memory_space=pl.ANY)


def loads_of(sources, targets, sems):
    return [
        pltpu.make_async_copy(src, dst, sems.at[k])
        for k, (src, dst) in enumerate(zip(sources, targets))
    ]


def buffers(*arrays):
    return [pltpu.VMEM(a.shape, a.dtype) for a in arrays] + [
        pltpu.SemaphoreType.DMA((len(arrays),))
    ]


def swap(x, axes, count):
    if count == 1:
        return x
    return lax.all_to_all(x, axes, 0, 0, tiled=True)


GROUPS = ("core", ("x", "y"), "z")


def owner_index():
    index = jnp.int32(0)
    for axes in GROUPS:
        index = index * lax.axis_size(axes) + lax.axis_index(axes)
    return index


def exchange(x, mask):
    devices = lax.axis_size(EVERYONE)
    if devices == 1:
        return x
    return lax.ppermute(x, EVERYONE, [(i, i ^ mask) for i in range(devices)])


def sum_group(got, count):
    return jnp.sum(got.reshape(count, -1, got.shape[1]).astype(F32), axis=0)


def copies(x, count):
    return jnp.broadcast_to(x[None], (count,) + x.shape).reshape(-1, x.shape[1])


def reduce_rows(keep, send):
    x = keep.astype(F32) + exchange(send, 1).astype(F32)
    for axes in GROUPS[1:]:
        count = lax.axis_size(axes)
        x = sum_group(swap(x.astype(BF), axes, count), count)
    return x


def gather_halves(x):
    for axes in reversed(GROUPS[1:]):
        count = lax.axis_size(axes)
        x = swap(copies(x, count), axes, count)
    return x, exchange(x, 1)


def reduce_with_tail(keep, send, wait_for):
    cols = keep.shape[1]
    rows = keep.shape[0] - TAIL
    got = exchange(send, 1)
    got, wait_for = lax.optimization_barrier((got, wait_for))
    x = (*in_far(keep), got)
    for step, (axes, kernel) in enumerate(zip(GROUPS[1:], (fold_pair_kernel, fold_group_kernel))):
        count = lax.axis_size(axes)
        part = rows // count
        shape_out = (count, part + TAIL, cols)
        manual = dict(
            in_specs=[IN_HBM, IN_VMEM],
            out_specs=IN_HBM,
            scratch_shapes=[
                pltpu.VMEM(keep.shape, BF), pltpu.VMEM(shape_out, BF),
                pltpu.SemaphoreType.DMA((count + 1,)), pltpu.SemaphoreType.DMA((count,)),
            ],
        )
        x = pl.pallas_call(
            kernel,
            out_shape=pltpu.HBM(shape_out, BF),
            compiler_params=params(),
            cost_estimate=cost(3.0),
            **(manual if step == 0 else {}),
        )(*x)
        x = (swap(x.reshape(-1, cols), axes, count).reshape(x.shape),)
        rows = part
    x = jnp.sum(x[0].astype(F32), axis=0)
    return x[:rows].astype(BF), x[rows:], wait_for


def bit_masks(devices):
    slow = devices // lax.axis_size("z")
    order = [1 << b for b in range(1, devices.bit_length() - 1)]
    return (
        [m for m in order if m == slow]
        + [m for m in reversed(order) if m < slow]
        + [m for m in order if m > slow]
    )


def halving_sum(keep, send):
    devices = lax.axis_size(EVERYONE)
    masks = [1] + bit_masks(devices)
    place = lax.axis_index(EVERYONE)
    for mask, after in zip(masks, masks[1:]):
        rows, cols = keep.shape
        bit = ((place & after) > 0).astype(jnp.int32).reshape(1)
        got = exchange(send, mask)
        keep, send = pl.pallas_call(
            fold_split_kernel,
            in_specs=[pl.BlockSpec(memory_space=pltpu.SMEM)]
            + [pl.BlockSpec(memory_space=pltpu.VMEM)] * 2,
            out_shape=(far(rows // 2, cols, BF), shape(rows // 2, cols, BF)),
            compiler_params=params(),
            cost_estimate=cost(1.0),
            name="fold_split",
        )(bit, *in_far(keep), got)
    got = exchange(send, masks[-1])
    x = (keep.astype(F32) + got.astype(F32)).astype(BF)
    for mask in reversed(masks):
        other = exchange(x, mask)
        x = jnp.where(
            (place & mask) > 0, jnp.concatenate([other, x], 0), jnp.concatenate([x, other], 0)
        )
    return x


def padded_rows(rows, devices):
    return -(-rows // (16 * devices)) * 16 * devices


def per_device(
    node, coarse, edge, up, w1, w2, gain, nw1, nw2, ngain, ncot, ccot, ecot, ucot,
    send_rows, edge_sender, edge_receiver, up_sender, up_receiver,
):
    n, lat = node.shape
    width = w2.shape[0]
    ccount = coarse.shape[0]
    ecount = edge.shape[0]
    ucount = up.shape[0]
    devices, slots = send_rows.shape[1], send_rows.shape[2]
    imports = devices * slots
    es, er = in_far(edge_sender.reshape(1, ecount), edge_receiver.reshape(1, ecount))
    us, ur = in_far(up_sender.reshape(1, ucount), up_receiver.reshape(1, ucount))
    gain_row, ngain_row = in_far(gain.reshape(1, lat), ngain.reshape(1, lat))
    own = owner_index()
    core = lax.axis_index("core").reshape(1)

    table = send_rows.reshape(imports)
    hot_send = (table[:, None] == jnp.arange(n, dtype=jnp.int32)[None, :]).astype(BF)
    outgoing = dot(hot_send, node).astype(BF)
    halo = lax.all_to_all(
        outgoing.reshape(devices, slots, lat), EVERYONE, 0, 0, tiled=True
    ).reshape(imports, lat)

    up_pre, up_xs, up_xr, keep, send = pl.pallas_call(
        up_forward_kernel,
        in_specs=[IN_VMEM] * 2 + [IN_SMEM] + [IN_VMEM] * 2 + [IN_HBM] * 4,
        out_shape=(
            far(ucount, width, F32), far(ucount, lat, BF), far(ucount, lat, BF),
            far(ccount // 2, lat, BF), shape(ccount // 2, lat, BF),
        ),
        scratch_shapes=[pltpu.VMEM((ccount, lat), F32)] + buffers(node, coarse, w1, w2),
        compiler_params=params(),
        cost_estimate=cost(5.0),
        name="up_forward",
    )(us, ur, core, *in_far(up), gain_row, *in_far(node, coarse, w1, w2))

    coarse_total = reduce_rows(keep, send)

    edge_args = (w1, edge, node, coarse, w2)
    staging = [far(ecount, width, F32), far(ecount, lat, BF)]
    pre, xs, fine_total = pl.pallas_call(
        edge_forward_kernel,
        in_specs=[IN_VMEM] * 4 + [IN_HBM] * 5,
        out_specs=[IN_HBM] * 2 + [IN_VMEM],
        out_shape=(*staging, far(n, lat, BF)),
        scratch_shapes=buffers(*edge_args, *staging)[:-1]
        + [pltpu.SemaphoreType.DMA((8,)), pltpu.SemaphoreType.DMA((2,))],
        compiler_params=params(limit=BIG_VMEM_LIMIT),
        cost_estimate=cost(9.0),
        name="edge_forward",
    )(es, er, halo, gain_row, *in_far(*edge_args))

    node_args = (node, fine_total, nw1, nw2, ncot)
    staging = [
        far(n, width, BF), far(n, lat, F32), far(n, lat, F32), far(n, width, BF), far(n, lat, BF),
    ]
    ngg, node_dp, fine_grad, grad_n, node_hidden, node_dy = pl.pallas_call(
        node_kernel,
        in_specs=[IN_VMEM] + [IN_HBM] * 5,
        out_specs=[IN_VMEM] + [IN_HBM] * 5,
        out_shape=(shape(1, lat, F32), *staging),
        scratch_shapes=buffers(*node_args) + buffers(*staging),
        compiler_params=params(),
        cost_estimate=cost(5.0),
        name="node_mlp",
    )(ngain_row, *in_far(*node_args))

    edge_args = (pre, w2, ecot, fine_grad, w1, edge, xs, node)
    staging = [
        far(ecount, lat, F32), far(3 * lat, width, BF), far(width, lat, BF), far(n, lat, F32),
        far(ccount, lat, BF),
    ]
    gg, returning, grad_e, gw1, gw2, node_part, coarse_local = pl.pallas_call(
        edge_backward_kernel,
        in_specs=[IN_VMEM] * 3 + [IN_HBM] * 8,
        out_specs=[IN_VMEM] * 2 + [IN_HBM] * 5,
        out_shape=(shape(1, lat, F32), shape(imports, lat, BF), *staging),
        scratch_shapes=buffers(*edge_args) + buffers(*staging),
        compiler_params=params(limit=BIG_VMEM_LIMIT),
        cost_estimate=cost(15.0),
        name="edge_backward",
    )(es, er, gain_row, *in_far(*edge_args))

    returned = lax.all_to_all(
        returning.reshape(devices, slots, lat), EVERYONE, 0, 0, tiled=True
    ).reshape(imports, lat)

    mine = ccount // devices
    padded = -(-mine // 16) * 16
    pad = lambda a: jnp.pad(a, ((0, padded - mine), (0, 0))) if padded > mine else a
    own_coarse = pad(lax.dynamic_slice_in_dim(coarse, own * mine, mine, 0))
    own_cot = pad(lax.dynamic_slice_in_dim(ccot, own * mine, mine, 0))
    node_rows = padded_rows(2 * lat + width, devices)
    node_args = (nw1, nw2, node, node_dp, fine_total, node_hidden, node_dy)
    coarse_grad, coarse_after, node_keep, node_send, ngg_sum = pl.pallas_call(
        coarse_kernel,
        in_specs=[IN_SMEM] + [IN_VMEM] * 5 + [IN_HBM] * 7,
        out_shape=(
            shape(padded, lat, BF), far(padded, lat, F32), far(node_rows // 2, lat, BF),
            shape(node_rows // 2, lat, BF), shape(1, lat, F32),
        ),
        scratch_shapes=[pltpu.VMEM((node_rows, lat), F32)] + buffers(*node_args),
        compiler_params=params(),
        cost_estimate=cost(5.0),
        name="coarse_mlp",
    )(
        core, own_coarse, pad(coarse_total), own_cot, ngain_row, ngg,
        *in_far(*node_args),
    )
    cg_own, cg_other = gather_halves(coarse_grad[:mine])

    node_total = halving_sum(node_keep, node_send)

    edge_rows = padded_rows(ccount + 3 * lat + width, devices)
    up_args = (up_pre, w2, ucot, w1, coarse_local, gw2, gw1, up, up_xs, up_xr)
    grad_u, up_node_part, keep, send = pl.pallas_call(
        up_backward_kernel,
        in_specs=[IN_VMEM] * 2 + [IN_SMEM] + [IN_VMEM] * 6 + [IN_HBM] * 10,
        out_specs=[IN_HBM] * 4,
        out_shape=(
            far(ucount, lat, F32), far(n, lat, F32), far(edge_rows // 2 + TAIL, lat, BF),
            far(edge_rows // 2 + TAIL, lat, BF),
        ),
        scratch_shapes=[
            pltpu.VMEM((ccount, lat), F32), pltpu.VMEM((edge_rows + 2 * TAIL, lat), BF),
        ]
        + [pltpu.VMEM((ucount, lat), F32), pltpu.VMEM((n, lat), F32)]
        + buffers(*up_args)
        + [pltpu.SemaphoreType.DMA((4,))],
        compiler_params=params(),
        cost_estimate=cost(8.0),
        name="up_backward",
    )(
        us, ur, jnp.stack([own, core[0]]), cg_own, cg_other, gain_row, gg, ngg_sum,
        *in_far(coarse_after[:mine]), *in_far(*up_args),
    )
    block, gains, returned = reduce_with_tail(keep, send, returned)
    own_half, other_half = gather_halves(block)
    edge_scale = 1.0 / math.sqrt((ecount + ucount) * devices)
    node_scale = 1.0 / math.sqrt(n * devices + ccount)
    halves = [ccount // 2, 3 * lat // 2, width // 2]
    outs = tuple(pltpu.HBM((2, rows, lat), F32) for rows in halves)

    def place_of(flip):
        return [
            pl.BlockSpec((1, rows, lat), lambda i, c: (c[0] ^ flip, 0, 0)) for rows in halves
        ]

    half_spec = pl.BlockSpec(own_half.shape, lambda i, c: (0, 0))
    written = pl.pallas_call(
        functools.partial(widen_kernel, scale=edge_scale),
        grid_spec=pltpu.PrefetchScalarGridSpec(
            num_scalar_prefetch=1, grid=(1,), in_specs=[half_spec], out_specs=place_of(0)
        ),
        out_shape=outs,
        compiler_params=params("arbitrary"),
        cost_estimate=cost(2.5),
        name="widen_own",
    )(core, own_half)
    written = pl.pallas_call(
        functools.partial(widen_other_kernel, scale=edge_scale),
        grid_spec=pltpu.PrefetchScalarGridSpec(
            num_scalar_prefetch=1,
            grid=(1,),
            in_specs=[half_spec] + [pl.BlockSpec(memory_space=pl.ANY)] * 3,
            out_specs=place_of(1),
        ),
        out_shape=outs,
        input_output_aliases={2: 0, 3: 1, 4: 2},
        compiler_params=params("arbitrary"),
        cost_estimate=cost(2.5),
        name="widen_other",
    )(core, other_half, *in_far(*written))
    grad_coarse, grad_edge_in, grad_edge_out = (a.reshape(-1, lat) for a in written)

    grad_nodes = (
        grad_n
        + node_part
        + up_node_part
        + lax.dot_general(hot_send, returned, (((0,), (0,)), ((), ())), preferred_element_type=F32)
    )
    grad_node_in = node_total[: 2 * lat].astype(F32) * node_scale
    grad_node_out = node_total[2 * lat : 2 * lat + width].astype(F32) * node_scale
    return (
        grad_nodes,
        grad_coarse,
        grad_e,
        grad_u,
        grad_edge_in,
        grad_edge_out,
        gains[0] * edge_scale,
        grad_node_in,
        grad_node_out,
        gains[1] * node_scale,
    )


def split_mesh(mesh):
    face, band = mesh.shape["face"], mesh.shape["band"]
    z = 1
    while z * z < face or face % z:
        z += 1
    core = 2 if band % 2 == 0 else 1
    return Mesh(
        mesh.devices.reshape(z, face // z, band // core, core), ("z", "x", "y", "core")
    )


def solution(mesh):
    rows, split = P(EVERYONE, None), P(EVERYONE)
    return jax.shard_map(
        per_device,
        mesh=split_mesh(mesh),
        in_specs=(
            rows, P(), rows, rows, P(), P(), P(), P(), P(), P(), rows, P(), rows, rows,
            P(EVERYONE, None, None), split, split, split, split,
        ),
        out_specs=(rows, P(), rows, rows, P(), P(), P(), P(), P(), P()),
        check_vma=False,
    )
```

```python
import functools
import math

import jax
import jax.numpy as jnp
from jax import lax
from jax.experimental import pallas as pl
from jax.experimental.pallas import tpu as pltpu
from jax.sharding import Mesh, PartitionSpec as P

EPSILON = 1e-05
BF = jnp.bfloat16
F32 = jnp.float32
TAIL = 16
EVERYONE = ("z", "x", "y", "core")
VMEM_LIMIT = 24 * 1024 * 1024
BIG_VMEM_LIMIT = 50 * 1024 * 1024


def dot(a, b):
    return lax.dot_general(a, b, (((1,), (0,)), ((), ())), preferred_element_type=F32)


def dot_lt(a, b):
    return lax.dot_general(a, b, (((0,), (0,)), ((), ())), preferred_element_type=F32)


def dot_rt(a, b):
    return lax.dot_general(a, b, (((1,), (1,)), ((), ())), preferred_element_type=F32)


def onehot_t(index_row, rows, offset=0):
    ids = lax.broadcasted_iota(jnp.int32, (rows, index_row.shape[1]), 0) + offset
    return jnp.where(ids == index_row, 1.0, 0.0).astype(BF)


def hidden_of(pre):
    return (pre * jax.nn.sigmoid(pre)).astype(BF)


def normalise(projected):
    center = projected - jnp.mean(projected, axis=1, keepdims=True)
    inv_std = lax.rsqrt(jnp.mean(center * center, axis=1, keepdims=True) + EPSILON)
    return center * inv_std, inv_std


def grad_to_pre(pre, normed, inv_std, cot, gain, w2):
    gain_part = jnp.sum(cot * normed, axis=0, keepdims=True)
    scaled = cot * gain
    d_proj = (
        inv_std
        * (
            scaled
            - jnp.mean(scaled, axis=1, keepdims=True)
            - normed * jnp.mean(scaled * normed, axis=1, keepdims=True)
        )
    ).astype(BF)
    d_hidden = dot_rt(d_proj, w2)
    logistic = jax.nn.sigmoid(pre)
    d_pre = (d_hidden * logistic * (1.0 + pre * (1.0 - logistic))).astype(BF)
    return gain_part, d_proj, d_pre


def gather_f32(onehot, table):
    high = table.astype(BF)
    low = (table - high.astype(F32)).astype(BF)
    return dot_lt(onehot, high) + dot_lt(onehot, low)


def split_rows(ref, bit, keep_ref, send_ref):
    half = keep_ref.shape[0]
    keep_ref[...] = ref[pl.ds(pl.multiple_of(bit * half, 16), half), :].astype(BF)
    send_ref[...] = ref[pl.ds(pl.multiple_of((1 - bit) * half, 16), half), :].astype(BF)


def fold_split_kernel(bit, keep, recv, keep_ref, send_ref):
    half = keep_ref.shape[0]
    for side, out_ref in ((bit[0], keep_ref), (1 - bit[0], send_ref)):
        rows = pl.ds(pl.multiple_of(side * half, 16), half)
        out_ref[...] = (keep[rows, :].astype(F32) + recv[rows, :].astype(F32)).astype(BF)


def fold_plain_kernel(keep, recv, out_ref):
    out_ref[...] = (keep[...].astype(F32) + recv[...].astype(F32)).astype(BF)


def fold_pair_kernel(keep_far, recv, out_far, keep, out, sems, out_sems):
    count, rows, _ = out.shape
    rows -= TAIL
    spans = [(count * rows, TAIL)] + [(k * rows, rows) for k in range(count)]
    loads = [
        pltpu.make_async_copy(
            keep_far.at[pl.ds(at, size)], keep.at[pl.ds(at, size)], sems.at[k]
        )
        for k, (at, size) in enumerate(spans)
    ]
    for load in loads:
        load.start()
    sums = []
    outs = []
    for k, (at, size) in enumerate(spans):
        loads[k].wait()
        piece = slice(at, at + size)
        total = (keep[piece].astype(F32) + recv[piece].astype(F32)).astype(BF)
        if k == 0:
            sums.append(total)
            continue
        out[k - 1, 0:rows] = total
        out[k - 1, rows:] = sums[0]
        outs.append(store_out(out.at[k - 1], out_far.at[k - 1], out_sems.at[k - 1]))
    for copy in outs:
        copy.wait()


def fold_group_kernel(got, out_ref):
    group = got.shape[0]
    count, rows, _ = out_ref.shape
    rows -= TAIL

    def total(at, size):
        piece = slice(at, at + size)
        acc = got[0, piece].astype(F32)
        for k in range(1, group):
            acc += got[k, piece].astype(F32)
        return acc.astype(BF)

    tail = total(count * rows, TAIL)
    for k in range(count):
        out_ref[k, 0:rows] = total(k * rows, rows)
        out_ref[k, rows:] = tail


def up_forward_kernel(
    us, ur, core, gain, node_far, coarse_far, up_far, w1_far, w2_far,
    p_far, xs_far, xr_far, keep_ref, send_ref,
    part, node, coarse, up, w1, w2, sems, p_out, xs_out, xr_out, out_sems,
):
    loads = loads_of(
        (node_far, coarse_far, up_far, w1_far, w2_far), (node, coarse, up, w1, w2), sems
    )
    for load in loads:
        load.start()
    lat = up.shape[1]
    hot_s = onehot_t(us[...], node.shape[0])
    hot_r = onehot_t(ur[...], coarse.shape[0])
    loads[0].wait()
    xs = dot_lt(hot_s, node[...]).astype(BF)
    xs_out[...] = xs
    outs = [store_out(xs_out, xs_far, out_sems.at[0])]
    loads[1].wait()
    xr = dot_lt(hot_r, coarse[...]).astype(BF)
    xr_out[...] = xr
    outs.append(store_out(xr_out, xr_far, out_sems.at[1]))
    loads[2].wait()
    loads[3].wait()
    pre = dot(up[...], w1[0:lat]) + dot(xs, w1[lat : 2 * lat]) + dot(xr, w1[2 * lat :])
    p_out[...] = pre
    outs.append(store_out(p_out, p_far, out_sems.at[2]))
    loads[4].wait()
    normed, _ = normalise(dot(hidden_of(pre), w2[...]))
    new = (up[...].astype(F32) + normed * gain[...]).astype(BF)
    part[...] = dot(hot_r, new)
    split_rows(part, core[0], keep_ref, send_ref)
    for out in outs:
        out.wait()


def store_out(staging, target, sem):
    copy = pltpu.make_async_copy(staging, target, sem)
    copy.start()
    return copy


def edge_forward_kernel(
    es, er, halo, gain, w1_far, edge_far, node_far, coarse_far, w2_far,
    p_far, xs_far, total_ref, w1, edge, node, coarse, w2, pre_out, xs_out, sems, out_sems,
):
    lat = edge.shape[1]
    n = node.shape[0]
    imports = halo.shape[0]
    first, last, middle = (
        pltpu.make_async_copy(
            w1_far.at[k * lat : (k + 1) * lat], w1.at[k * lat : (k + 1) * lat], sems.at[5 + k]
        )
        for k in (0, 2, 1)
    )
    edge_load, node_load, coarse_load, w2_load = loads_of(
        (edge_far, node_far, coarse_far, w2_far), (edge, node, coarse, w2), sems
    )
    for load in (node_load, last, edge_load, first, coarse_load, middle, w2_load):
        load.start()
    sender = es[...]
    hot_r = onehot_t(er[...], n)
    hot_n = onehot_t(sender, n)
    node_load.wait()
    xr = dot_lt(hot_r, node[...]).astype(BF)
    xs = dot_lt(hot_n, node[...]) + dot_lt(onehot_t(sender, imports, n), halo[...])
    last.wait()
    pre = dot(xr, w1[2 * lat :])
    edge_load.wait()
    first.wait()
    pre += dot(edge[...], w1[0:lat])
    hot_c = onehot_t(sender, coarse.shape[0], n + imports)
    coarse_load.wait()
    xs = (xs + dot_lt(hot_c, coarse[...])).astype(BF)
    xs_out[...] = xs
    outs = [store_out(xs_out, xs_far, out_sems.at[0])]
    middle.wait()
    pre += dot(xs, w1[lat : 2 * lat])
    pre_out[...] = pre
    outs.append(store_out(pre_out, p_far, out_sems.at[1]))
    hidden = hidden_of(pre)
    w2_load.wait()
    normed, _ = normalise(dot(hidden, w2[...]))
    new = (edge[...].astype(F32) + normed * gain[...]).astype(BF)
    total_ref[...] = dot(hot_r, new).astype(BF)
    for out in outs:
        out.wait()


def node_kernel(
    ngain, node_far, total_far, nw1_far, nw2_far, ncot_far,
    ngg_ref, dp_far, fg_far, gn_far, hidden_far, dy_far,
    node, total, nw1, nw2, ncot, sems, dp, fg, gn, hidden_out, dy, out_sems,
):
    loads = loads_of(
        (node_far, total_far, nw1_far, nw2_far, ncot_far), (node, total, nw1, nw2, ncot), sems
    )
    for load in loads:
        load.start()
    lat = node.shape[1]
    for load in loads[:3]:
        load.wait()
    pre = dot(node[...], nw1[0:lat]) + dot(total[...], nw1[lat:])
    hidden = hidden_of(pre)
    hidden_out[...] = hidden
    outs = [store_out(hidden_out, hidden_far, out_sems.at[0])]
    loads[3].wait()
    normed, inv_std = normalise(dot(hidden, nw2[...]))
    loads[4].wait()
    cot = ncot[...].astype(F32)
    gain_part, d_proj, d_pre = grad_to_pre(pre, normed, inv_std, cot, ngain[...], nw2[...])
    ngg_ref[...] = gain_part
    dy[...] = d_proj
    outs.append(store_out(dy, dy_far, out_sems.at[1]))
    dp[...] = d_pre
    outs.append(store_out(dp, dp_far, out_sems.at[2]))
    fg[...] = dot_rt(d_pre, nw1[lat:])
    outs.append(store_out(fg, fg_far, out_sems.at[3]))
    gn[...] = cot + dot_rt(d_pre, nw1[0:lat])
    outs.append(store_out(gn, gn_far, out_sems.at[4]))
    for out in outs:
        out.wait()


def edge_backward_kernel(
    es, er, gain, pre_far, w2_far, ecot_far, fg_far, w1_far, edge_far, xs_far, node_far,
    gg_ref, ret_ref, ge_far, gw1_far, gw2_far, np_far, cp_far,
    pre, w2, ecot, fg, w1, edge, xs, node, sems, ge, gw1, gw2, np_out, cp, out_sems,
):
    lat = edge.shape[1]
    n = node.shape[0]
    imports = ret_ref.shape[0]
    loads = loads_of(
        (pre_far, w2_far, ecot_far, fg_far, w1_far, edge_far, xs_far, node_far),
        (pre, w2, ecot, fg, w1, edge, xs, node),
        sems,
    )
    for load in loads:
        load.start()
    hot_r = onehot_t(er[...], n)
    loads[0].wait()
    hidden = hidden_of(pre[...])
    loads[1].wait()
    normed, inv_std = normalise(dot(hidden, w2[...]))
    loads[2].wait()
    loads[3].wait()
    cot = ecot[...].astype(F32) + gather_f32(hot_r, fg[...])
    gain_part, d_proj, d_pre = grad_to_pre(pre[...], normed, inv_std, cot, gain[...], w2[...])
    gg_ref[...] = gain_part
    loads[4].wait()
    ge[...] = cot + dot_rt(d_pre, w1[0:lat])
    outs = [store_out(ge, ge_far, out_sems.at[0])]
    loads[5].wait()
    gw1[0:lat] = dot_lt(edge[...], d_pre).astype(BF)
    loads[6].wait()
    gw1[lat : 2 * lat] = dot_lt(xs[...], d_pre).astype(BF)
    recv = dot(hot_r, d_pre).astype(BF)
    loads[7].wait()
    gw1[2 * lat :] = dot_lt(node[...], recv).astype(BF)
    outs.append(store_out(gw1, gw1_far, out_sems.at[1]))
    gw2[...] = dot_lt(hidden, d_proj).astype(BF)
    outs.append(store_out(gw2, gw2_far, out_sems.at[2]))
    w_s = w1[lat : 2 * lat]
    sender = es[...]
    count = cp.shape[0]
    sums = dot(onehot_t(sender, count, n + imports), d_pre).astype(BF)
    cp[...] = dot_rt(sums, w_s).astype(BF)
    outs.append(store_out(cp, cp_far, out_sems.at[3]))
    sums = dot(onehot_t(sender, n), d_pre).astype(BF)
    np_out[...] = dot_rt(sums, w_s) + dot_rt(recv, w1[2 * lat :])
    outs.append(store_out(np_out, np_far, out_sems.at[4]))
    sums = dot(onehot_t(sender, imports, n), d_pre).astype(BF)
    ret_ref[...] = dot_rt(sums, w_s).astype(BF)
    for out in outs:
        out.wait()


def coarse_kernel(
    core, rows, total_in, ccot, ngain, ngg,
    nw1_far, nw2_far, node_far, dp_far, fine_far, hidden_far, dy_far,
    cg_ref, after_ref, keep_ref, send_ref, gg_ref,
    pay, nw1, nw2, node, dp, fine, node_hidden, dy, sems,
):
    loads = loads_of(
        (nw1_far, nw2_far, node_far, dp_far, fine_far, hidden_far, dy_far),
        (nw1, nw2, node, dp, fine, node_hidden, dy),
        sems,
    )
    for load in loads:
        load.start()
    lat = rows.shape[1]
    width = nw2.shape[0]
    used = 2 * lat + width
    total = total_in[...].astype(BF)
    loads[0].wait()
    pre = dot(rows[...], nw1[0:lat]) + dot(total, nw1[lat:])
    hidden = hidden_of(pre)
    loads[1].wait()
    normed, inv_std = normalise(dot(hidden, nw2[...]))
    cot = ccot[...].astype(F32)
    gain_part, d_proj, d_pre = grad_to_pre(pre, normed, inv_std, cot, ngain[...], nw2[...])
    grad = dot_rt(d_pre, nw1[lat:]).astype(BF)
    for k in range(cg_ref.shape[0] // grad.shape[0]):
        cg_ref[k * grad.shape[0] : (k + 1) * grad.shape[0]] = grad
    after_ref[...] = cot + dot_rt(d_pre, nw1[0:lat])
    gg_ref[...] = ngg[...] + gain_part
    for load in loads[2:]:
        load.wait()
    pay[0:lat] = dot_lt(node[...], dp[...]) + dot_lt(rows[...], d_pre)
    pay[lat : 2 * lat] = dot_lt(fine[...], dp[...]) + dot_lt(total, d_pre)
    pay[2 * lat : used] = dot_lt(node_hidden[...], dy[...]) + dot_lt(hidden, d_proj)
    if used < pay.shape[0]:
        pay[used:] = jnp.zeros((pay.shape[0] - used, lat), F32)
    split_rows(pay, core[0], keep_ref, send_ref)


def up_backward_kernel(
    us, ur, place, cg_own, cg_other, gain, gg, ngg, after,
    pre_far, w2_far, ucot_far, w1_far, cp_far, gw2_far, gw1_far, up_far, xs_far, xr_far,
    gu_far, np_far, keep_far, send_far,
    csum, pay, gu, np_out, pre_ref, w2, ucot, w1, cp, gw2, gw1, up, xs, xr, sems, out_sems,
):
    loads = loads_of(
        (pre_far, w2_far, ucot_far, w1_far, cp_far, gw2_far, gw1_far, up_far, xs_far, xr_far),
        (pre_ref, w2, ucot, w1, cp, gw2, gw1, up, xs, xr),
        sems,
    )
    for load in loads:
        load.start()
    lat = up.shape[1]
    half = cg_own.shape[0]
    coarse = csum.shape[0]
    core = place[1]
    hot_r = onehot_t(ur[...], coarse)
    turned = ur[...] - core * half
    turned = jnp.where(turned < 0, turned + coarse, turned)
    loads[2].wait()
    cot = (
        ucot[...].astype(F32)
        + dot_lt(onehot_t(turned, half), cg_own[...])
        + dot_lt(onehot_t(turned, half, half), cg_other[...])
    )
    loads[0].wait()
    pre = pre_ref[...]
    hidden = hidden_of(pre)
    loads[1].wait()
    normed, inv_std = normalise(dot(hidden, w2[...]))
    gain_part, d_proj, d_pre = grad_to_pre(pre, normed, inv_std, cot, gain[...], w2[...])
    loads[3].wait()
    gu[...] = cot + dot_rt(d_pre, w1[0:lat])
    outs = [store_out(gu, gu_far, out_sems.at[2])]
    send = dot(onehot_t(us[...], np_out.shape[0]), d_pre).astype(BF)
    np_out[...] = dot_rt(send, w1[lat : 2 * lat])
    outs.append(store_out(np_out, np_far, out_sems.at[3]))
    loads[4].wait()
    csum[...] = cp[...].astype(F32) + dot_rt(dot(hot_r, d_pre).astype(BF), w1[2 * lat :])
    count = after.shape[0]
    mine = pl.ds(pl.multiple_of(place[0] * count, 8), count)
    csum[mine, :] = csum[mine, :] + after[...]
    rows = pay.shape[0] // 2 - TAIL
    c_half, h_half, w_half = coarse // 2, gw1.shape[0] // 2, gw2.shape[0] // 2

    def send_piece(start, size):
        for h in range(2):
            src = pay.at[pl.ds(h * (rows + TAIL) + start, size)]

            @pl.when(core == h)
            def _():
                pltpu.make_async_copy(
                    src, keep_far.at[pl.ds(start, size)], out_sems.at[0]
                ).start()

            @pl.when(core != h)
            def _():
                pltpu.make_async_copy(
                    src, send_far.at[pl.ds(start, size)], out_sems.at[1]
                ).start()

    def put(start, size, full):
        for h in range(2):
            at = h * (rows + TAIL) + start
            pay[at : at + size] = full[h * size : (h + 1) * size].astype(BF)

    put(0, c_half, csum)
    send_piece(0, c_half)
    loads[5].wait()
    put(c_half + h_half, w_half, gw2[...].astype(F32) + dot_lt(hidden, d_proj))
    send_piece(c_half + h_half, w_half)
    for load in loads[6:]:
        load.wait()
    w1_part = jnp.concatenate(
        [
            gw1[k * lat : (k + 1) * lat].astype(F32) + dot_lt(x[...], d_pre)
            for k, x in enumerate((up, xs, xr))
        ],
        axis=0,
    )
    put(c_half, h_half, w1_part)
    send_piece(c_half, h_half)
    used = c_half + h_half + w_half
    ids = lax.broadcasted_iota(jnp.int32, (TAIL, lat), 0)
    edge_row = jnp.broadcast_to(gg[...] + gain_part, (TAIL, lat))
    node_row = jnp.broadcast_to(ngg[...], (TAIL, lat))
    tail = jnp.where(ids == 0, edge_row, jnp.where(ids == 1, node_row, 0.0)).astype(BF)
    for h in range(2):
        at = h * (rows + TAIL)
        if used < rows:
            pay[at + used : at + rows] = jnp.zeros((rows - used, lat), BF)
        pay[at + rows : at + rows + TAIL] = tail
    send_piece(used, rows + TAIL - used)
    for k, out_far in enumerate((keep_far, send_far)):
        pltpu.make_async_copy(pay.at[pl.ds(0, rows + TAIL)], out_far, out_sems.at[k]).wait()
    for out in outs:
        out.wait()


def widen_kernel(core, half, coarse_ref, first_ref, second_ref, *, scale):
    start = 0
    for out_ref, factor in ((coarse_ref, None), (first_ref, scale), (second_ref, scale)):
        rows = out_ref.shape[1]
        values = half[start : start + rows].astype(F32)
        out_ref[0] = values if factor is None else values * factor
        start += rows


def widen_other_kernel(core, half, c_in, f_in, s_in, coarse_ref, first_ref, second_ref, *, scale):
    widen_kernel(core, half, coarse_ref, first_ref, second_ref, scale=scale)


def params(*semantics, limit=VMEM_LIMIT):
    return pltpu.CompilerParams(dimension_semantics=semantics or None, vmem_limit_bytes=limit)


def cost(micros):
    return pl.CostEstimate(
        flops=int(micros * 1.1e9), transcendentals=0, bytes_accessed=int(micros * 3.0e6)
    )


def shape(rows, cols, dtype):
    return jax.ShapeDtypeStruct((rows, cols), dtype)


def far(rows, cols, dtype):
    return pltpu.HBM((rows, cols), dtype)


def in_far(*arrays):
    return [pltpu.with_memory_space_constraint(a, pltpu.HBM) for a in arrays]


IN_VMEM = pl.BlockSpec(memory_space=pltpu.VMEM)
IN_SMEM = pl.BlockSpec(memory_space=pltpu.SMEM)
IN_HBM = pl.BlockSpec(memory_space=pl.ANY)


def loads_of(sources, targets, sems):
    return [
        pltpu.make_async_copy(src, dst, sems.at[k])
        for k, (src, dst) in enumerate(zip(sources, targets))
    ]


def buffers(*arrays):
    return [pltpu.VMEM(a.shape, a.dtype) for a in arrays] + [
        pltpu.SemaphoreType.DMA((len(arrays),))
    ]


def swap(x, axes, count):
    if count == 1:
        return x
    return lax.all_to_all(x, axes, 0, 0, tiled=True)


GROUPS = ("core", ("x", "y"), "z")


def owner_index():
    index = jnp.int32(0)
    for axes in GROUPS:
        index = index * lax.axis_size(axes) + lax.axis_index(axes)
    return index


def exchange(x, mask):
    devices = lax.axis_size(EVERYONE)
    if devices == 1:
        return x
    return lax.ppermute(x, EVERYONE, [(i, i ^ mask) for i in range(devices)])


def sum_group(got, count):
    return jnp.sum(got.reshape(count, -1, got.shape[1]).astype(F32), axis=0)


def copies(x, count):
    return jnp.broadcast_to(x[None], (count,) + x.shape).reshape(-1, x.shape[1])


def reduce_rows(keep, send):
    x = pl.pallas_call(
        fold_plain_kernel,
        out_shape=far(*keep.shape, BF),
        compiler_params=params(),
        cost_estimate=cost(1.0),
        name="fold_plain",
    )(*in_far(keep), exchange(send, 1))
    for axes in GROUPS[1:]:
        count = lax.axis_size(axes)
        x = sum_group(swap(x.astype(BF), axes, count), count)
    return x


def gather_halves(x, copied=False):
    for step, axes in enumerate(reversed(GROUPS[1:])):
        count = lax.axis_size(axes)
        x = swap(x if copied and step == 0 else copies(x, count), axes, count)
    return x, exchange(x, 1)


def reduce_with_tail(keep, send, wait_for):
    cols = keep.shape[1]
    rows = keep.shape[0] - TAIL
    got = exchange(send, 1)
    got, wait_for = lax.optimization_barrier((got, wait_for))
    x = (*in_far(keep), got)
    for step, (axes, kernel) in enumerate(zip(GROUPS[1:], (fold_pair_kernel, fold_group_kernel))):
        count = lax.axis_size(axes)
        part = rows // count
        shape_out = (count, part + TAIL, cols)
        manual = dict(
            in_specs=[IN_HBM, IN_VMEM],
            out_specs=IN_HBM,
            scratch_shapes=[
                pltpu.VMEM(keep.shape, BF), pltpu.VMEM(shape_out, BF),
                pltpu.SemaphoreType.DMA((count + 1,)), pltpu.SemaphoreType.DMA((count,)),
            ],
        )
        x = pl.pallas_call(
            kernel,
            out_shape=pltpu.HBM(shape_out, BF),
            compiler_params=params(),
            cost_estimate=cost(3.0),
            **(manual if step == 0 else {}),
        )(*x)
        x = (swap(x.reshape(-1, cols), axes, count).reshape(x.shape),)
        rows = part
    x = jnp.sum(x[0].astype(F32), axis=0)
    return x[:rows].astype(BF), x[rows:], wait_for


def bit_masks(devices):
    slow = devices // lax.axis_size("z")
    order = [1 << b for b in range(1, devices.bit_length() - 1)]
    return (
        [m for m in order if m == slow]
        + [m for m in reversed(order) if m < slow]
        + [m for m in order if m > slow]
    )


def halving_sum(keep, send):
    devices = lax.axis_size(EVERYONE)
    masks = [1] + bit_masks(devices)
    place = lax.axis_index(EVERYONE)
    for mask, after in zip(masks, masks[1:]):
        rows, cols = keep.shape
        bit = ((place & after) > 0).astype(jnp.int32).reshape(1)
        got = exchange(send, mask)
        keep, send = pl.pallas_call(
            fold_split_kernel,
            in_specs=[pl.BlockSpec(memory_space=pltpu.SMEM)]
            + [pl.BlockSpec(memory_space=pltpu.VMEM)] * 2,
            out_shape=(far(rows // 2, cols, BF), shape(rows // 2, cols, BF)),
            compiler_params=params(),
            cost_estimate=cost(1.0),
            name="fold_split",
        )(bit, *in_far(keep), got)
    got = exchange(send, masks[-1])
    x = (keep.astype(F32) + got.astype(F32)).astype(BF)
    for mask in reversed(masks):
        other = exchange(x, mask)
        x = jnp.where(
            (place & mask) > 0, jnp.concatenate([other, x], 0), jnp.concatenate([x, other], 0)
        )
    return x


def padded_rows(rows, devices):
    return -(-rows // (16 * devices)) * 16 * devices


def per_device(
    node, coarse, edge, up, w1, w2, gain, nw1, nw2, ngain, ncot, ccot, ecot, ucot,
    send_rows, edge_sender, edge_receiver, up_sender, up_receiver,
):
    n, lat = node.shape
    width = w2.shape[0]
    ccount = coarse.shape[0]
    ecount = edge.shape[0]
    ucount = up.shape[0]
    devices, slots = send_rows.shape[1], send_rows.shape[2]
    imports = devices * slots
    es, er = in_far(edge_sender.reshape(1, ecount), edge_receiver.reshape(1, ecount))
    us, ur = in_far(up_sender.reshape(1, ucount), up_receiver.reshape(1, ucount))
    gain_row, ngain_row = in_far(gain.reshape(1, lat), ngain.reshape(1, lat))
    own = owner_index()
    core = lax.axis_index("core").reshape(1)

    table = send_rows.reshape(imports)
    hot_send = (table[:, None] == jnp.arange(n, dtype=jnp.int32)[None, :]).astype(BF)
    outgoing = dot(hot_send, node).astype(BF)
    halo = lax.all_to_all(
        outgoing.reshape(devices, slots, lat), EVERYONE, 0, 0, tiled=True
    ).reshape(imports, lat)

    up_args = (node, coarse, up, w1, w2)
    staging = [far(ucount, width, F32), far(ucount, lat, BF), far(ucount, lat, BF)]
    up_pre, up_xs, up_xr, keep, send = pl.pallas_call(
        up_forward_kernel,
        in_specs=[IN_VMEM] * 2 + [IN_SMEM] + [IN_VMEM] + [IN_HBM] * 5,
        out_specs=[IN_HBM] * 3 + [IN_VMEM] * 2,
        out_shape=(*staging, far(ccount // 2, lat, BF), shape(ccount // 2, lat, BF)),
        scratch_shapes=[pltpu.VMEM((ccount, lat), F32)] + buffers(*up_args) + buffers(*staging),
        compiler_params=params(),
        cost_estimate=cost(5.0),
        name="up_forward",
    )(us, ur, core, gain_row, *in_far(*up_args))

    coarse_total = reduce_rows(keep, send)

    edge_args = (w1, edge, node, coarse, w2)
    staging = [far(ecount, width, F32), far(ecount, lat, BF)]
    pre, xs, fine_total = pl.pallas_call(
        edge_forward_kernel,
        in_specs=[IN_VMEM] * 4 + [IN_HBM] * 5,
        out_specs=[IN_HBM] * 2 + [IN_VMEM],
        out_shape=(*staging, far(n, lat, BF)),
        scratch_shapes=buffers(*edge_args, *staging)[:-1]
        + [pltpu.SemaphoreType.DMA((8,)), pltpu.SemaphoreType.DMA((2,))],
        compiler_params=params(limit=BIG_VMEM_LIMIT),
        cost_estimate=cost(9.0),
        name="edge_forward",
    )(es, er, halo, gain_row, *in_far(*edge_args))

    node_args = (node, fine_total, nw1, nw2, ncot)
    staging = [
        far(n, width, BF), far(n, lat, F32), far(n, lat, F32), far(n, width, BF), far(n, lat, BF),
    ]
    ngg, node_dp, fine_grad, grad_n, node_hidden, node_dy = pl.pallas_call(
        node_kernel,
        in_specs=[IN_VMEM] + [IN_HBM] * 5,
        out_specs=[IN_VMEM] + [IN_HBM] * 5,
        out_shape=(shape(1, lat, F32), *staging),
        scratch_shapes=buffers(*node_args) + buffers(*staging),
        compiler_params=params(),
        cost_estimate=cost(5.0),
        name="node_mlp",
    )(ngain_row, *in_far(*node_args))

    edge_args = (pre, w2, ecot, fine_grad, w1, edge, xs, node)
    staging = [
        far(ecount, lat, F32), far(3 * lat, width, BF), far(width, lat, BF), far(n, lat, F32),
        far(ccount, lat, BF),
    ]
    gg, returning, grad_e, gw1, gw2, node_part, coarse_local = pl.pallas_call(
        edge_backward_kernel,
        in_specs=[IN_VMEM] * 3 + [IN_HBM] * 8,
        out_specs=[IN_VMEM] * 2 + [IN_HBM] * 5,
        out_shape=(shape(1, lat, F32), shape(imports, lat, BF), *staging),
        scratch_shapes=buffers(*edge_args) + buffers(*staging),
        compiler_params=params(limit=BIG_VMEM_LIMIT),
        cost_estimate=cost(15.0),
        name="edge_backward",
    )(es, er, gain_row, *in_far(*edge_args))

    returned = lax.all_to_all(
        returning.reshape(devices, slots, lat), EVERYONE, 0, 0, tiled=True
    ).reshape(imports, lat)

    mine = ccount // devices
    padded = -(-mine // 16) * 16
    pad = lambda a: jnp.pad(a, ((0, padded - mine), (0, 0))) if padded > mine else a
    own_coarse = pad(lax.dynamic_slice_in_dim(coarse, own * mine, mine, 0))
    own_cot = pad(lax.dynamic_slice_in_dim(ccot, own * mine, mine, 0))
    cg_copies = lax.axis_size(GROUPS[-1]) if padded == mine else 1
    node_rows = padded_rows(2 * lat + width, devices)
    node_args = (nw1, nw2, node, node_dp, fine_total, node_hidden, node_dy)
    coarse_grad, coarse_after, node_keep, node_send, ngg_sum = pl.pallas_call(
        coarse_kernel,
        in_specs=[IN_SMEM] + [IN_VMEM] * 5 + [IN_HBM] * 7,
        out_shape=(
            shape(padded * cg_copies, lat, BF), far(padded, lat, F32),
            far(node_rows // 2, lat, BF),
            shape(node_rows // 2, lat, BF), shape(1, lat, F32),
        ),
        scratch_shapes=[pltpu.VMEM((node_rows, lat), F32)] + buffers(*node_args),
        compiler_params=params(),
        cost_estimate=cost(5.0),
        name="coarse_mlp",
    )(
        core, own_coarse, pad(coarse_total), own_cot, ngain_row, ngg,
        *in_far(*node_args),
    )
    if cg_copies == 1:
        coarse_grad = coarse_grad[:mine]
    cg_own, cg_other = gather_halves(coarse_grad, copied=cg_copies > 1)

    node_total = halving_sum(node_keep, node_send)

    edge_rows = padded_rows(ccount + 3 * lat + width, devices)
    up_args = (up_pre, w2, ucot, w1, coarse_local, gw2, gw1, up, up_xs, up_xr)
    grad_u, up_node_part, keep, send = pl.pallas_call(
        up_backward_kernel,
        in_specs=[IN_VMEM] * 2 + [IN_SMEM] + [IN_VMEM] * 6 + [IN_HBM] * 10,
        out_specs=[IN_HBM] * 4,
        out_shape=(
            far(ucount, lat, F32), far(n, lat, F32), far(edge_rows // 2 + TAIL, lat, BF),
            far(edge_rows // 2 + TAIL, lat, BF),
        ),
        scratch_shapes=[
            pltpu.VMEM((ccount, lat), F32), pltpu.VMEM((edge_rows + 2 * TAIL, lat), BF),
        ]
        + [pltpu.VMEM((ucount, lat), F32), pltpu.VMEM((n, lat), F32)]
        + buffers(*up_args)
        + [pltpu.SemaphoreType.DMA((4,))],
        compiler_params=params(),
        cost_estimate=cost(8.0),
        name="up_backward",
    )(
        us, ur, jnp.stack([own, core[0]]), cg_own, cg_other, gain_row, gg, ngg_sum,
        *in_far(coarse_after[:mine]), *in_far(*up_args),
    )
    block, gains, returned = reduce_with_tail(keep, send, returned)
    own_half, other_half = gather_halves(block)
    edge_scale = 1.0 / math.sqrt((ecount + ucount) * devices)
    node_scale = 1.0 / math.sqrt(n * devices + ccount)
    halves = [ccount // 2, 3 * lat // 2, width // 2]
    outs = tuple(pltpu.HBM((2, rows, lat), F32) for rows in halves)

    def place_of(flip):
        return [
            pl.BlockSpec((1, rows, lat), lambda i, c: (c[0] ^ flip, 0, 0)) for rows in halves
        ]

    half_spec = pl.BlockSpec(own_half.shape, lambda i, c: (0, 0))
    written = pl.pallas_call(
        functools.partial(widen_kernel, scale=edge_scale),
        grid_spec=pltpu.PrefetchScalarGridSpec(
            num_scalar_prefetch=1, grid=(1,), in_specs=[half_spec], out_specs=place_of(0)
        ),
        out_shape=outs,
        compiler_params=params("arbitrary"),
        cost_estimate=cost(2.5),
        name="widen_own",
    )(core, own_half)
    written = pl.pallas_call(
        functools.partial(widen_other_kernel, scale=edge_scale),
        grid_spec=pltpu.PrefetchScalarGridSpec(
            num_scalar_prefetch=1,
            grid=(1,),
            in_specs=[half_spec] + [pl.BlockSpec(memory_space=pl.ANY)] * 3,
            out_specs=place_of(1),
        ),
        out_shape=outs,
        input_output_aliases={2: 0, 3: 1, 4: 2},
        compiler_params=params("arbitrary"),
        cost_estimate=cost(2.5),
        name="widen_other",
    )(core, other_half, *in_far(*written))
    grad_coarse, grad_edge_in, grad_edge_out = (a.reshape(-1, lat) for a in written)

    grad_nodes = (
        grad_n
        + node_part
        + up_node_part
        + lax.dot_general(hot_send, returned, (((0,), (0,)), ((), ())), preferred_element_type=F32)
    )
    grad_node_in = node_total[: 2 * lat].astype(F32) * node_scale
    grad_node_out = node_total[2 * lat : 2 * lat + width].astype(F32) * node_scale
    return (
        grad_nodes,
        grad_coarse,
        grad_e,
        grad_u,
        grad_edge_in,
        grad_edge_out,
        gains[0] * edge_scale,
        grad_node_in,
        grad_node_out,
        gains[1] * node_scale,
    )


def split_mesh(mesh):
    face, band = mesh.shape["face"], mesh.shape["band"]
    z = 1
    while z * z < face or face % z:
        z += 1
    core = 2 if band % 2 == 0 else 1
    return Mesh(
        mesh.devices.reshape(z, face // z, band // core, core), ("z", "x", "y", "core")
    )


def solution(mesh):
    rows, split = P(EVERYONE, None), P(EVERYONE)
    return jax.shard_map(
        per_device,
        mesh=split_mesh(mesh),
        in_specs=(
            rows, P(), rows, rows, P(), P(), P(), P(), P(), P(), rows, P(), rows, rows,
            P(EVERYONE, None, None), split, split, split, split,
        ),
        out_specs=(rows, P(), rows, rows, P(), P(), P(), P(), P(), P()),
        check_vma=False,
    )
```
